512 devices in a mesh: member: 8 (over z_lo, core), grid: 64 (over z_hi, y, x).
Axes of the slice: x: 4, y: 4, z: 16 (z_hi: 4, z_lo: 4; z = z_hi * 4 + z_lo), core: 2. Of those that a mesh axis runs over, the one named last changes fastest.
Arguments:
- states: bfloat16 [8, 8192, 1024], P('member', 'grid'), may hold values from -16 to 16
- norm_scale_vector: float32 [1024], replicated, may hold values from 0.1 to 1.9
- query_weight: bfloat16 [1024, 512], P('grid'), may hold values from -2 to 2
- key_weight: bfloat16 [1024, 512], P('grid'), may hold values from -2 to 2
- value_weight: bfloat16 [1024, 512], P('grid'), may hold values from -0.1875 to 0.1875
- output_weight: bfloat16 [512, 1024], P('grid'), may hold values from -0.25 to 0.25
- head_weight: bfloat16 [1024, 128], P('grid'), may hold values from -0.5 to 0.5
- neighbours: int32 [8192, 8], P('grid'), may hold values from 0 to 8191, as said below
- observed: float32 [8192, 128], P('grid'), may hold values from -16 to 16
Outputs:
- grad_input: bfloat16 [8, 8192, 1024], P('member', 'grid')
- grad_mixing: float32 [512, 1024], P('grid')
- grad_head: float32 [1024, 128], P('grid')
- grad_key_value: float32 [8, 8192, 1024], P('member', 'grid')
The draws below stay inside these ranges and needn't reach their ends.
Inputs may be any that keep to these rules, and one draw needn't show every extreme that they name: `neighbours`: the first neighbour of every point is the point itself; every neighbour index lies within 32 positions of the point's own index, and that distance occurs.
All inputs are finite; a program needn't handle non-finite values.
Results may differ from the reference program's by a relative error of at most 0.035.
Values may be sent and summed in bfloat16 or wider, within the bound.
No kernel may reach another device: no remote copies, remote signals or barrier semaphores. Data moves between devices by JAX's collectives and lax.ppermute only.
A program may use at most 64 MiB of HBM per device.

```python
import math
import jax
import jax.numpy as jnp
from jax import lax

D = 1024
HEADS = 8
HDIM = 64
NVAR = 128
KNB = 8
P_DEV = 128
HD = 512
HALO = 32
NPTS = 8192
ENSEMBLE_SIZE = 8
N_GRID = 64


def query_and_key(key):
    base_draw = jnp.clip(jax.random.normal(jax.random.fold_in(key, 101), (D, HD), jnp.float32), -6.0, 6.0)
    w_first = base_draw * D ** (-0.5)
    jitter = jnp.clip(jax.random.normal(jax.random.fold_in(key, 102), (D, HD), jnp.float32), -6.0, 6.0) * D ** (-0.5)
    w_second = jitter
    return (jnp.clip(w_first, -2.0, 2.0), w_second)


def draw_query_weight(key, part):
    return query_and_key(key)[0].astype(jnp.bfloat16)


def draw_key_weight(key, part):
    return query_and_key(key)[1].astype(jnp.bfloat16)


def draw_neighbours(key, part):
    offsets = jax.random.randint(jax.random.fold_in(key, 201), (NPTS, KNB), -HALO, HALO + 1, dtype=jnp.int32)
    offsets = offsets.at[:, 0].set(0)
    offsets = offsets.at[HALO, 1].set(-HALO)
    offsets = offsets.at[NPTS - 1 - HALO, 1].set(HALO)
    position = jnp.arange(NPTS, dtype=jnp.int32)[:, None]
    return jnp.clip(position + offsets, 0, NPTS - 1).astype(jnp.int32)


def with_spikes(array, stream_key, source, target, shards_of, factor):
    owner, partner = [(jnp.arange(array.shape[dim]) // (array.shape[dim] // shards_of)).reshape([-1 if axis == dim else 1 for axis in range(array.ndim)]) for dim in (source, target)]
    chosen = jax.random.permutation(stream_key, shards_of)[partner]
    strong = (owner == chosen) | (owner == (partner + shards_of // 2) % shards_of)
    return jnp.where(strong, factor * array, array)


def levels(stream_key, extent, cuts, least, largest):
    level = 1.0
    for dim, parts in cuts:
        heights = jax.random.uniform(jax.random.fold_in(jax.random.fold_in(stream_key, 6), dim), (parts,), jnp.float32, least / len(cuts), largest / len(cuts))
        level = level * jnp.repeat(jnp.exp(heights), extent[dim] // parts).reshape((-1,) + (1,) * (len(extent) - 1 - dim))
    return level


def bell_draw(key, shape, scale, limit, shards=(), held_as=jnp.bfloat16):
    drawn = jax.random.normal(key, shape, jnp.float32) * scale
    if len(shards) > 0:
        drawn = levels(key, shape, shards, -0.22, 0.18) * drawn
    return jnp.clip(drawn, min=-limit, max=limit).astype(held_as)


def noise_with(key, extent, scale, bound, cuts, heavy, kind=jnp.bfloat16):
    array = scale * jax.random.normal(key, extent, jnp.float32)
    if cuts:
        array = array * levels(key, extent, cuts, -0.22, 0.18)
    return jnp.clip(with_spikes(array, jax.random.fold_in(key, 3), *heavy), -bound, bound).astype(kind)


def setup_inputs(seed: int = 0) -> dict:
    keys = jax.random.split(jax.random.key(seed), 10)
    return {
        "states": noise_with(keys[0], (ENSEMBLE_SIZE, NPTS, D), 1.0, 16.0, ((0, 8), (1, 64)), (1, 2, 64, 4.0)),
        "norm_scale_vector": jnp.clip(1.0 + 0.18 * jax.random.normal(keys[1], (D,), jnp.float32), 0.1, 1.9),
        "query_weight": draw_query_weight(jax.random.fold_in(keys[9], 71), 0),
        "key_weight": draw_key_weight(jax.random.fold_in(keys[9], 71), 0),
        "value_weight": bell_draw(keys[4], (D, HD), D ** -0.5, 0.1875, ((0, 64),)),
        "output_weight": bell_draw(keys[5], (HD, D), HD ** -0.5, 0.25, ((0, 64),)),
        "head_weight": bell_draw(keys[6], (D, NVAR), NVAR ** -0.5, 0.5, ((0, 64),)),
        "neighbours": draw_neighbours(jax.random.fold_in(keys[9], 71), 0),
        "observed": bell_draw(keys[8], (NPTS, NVAR), 3.0, 16.0, ((0, 64),), jnp.float32),
    }


epsilon = 1e-05
smooth = 0.1

def layer_norm(states, norm_scale_vector):
    values = states.astype(jnp.float32)
    center = values - lax.optimization_barrier(jnp.mean(values, axis=-1, keepdims=True))
    inverse_spread = lax.rsqrt(lax.optimization_barrier(jnp.mean(center * center, axis=-1, keepdims=True)) + epsilon)
    return (center * inverse_spread, inverse_spread)

def gradient_of(spread):
    return spread / jnp.sqrt(spread * spread + smooth * smooth)

def attend(query_rows, gathered):
    number = query_rows.shape[0]
    query_heads = query_rows.astype(jnp.float32).reshape(number, HEADS, HDIM)
    key_heads = gathered[:, :, :HD].astype(jnp.float32).reshape(number, KNB, HEADS, HDIM)
    value_heads = gathered[:, :, HD:].astype(jnp.float32).reshape(number, KNB, HEADS, HDIM)
    scores = jnp.einsum('rhe,rkhe->rhk', query_heads, key_heads) * (1.0 / math.sqrt(HDIM))
    highest = lax.optimization_barrier(jnp.max(scores, axis=-1, keepdims=True))
    exponent = jnp.exp(scores - highest)
    attention = exponent / lax.optimization_barrier(jnp.sum(exponent, axis=-1, keepdims=True))
    attention_cast = attention.astype(jnp.bfloat16)
    attended_rows = jnp.einsum('rhk,rkhe->rhe', attention_cast.astype(jnp.float32), value_heads)
    return (attended_rows.reshape(number, HD).astype(jnp.bfloat16), attention, attention_cast)

def attend_back(query_rows, gathered, attention, attention_cast, grad_mixed):
    number = query_rows.shape[0]
    query_heads = query_rows.astype(jnp.float32).reshape(number, HEADS, HDIM)
    key_heads = gathered[:, :, :HD].astype(jnp.float32).reshape(number, KNB, HEADS, HDIM)
    value_heads = gathered[:, :, HD:].astype(jnp.float32).reshape(number, KNB, HEADS, HDIM)
    grad_heads = grad_mixed.astype(jnp.float32).reshape(number, HEADS, HDIM)
    grad_prob = jnp.einsum('rhe,rkhe->rhk', grad_heads, value_heads)
    grad_score = attention * (grad_prob - lax.optimization_barrier(jnp.sum(attention * grad_prob, axis=-1, keepdims=True))) * (1.0 / math.sqrt(HDIM))
    grad_query = jnp.einsum('rhk,rkhe->rhe', grad_score, key_heads)
    grad_keys = jnp.einsum('rhk,rhe->rkhe', grad_score, query_heads)
    grad_values = jnp.einsum('rhk,rhe->rkhe', attention_cast.astype(jnp.float32), grad_heads)
    returned = jnp.concatenate([grad_keys.reshape(number, KNB, HD), grad_values.reshape(number, KNB, HD)], axis=-1)
    return (grad_query.reshape(number, HD).astype(jnp.bfloat16), returned)

def forward_pass(states, norm_scale_vector, query_weight, key_weight, value_weight, output_weight, head_weight, neighbours):
    centred_rows, inverse_spread = layer_norm(states, norm_scale_vector)
    normed = (centred_rows * norm_scale_vector).astype(jnp.bfloat16)
    query_rows = jnp.dot(normed, query_weight, preferred_element_type=jnp.float32).astype(jnp.bfloat16)
    key_part = jnp.dot(normed, key_weight, preferred_element_type=jnp.float32).astype(jnp.bfloat16)
    value_part = jnp.dot(normed, value_weight, preferred_element_type=jnp.float32).astype(jnp.bfloat16)
    key_value_pair = jnp.concatenate([key_part, value_part], axis=1)

    def one_block(pair_rows):
        row_block, nearby = pair_rows
        mixed_rows, attention, attention_cast = attend(row_block, jnp.take(key_value_pair, nearby, axis=0))
        return mixed_rows
    attended_rows = lax.map(one_block, (query_rows.reshape(N_GRID, P_DEV, HD), neighbours.reshape(N_GRID, P_DEV, KNB))).reshape(NPTS, HD)
    layer_output = (states.astype(jnp.float32) + jnp.dot(attended_rows, output_weight, preferred_element_type=jnp.float32)).astype(jnp.bfloat16)
    member_prediction = jnp.dot(layer_output, head_weight, preferred_element_type=jnp.float32)
    return (centred_rows, inverse_spread, query_rows, key_value_pair, attended_rows, layer_output, member_prediction)

def reference(states, norm_scale_vector, query_weight, key_weight, value_weight, output_weight, head_weight, neighbours, observed):

    def prediction_only(ensemble_states):
        return forward_pass(ensemble_states, norm_scale_vector, query_weight, key_weight, value_weight, output_weight, head_weight, neighbours)[6]
    ensemble_predictions = lax.map(prediction_only, states)
    pairwise_total = jnp.zeros_like(ensemble_predictions)
    for member_index in range(ENSEMBLE_SIZE):
        pairwise_total = pairwise_total + gradient_of(ensemble_predictions - ensemble_predictions[member_index][None])
    prediction_gradient = (gradient_of(ensemble_predictions - observed[None]) - pairwise_total / (ENSEMBLE_SIZE - 1)).astype(jnp.bfloat16)

    def member_step(totals, item):
        ensemble_states, member_grad = item
        centred_rows, inverse_spread, query_rows, key_value_pair, attended_rows, layer_output, member_prediction = forward_pass(ensemble_states, norm_scale_vector, query_weight, key_weight, value_weight, output_weight, head_weight, neighbours)
        grad_output = jnp.dot(member_grad, head_weight.T, preferred_element_type=jnp.float32)
        output_cast = grad_output.astype(jnp.bfloat16)
        grad_mixed = jnp.dot(output_cast, output_weight.T, preferred_element_type=jnp.float32).astype(jnp.bfloat16)
        mixing_total = totals[0] + jnp.dot(attended_rows.astype(jnp.float32).T, grad_output, precision=lax.Precision.HIGHEST)
        head_total = totals[1] + jnp.dot(layer_output.T, member_grad, preferred_element_type=jnp.float32)

        def block_back(accumulated, triple):
            row_block, nearby, grad_rows = triple
            gathered = jnp.take(key_value_pair, nearby, axis=0)
            mixed_rows, attention, attention_cast = attend(row_block, gathered)
            grad_query, returned = attend_back(row_block, gathered, attention, attention_cast, grad_rows)
            accumulated = accumulated.at[nearby.reshape(-1)].add(returned.reshape(-1, 2 * HD))
            return (accumulated, grad_query)
        accumulated, grad_query = lax.scan(block_back, jnp.zeros((NPTS, 2 * HD), jnp.float32), (query_rows.reshape(N_GRID, P_DEV, HD), neighbours.reshape(N_GRID, P_DEV, KNB), grad_mixed.reshape(N_GRID, P_DEV, HD)))
        grad_query = grad_query.reshape(NPTS, HD)
        grad_keys = accumulated[:, :HD].astype(jnp.bfloat16)
        grad_values = accumulated[:, HD:].astype(jnp.bfloat16)
        grad_normed = jnp.dot(grad_query, query_weight.T, preferred_element_type=jnp.float32)
        grad_normed = grad_normed + jnp.dot(grad_keys, key_weight.T, preferred_element_type=jnp.float32)
        grad_normed = grad_normed + jnp.dot(grad_values, value_weight.T, preferred_element_type=jnp.float32)
        grad_centred = grad_normed * norm_scale_vector
        grad_states = inverse_spread * (grad_centred - lax.optimization_barrier(jnp.mean(grad_centred, axis=-1, keepdims=True)) - centred_rows * lax.optimization_barrier(jnp.mean(grad_centred * centred_rows, axis=-1, keepdims=True)))
        return ((mixing_total, head_total), ((grad_output + grad_states).astype(jnp.bfloat16), accumulated))
    starting = (jnp.zeros((HD, D), jnp.float32), jnp.zeros((D, NVAR), jnp.float32))
    totals, member_outputs = lax.scan(member_step, starting, (states, prediction_gradient))
    grad_input, grad_key_value = member_outputs
    scaling = 1.0 / math.sqrt(ENSEMBLE_SIZE * NPTS)
    return (grad_input, totals[0] * scaling, totals[1] * scaling, grad_key_value)
```

```python
import functools
import math

import jax
import jax.numpy as jnp
from jax import lax
from jax.experimental import pallas as pl
from jax.experimental.pallas import tpu as pltpu
from jax.sharding import Mesh, PartitionSpec as P

HEADS = 8
HDIM = 64
KNB = 8
HALO = 32
PTS = 128
EXT = PTS + 2 * HALO
D = 1024
HD = 512
NVAR = 128
LANE = 128

epsilon = 1e-05
smooth = 0.1

MEMBER = ("zl", "core")
GRID = ("zh", "y", "x")
PLANE = ("y", "x")
COLUMN = ("zl", "core", "zh")

BF = jnp.bfloat16
F32 = jnp.float32
VM = pl.BlockSpec(memory_space=pltpu.VMEM)
SM = pl.BlockSpec(memory_space=pltpu.SMEM)
HB = pl.BlockSpec(memory_space=pl.ANY)


def nn(a, b):
    return lax.dot_general(a, b, (((1,), (0,)), ((), ())), preferred_element_type=F32)


def nt(a, b):
    return lax.dot_general(a, b, (((1,), (1,)), ((), ())), preferred_element_type=F32)


def tn(a, b):
    return lax.dot_general(a, b, (((0,), (0,)), ((), ())), preferred_element_type=F32)


def call(body, outs, args, specs=None, scratch=(), cost=(1e9, 4e6), limit=40 << 20):
    return pl.pallas_call(
        body,
        out_shape=tuple(jax.ShapeDtypeStruct(s, d) for s, d in outs),
        in_specs=list(specs) if specs is not None else [VM] * len(args),
        out_specs=tuple(VM for _ in outs),
        scratch_shapes=list(scratch),
        compiler_params=pltpu.CompilerParams(vmem_limit_bytes=limit),
        cost_estimate=pl.CostEstimate(
            flops=int(cost[0]), bytes_accessed=int(cost[1]), transcendentals=0
        ),
    )(*args)


def normalised(rows):
    values = rows.astype(F32)
    center = values - jnp.mean(values, axis=-1, keepdims=True)
    inverse = lax.rsqrt(jnp.mean(center * center, axis=-1, keepdims=True) + epsilon)
    return center * inverse, inverse


def prepare_body(before, own, after, scale, rel, normed, count):
    for part, at in ((before, 0), (own, HALO), (after, HALO + PTS)):
        centred, _ = normalised(part[...])
        normed[at : at + part.shape[0], :] = (centred * scale[...]).astype(BF)
    place = lax.broadcasted_iota(jnp.int32, (PTS, EXT), 1)
    total = jnp.zeros((PTS, EXT), F32)
    for k in range(KNB):
        total = total + (place == rel[:, k : k + 1]).astype(F32)
    count[...] = total


def halves(tile_shape, head):
    lane = lax.broadcasted_iota(jnp.int32, tile_shape, 1)
    return (lane < HDIM) if head == 0 else (lane >= HDIM)


def forward_body(
    zh_n, rs, ro, core, normed, states, count, own, other,
    wqkv, wout, whead, q, kv, probs, mixed, out, fore, sq, so, sh,
):
    pn = wqkv.shape[0] // zh_n
    qrows = 6 * rs
    orows = 4 * ro

    def pieces(buf, c):
        for zh in range(zh_n):
            at = pl.ds(zh * pn, pn)
            for t in range(6):
                yield (
                    buf.at[:, zh, pl.ds(t * rs, rs), :],
                    wqkv.at[at, :, pl.ds((6 * c + t) * LANE, LANE)],
                    sq.at[c, zh, t],
                )
            for t in range(4):
                yield (
                    buf.at[:, zh, pl.ds(qrows + t * ro, ro), :],
                    wout.at[at, :, pl.ds((4 * c + t) * LANE, LANE)],
                    so.at[c, zh, t],
                )
            yield (
                buf.at[:, zh, pl.ds(qrows + orows, rs // 2), :],
                whead.at[at, c],
                sh.at[c, zh],
            )

    def begin(a, b):
        for src, dst, sem in pieces(a, 0):
            pltpu.make_async_copy(src, dst, sem).start()
        for src, dst, sem in pieces(b, 1):
            pltpu.make_async_copy(src, dst, sem).start()

    @pl.when(core[0] == 0)
    def _():
        begin(own, other)

    @pl.when(core[0] != 0)
    def _():
        begin(other, own)

    for c in range(2):
        for src, dst, sem in pieces(own, c):
            pltpu.make_async_copy(src, dst, sem).wait()

    rows = normed[...]
    weights = wqkv[...].reshape(D, 3 * HD)
    q[...] = nn(rows[HALO : HALO + PTS], weights[:, :HD]).astype(BF)
    kv[...] = nn(rows, weights[:, HD:]).astype(BF)
    times = count[...]
    here = times > 0
    for pair in range(HEADS // 2):
        at = pl.ds(pair * LANE, LANE)
        q2, k2, v2 = q[:, at], kv[:, at], kv[:, pl.ds(HD + pair * LANE, LANE)]
        got = []
        for side in range(2):
            chosen = jnp.where(halves((PTS, LANE), side), q2, jnp.zeros_like(q2))
            score = nt(chosen, k2) * (1.0 / math.sqrt(HDIM))
            score = jnp.where(here, score, -1e30)
            highest = jnp.max(score, axis=-1, keepdims=True)
            power = jnp.exp(score - highest)
            prob = power / jnp.sum(times * power, axis=-1, keepdims=True)
            prob = prob.astype(BF)
            probs[2 * pair + side] = prob
            got.append(nn((times * prob.astype(F32)).astype(BF), v2))
        mixed[:, at] = jnp.where(halves((PTS, LANE), 0), got[0], got[1]).astype(BF)
    flat_out = wout[...].astype(F32).reshape(HD, D).astype(BF)
    flat_head = whead[...].astype(F32).reshape(D, NVAR).astype(BF)
    layer = (states[...].astype(F32) + nn(mixed[...], flat_out)).astype(BF)
    out[...] = layer
    fore[...] = nn(layer, flat_head)


def slope(z):
    return z * lax.rsqrt(z * z + smooth * smooth)


def score_body(members, zh_n, every, fore, observed, mixed, out, gf, wg):
    mine = fore[...]
    total = jnp.zeros_like(mine)
    for m in range(members):
        total = total + slope(mine - every[m])
    grad = (slope(mine - observed[...]) - total * (1.0 / (members - 1))).astype(BF)
    gf[...] = grad
    pn = wg.shape[0]
    heads = tn(out[...], grad)
    factor = tn(mixed[...], grad)
    rb, ra = D // (zh_n * pn), HD // (zh_n * pn)
    for zh in range(zh_n):
        wg[:, zh, 0:rb, :] = (
            heads[zh * pn * rb : (zh + 1) * pn * rb].reshape(pn, rb, NVAR).astype(BF)
        )
        wg[:, zh, rb : rb + ra, :] = (
            factor[zh * pn * ra : (zh + 1) * pn * ra].reshape(pn, ra, NVAR).astype(BF)
        )


def backward_body(gf, whead, wout, q, kv, probs, count, gq, mid, lower, upper):
    flat_out = wout[...].astype(F32).reshape(HD, D).astype(BF)
    flat_head = whead[...].astype(F32).reshape(D, NVAR).astype(BF)
    go = nt(gf[...], flat_head).astype(BF)
    gm = nt(go, flat_out).astype(BF)
    times = count[...]
    for pair in range(HEADS // 2):
        at = pl.ds(pair * LANE, LANE)
        vat = pl.ds(HD + pair * LANE, LANE)
        q2, k2, v2 = q[:, at], kv[:, at], kv[:, vat]
        g2 = gm[:, pair * LANE : (pair + 1) * LANE]
        gqs, gks, gvs = [], [], []
        for side in range(2):
            chosen = jnp.where(halves((PTS, LANE), side), g2, jnp.zeros_like(g2))
            gp = nt(chosen, v2)
            weight = times * probs[2 * pair + side].astype(F32)
            centre = jnp.sum(weight * gp, axis=-1, keepdims=True)
            gs = (weight * (gp - centre) * (1.0 / math.sqrt(HDIM))).astype(BF)
            gqs.append(nn(gs, k2))
            gks.append(tn(gs, q2))
            gvs.append(tn(weight.astype(BF), g2))
        gq[:, at] = jnp.where(halves((PTS, LANE), 0), gqs[0], gqs[1]).astype(BF)
        pick = halves((EXT, LANE), 0)
        for where_at, parts in ((at, gks), (vat, gvs)):
            total = jnp.where(pick, parts[0], parts[1])
            lower[:, where_at] = total[:HALO].astype(BF)
            mid[:, where_at] = total[HALO : HALO + PTS]
            upper[:, where_at] = total[HALO + PTS :].astype(BF)


def final_body(states, scale, gf, whead, wqkv, gq, mid, first, last, total, grad):
    flat_head = whead[...].astype(F32).reshape(D, NVAR).astype(BF)
    total[...] = mid[...]
    total[:HALO, :] += first[...].astype(F32)
    total[PTS - HALO :, :] += last[...].astype(F32)
    kvs = total[...].astype(BF)
    weights = wqkv[...].reshape(D, 3 * HD)
    gn = nt(gq[...], weights[:, :HD]) + nt(kvs, weights[:, HD:])
    centred, inverse = normalised(states[...])
    g = gn * scale[...]
    back = inverse * (
        g
        - jnp.mean(g, axis=-1, keepdims=True)
        - centred * jnp.mean(g * centred, axis=-1, keepdims=True)
    )
    grad[...] = (nt(gf[...], flat_head) + back).astype(BF)


def weights_body(scaling, parts, whead, mixing, head):
    flat_head = whead[...].astype(F32).reshape(D, NVAR).astype(BF)
    rb = head.shape[0]
    total = jnp.zeros(parts.shape[1:], F32)
    for i in range(parts.shape[0]):
        total = total + parts[i].astype(F32)
    total = total * scaling
    head[...] = total[:rb]
    factor = total[rb:]
    high = factor.astype(BF)
    low = (factor - high.astype(F32)).astype(BF)
    mixing[...] = nt(high, flat_head) + nt(low, flat_head)


def to_all(x, axes):
    n = lax.axis_size(axes)
    return lax.all_to_all(
        jnp.broadcast_to(x[None], (n, *x.shape)), axes, 0, 0, tiled=True
    )


def packed_half(query, key, value, out, head, core):
    qkv = jnp.concatenate([query, key, value], axis=1)
    rs, ro = qkv.shape[0], out.shape[0]

    def half(c):
        cols = [qkv[:, (6 * c + t) * LANE : (6 * c + t + 1) * LANE] for t in range(6)]
        cols += [out[:, (4 * c + t) * LANE : (4 * c + t + 1) * LANE] for t in range(4)]
        cols += [head[c * rs // 2 : (c + 1) * rs // 2]]
        return jnp.concatenate(cols, axis=0)

    return jnp.where(core == 0, half(0), half(1))


def gathered_halves(mine):
    column = to_all(mine, "zh")
    plane = to_all(column, PLANE)
    return plane, lax.ppermute(plane, "core", [(0, 1), (1, 0)])


def shards(
    states, norm_scale, query, key, value, out_w, head_w, neighbours, observed
):
    members = lax.axis_size(MEMBER)
    devices = lax.axis_size(GRID)
    zh_n = lax.axis_size("zh")
    pn = lax.axis_size(PLANE)
    core = lax.axis_index("core")
    inputs = states[0]
    rs, ro = query.shape[0], out_w.shape[0]

    up = [(i, i + 1) for i in range(devices - 1)]
    down = [(j, i) for i, j in up]
    own, other = gathered_halves(
        packed_half(query, key, value, out_w, head_w, core)
    )
    before = lax.ppermute(inputs[PTS - HALO :], GRID, up)
    after = lax.ppermute(inputs[:HALO], GRID, down)
    rel = neighbours - (lax.axis_index(GRID) * PTS - HALO)
    scale = norm_scale.reshape(1, D)
    normed, count = call(
        prepare_body,
        [((EXT, D), BF), ((PTS, EXT), F32)],
        (before, inputs, after, scale, rel),
        cost=(4e6, 1e6),
    )
    wqkv, wout, whead, q, kv, probs, mixed, out, fore = call(
        functools.partial(forward_body, zh_n, rs, ro),
        [
            ((devices, rs, 3 * HD), BF),
            ((devices, ro, D), BF),
            ((devices, 2, rs // 2, NVAR), BF),
            ((PTS, HD), BF),
            ((EXT, D), BF),
            ((HEADS, PTS, EXT), BF),
            ((PTS, HD), BF),
            ((PTS, D), BF),
            ((PTS, NVAR), F32),
        ],
        (core.reshape(1).astype(jnp.int32), normed, inputs, count, own, other),
        specs=(SM, VM, VM, VM, HB, HB),
        scratch=(
            pltpu.SemaphoreType.DMA((2, zh_n, 6)),
            pltpu.SemaphoreType.DMA((2, zh_n, 4)),
            pltpu.SemaphoreType.DMA((2, zh_n)),
        ),
        cost=(2e9, 1e7),
    )
    every = to_all(fore, MEMBER)
    gf, wg = call(
        functools.partial(score_body, members, zh_n),
        [
            ((PTS, NVAR), BF),
            ((pn, zh_n, (D + HD) // devices, NVAR), BF),
        ],
        (every, fore, observed, mixed, out),
        cost=(1e8, 2e6),
    )
    plane = lax.all_to_all(wg, PLANE, 0, 0, tiled=True)
    gq, mid, lower, upper = call(
        backward_body,
        [((PTS, HD), BF), ((PTS, D), F32), ((HALO, D), BF), ((HALO, D), BF)],
        (gf, whead, wout, q, kv, probs, count),
        cost=(1e9, 4e6),
    )
    last = lax.ppermute(lower, GRID, down)
    first = lax.ppermute(upper, GRID, up)
    total, grad_input = call(
        final_body,
        [((PTS, D), F32), ((PTS, D), BF)],
        (inputs, scale, gf, whead, wqkv, gq, mid, first, last),
        cost=(1e9, 4e6),
    )
    partial = jnp.sum(plane.astype(F32), axis=0).astype(BF)
    spread = jnp.broadcast_to(partial[None], (members, *partial.shape))
    parts = lax.all_to_all(
        spread.reshape(members * zh_n, *partial.shape[1:]), COLUMN, 0, 0, tiled=True
    )
    scaling = 1.0 / math.sqrt(members * devices * PTS)
    mixing, head = call(
        functools.partial(weights_body, scaling),
        [((HD // devices, D), F32), ((D // devices, NVAR), F32)],
        (parts, whead),
        cost=(1e8, 1e6),
    )
    return grad_input[None], mixing, head, total[None]


def refined(mesh):
    members, devices = mesh.shape["member"], mesh.shape["grid"]
    cut = {64: (4, 4, 4), 4: (1, 2, 2), 8: (2, 2, 2)}[devices]
    return Mesh(
        mesh.devices.reshape(members // 2, 2, *cut), ("zl", "core", "zh", "y", "x")
    )


def solution(mesh):
    rows = P(GRID, None)
    return jax.shard_map(
        shards,
        mesh=refined(mesh),
        in_specs=(
            P(MEMBER, GRID, None),
            P(),
            rows,
            rows,
            rows,
            rows,
            rows,
            rows,
            rows,
        ),
        out_specs=(P(MEMBER, GRID, None), rows, rows, P(MEMBER, GRID, None)),
        check_vma=False,
    )
```

```python
import functools
import math

import jax
import jax.numpy as jnp
from jax import lax
from jax.experimental import pallas as pl
from jax.experimental.pallas import tpu as pltpu
from jax.sharding import Mesh, PartitionSpec as P


HEADS = 8
HDIM = 64
KNB = 8
HALO = 32
PTS = 128
EXT = PTS + 2 * HALO
D = 1024
HD = 512
NVAR = 128
LANE = 128

epsilon = 1e-05
smooth = 0.1

MEMBER = ("zl", "core")
GRID = ("zh", "y", "x")
PLANE = ("y", "x")
COLUMN = ("zl", "core", "zh")

BF = jnp.bfloat16
F32 = jnp.float32


def nn(a, b):
    return lax.dot_general(a, b, (((1,), (0,)), ((), ())), preferred_element_type=F32)


def nt(a, b):
    return lax.dot_general(a, b, (((1,), (1,)), ((), ())), preferred_element_type=F32)


def tn(a, b):
    return lax.dot_general(a, b, (((0,), (0,)), ((), ())), preferred_element_type=F32)


SPECS = {
    "V": pl.BlockSpec(memory_space=pltpu.VMEM),
    "A": pl.BlockSpec(),
    "H": pl.BlockSpec(memory_space=pltpu.HBM),
}


def call(body, outs, args, places, scratch=(), cost=(1e9, 4e6), limit=16):
    taken, given = places.split(">")
    shapes = [
        jax.ShapeDtypeStruct(s, d) if at == "V" else pltpu.HBM(s, d)
        for (s, d), at in zip(outs, given, strict=True)
    ]
    args = [
        x if at == "V" else pltpu.with_memory_space_constraint(x, pltpu.HBM)
        for x, at in zip(args, taken, strict=True)
    ]
    return pl.pallas_call(
        body,
        out_shape=tuple(shapes),
        in_specs=[SPECS[at] for at in taken],
        out_specs=tuple(SPECS[at] for at in given),
        scratch_shapes=list(scratch),
        compiler_params=pltpu.CompilerParams(vmem_limit_bytes=limit << 20),
        cost_estimate=pl.CostEstimate(
            flops=int(cost[0]), bytes_accessed=int(cost[1]), transcendentals=0
        ),
    )(*args)


def normalised(rows):
    values = rows.astype(F32)
    center = values - jnp.mean(values, axis=-1, keepdims=True)
    inverse = lax.rsqrt(jnp.mean(center * center, axis=-1, keepdims=True) + epsilon)
    return center * inverse, inverse


def prepare_body(before, own, after, scale, rel, normed, count):
    for part, at in ((before, 0), (own, HALO), (after, HALO + PTS)):
        centred, _ = normalised(part[...])
        normed[at : at + part.shape[0], :] = (centred * scale[...]).astype(BF)
    place = lax.broadcasted_iota(jnp.int32, (PTS, EXT), 1)
    total = jnp.zeros((PTS, EXT), F32)
    for k in range(KNB):
        total = total + (place == rel[:, k : k + 1]).astype(F32)
    count[...] = total


def halves(tile_shape, head):
    lane = lax.broadcasted_iota(jnp.int32, tile_shape, 1)
    return (lane < HDIM) if head == 0 else (lane >= HDIM)


def fetched(pairs, sems):
    return [pltpu.make_async_copy(s, d, sems.at[i]) for i, (s, d) in enumerate(pairs)]


def send_out(pairs, sems):
    copies = fetched(pairs, sems)
    for copy in copies:
        copy.start()
    for copy in copies:
        copy.wait()


def pack_body(query, key, value, out, head, mine, plane, sems):
    rs, ro = query.shape[0], out.shape[0]

    def put(row, tile):
        size = tile.shape[0]
        mine[row : row + size, :] = tile

    for c in range(2):

        @pl.when(lax.axis_index("core") == c)
        def _():
            for t in range(6):
                weight = (query, key, value)[(6 * c + t) // 4]
                lane = (6 * c + t) % 4 * LANE
                put(t * rs, weight[:, lane : lane + LANE])
            for t in range(4):
                lane = (4 * c + t) * LANE
                put(6 * rs + t * ro, out[:, lane : lane + LANE])
            put(6 * rs + 4 * ro, head[c * rs // 2 : (c + 1) * rs // 2, :])

    send_out([(mine, plane.at[i]) for i in range(plane.shape[0])], sems)


def rest_body(*refs):
    *blocks, rest, sems = refs
    send_out(
        [
            (block, rest.at[i, k])
            for k, block in enumerate(blocks)
            for i in range(rest.shape[0])
        ],
        sems,
    )


def forward_body(
    zh_n, rs, ro, normed, states, count, own0, other0, own1, other1,
    wqkv_out, wout_out, whead_out, q_out, kv_out, probs_out, mixed, out, fore,
    wqkv, wout, whead, q, kv, probs, sq, so, sh, sems,
):
    core, zh = lax.axis_index("core"), lax.axis_index("zh")

    def leaving(i):
        src, dst = (
            (wqkv, wqkv_out),
            (wout, wout_out),
            (whead, whead_out),
            (q, q_out),
            (kv, kv_out),
            (probs, probs_out),
        )[i]
        return pltpu.make_async_copy(src, dst, sems.at[i])

    pn = wqkv.shape[0] // zh_n
    qrows = 6 * rs
    orows = 4 * ro

    def pieces(first, rest, c):
        for k in range(zh_n):
            at = pl.ds(lax.rem(zh + k, zh_n) * pn, pn)

            def rows(start, size):
                if k == 0:
                    return first.at[:, pl.ds(start, size), :]
                return rest.at[:, k - 1, pl.ds(start, size), :]

            for t in range(6):
                yield (
                    rows(t * rs, rs),
                    wqkv.at[at, :, pl.ds((6 * c + t) * LANE, LANE)],
                    sq.at[c, k, t],
                )
            for t in range(4):
                yield (
                    rows(qrows + t * ro, ro),
                    wout.at[at, :, pl.ds((4 * c + t) * LANE, LANE)],
                    so.at[c, k, t],
                )
            yield rows(qrows + orows, rs // 2), whead.at[at, c], sh.at[c, k]

    def begin(a, b):
        for c, pair in enumerate((a, b)):
            for src, dst, sem in pieces(*pair, c):
                pltpu.make_async_copy(src, dst, sem).start()

    @pl.when(core == 0)
    def _():
        begin((own0, own1), (other0, other1))

    @pl.when(core != 0)
    def _():
        begin((other0, other1), (own0, own1))

    for c in range(2):
        for src, dst, sem in pieces(own0, own1, c):
            pltpu.make_async_copy(src, dst, sem).wait()

    for i in range(3):
        leaving(i).start()
    rows = normed[...]
    weights = wqkv[...].reshape(D, 3 * HD)
    q[...] = nn(rows[HALO : HALO + PTS], weights[:, :HD]).astype(BF)
    kv[...] = nn(rows, weights[:, HD:]).astype(BF)
    for i in range(3, 5):
        leaving(i).start()
    times = count[...]
    here = times > 0
    for pair in range(HEADS // 2):
        at = pl.ds(pair * LANE, LANE)
        q2, k2, v2 = q[:, at], kv[:, at], kv[:, pl.ds(HD + pair * LANE, LANE)]
        got = []
        for side in range(2):
            chosen = jnp.where(halves((PTS, LANE), side), q2, jnp.zeros_like(q2))
            score = nt(chosen, k2) * (1.0 / math.sqrt(HDIM))
            score = jnp.where(here, score, -1e30)
            highest = jnp.max(score, axis=-1, keepdims=True)
            power = jnp.exp(score - highest)
            prob = power / jnp.sum(times * power, axis=-1, keepdims=True)
            weight = (times * prob.astype(BF).astype(F32)).astype(BF)
            probs[2 * pair + side] = weight
            got.append(nn(weight, v2))
        mixed[:, at] = jnp.where(halves((PTS, LANE), 0), got[0], got[1]).astype(BF)
    leaving(5).start()
    flat_out = wout[...].astype(F32).reshape(HD, D).astype(BF)
    flat_head = whead[...].astype(F32).reshape(D, NVAR).astype(BF)
    layer = (states[...].astype(F32) + nn(mixed[...], flat_out)).astype(BF)
    out[...] = layer
    mine = nn(layer, flat_head)
    for i in range(fore.shape[0]):
        fore[i] = mine
    for i in range(6):
        leaving(i).wait()


def slope(z):
    return z * lax.rsqrt(z * z + smooth * smooth)


def score_body(members, zh_n, every, fore, observed, mixed, out, gf, wg):
    mine = fore[0]
    total = jnp.zeros_like(mine)
    for m in range(members):
        total = total + slope(mine - every[m])
    grad = (slope(mine - observed[...]) - total * (1.0 / (members - 1))).astype(BF)
    gf[...] = grad
    pn = wg.shape[0]
    heads = tn(out[...], grad)
    factor = tn(mixed[...], grad)
    rb, ra = D // (zh_n * pn), HD // (zh_n * pn)
    for zh in range(zh_n):
        wg[:, zh, 0:rb, :] = (
            heads[zh * pn * rb : (zh + 1) * pn * rb].reshape(pn, rb, NVAR).astype(BF)
        )
        wg[:, zh, rb : rb + ra, :] = (
            factor[zh * pn * ra : (zh + 1) * pn * ra].reshape(pn, ra, NVAR).astype(BF)
        )


def backward_body(
    gf, whead_in, wout_in, q_in, kv_in, probs_in, gq, mid, lower, upper,
    whead, wout, q, kv, probs, sems,
):
    copies = fetched(
        (
            (whead_in, whead),
            (wout_in, wout),
            (kv_in, kv),
            (probs_in, probs),
            (q_in, q),
        ),
        sems,
    )
    for copy in copies:
        copy.start()
    copies[0].wait()
    flat_head = whead[...].astype(F32).reshape(D, NVAR).astype(BF)
    go = nt(gf[...], flat_head).astype(BF)
    copies[1].wait()
    flat_out = wout[...].astype(F32).reshape(HD, D).astype(BF)
    gm = nt(go, flat_out).astype(BF)
    for copy in copies[2:]:
        copy.wait()
    for pair in range(HEADS // 2):
        at = pl.ds(pair * LANE, LANE)
        vat = pl.ds(HD + pair * LANE, LANE)
        q2, k2, v2 = q[:, at], kv[:, at], kv[:, vat]
        g2 = gm[:, pair * LANE : (pair + 1) * LANE]
        gqs, gks, gvs = [], [], []
        for side in range(2):
            chosen = jnp.where(halves((PTS, LANE), side), g2, jnp.zeros_like(g2))
            gp = nt(chosen, v2)
            held = probs[2 * pair + side]
            weight = held.astype(F32)
            centre = jnp.sum(weight * gp, axis=-1, keepdims=True)
            gs = (weight * (gp - centre) * (1.0 / math.sqrt(HDIM))).astype(BF)
            gqs.append(nn(gs, k2))
            gks.append(tn(gs, q2))
            gvs.append(tn(held, g2))
        gq[:, at] = jnp.where(halves((PTS, LANE), 0), gqs[0], gqs[1]).astype(BF)
        pick = halves((EXT, LANE), 0)
        for where_at, parts in ((at, gks), (vat, gvs)):
            total = jnp.where(pick, parts[0], parts[1])
            lower[:, where_at] = total[:HALO].astype(BF)
            mid[:, where_at] = total[HALO : HALO + PTS]
            upper[:, where_at] = total[HALO + PTS :].astype(BF)


def final_body(
    states, scale, gf, whead_in, wqkv_in, gq, mid, first, last, total, grad,
    whead, wqkv, sems,
):
    copies = fetched(((wqkv_in, wqkv), (whead_in, whead)), sems)
    for copy in copies:
        copy.start()
    centred, inverse = normalised(states[...])
    copies[1].wait()
    flat_head = whead[...].astype(F32).reshape(D, NVAR).astype(BF)
    total[...] = mid[...]
    total[:HALO, :] += first[...].astype(F32)
    total[PTS - HALO :, :] += last[...].astype(F32)
    kvs = total[...].astype(BF)
    copies[0].wait()
    weights = wqkv[...].reshape(D, 3 * HD)
    gn = nt(gq[...], weights[:, :HD]) + nt(kvs, weights[:, HD:])
    g = gn * scale[...]
    back = inverse * (
        g
        - jnp.mean(g, axis=-1, keepdims=True)
        - centred * jnp.mean(g * centred, axis=-1, keepdims=True)
    )
    grad[...] = (nt(gf[...], flat_head) + back).astype(BF)


def spread_body(plane, spread):
    total = plane[0].astype(F32)
    for i in range(1, plane.shape[0]):
        total = total + plane[i].astype(F32)
    total = total.astype(BF)
    for i in range(spread.shape[0]):
        spread[i] = total


def weights_body(scaling, parts, whead, mixing, head):
    flat_head = whead[...].astype(F32).reshape(D, NVAR).astype(BF)
    rb = head.shape[0]
    total = jnp.zeros(parts.shape[1:], F32)
    for i in range(parts.shape[0]):
        total = total + parts[i].astype(F32)
    total = total * scaling
    head[...] = total[:rb]
    factor = total[rb:]
    high = factor.astype(BF)
    low = (factor - high.astype(F32)).astype(BF)
    mixing[...] = nt(high, flat_head) + nt(low, flat_head)


def shards(
    states, norm_scale, query, key, value, out_w, head_w, neighbours, observed
):
    members = lax.axis_size(MEMBER)
    devices = lax.axis_size(GRID)
    zh_n = lax.axis_size("zh")
    pn = lax.axis_size(PLANE)
    inputs = states[0]
    rs, ro = query.shape[0], out_w.shape[0]
    packed = 6 * rs + 4 * ro + rs // 2
    swap = [(0, 1), (1, 0)]
    up = [(i, i + 1) for i in range(devices - 1)]
    down = [(j, i) for i, j in up]

    mine, plane = call(
        pack_body,
        [((packed, LANE), BF), ((pn, packed, LANE), BF)],
        (query, key, value, out_w, head_w),
        "AAAAA>VH",
        scratch=(pltpu.SemaphoreType.DMA((pn,)),),
        cost=(1e6, 1e6),
        limit=4,
    )
    own0 = lax.all_to_all(plane, PLANE, 0, 0, tiled=True)
    blocks = []
    for k in range(1, zh_n):
        turn = [((i + k) % zh_n, i) for i in range(zh_n)]
        blocks.append(lax.ppermute(mine, "zh", turn))
    before = lax.ppermute(inputs[PTS - HALO :], GRID, up)
    after = lax.ppermute(inputs[:HALO], GRID, down)
    rel = neighbours - (lax.axis_index(GRID) * PTS - HALO)
    scale = norm_scale.reshape(1, D)
    normed, count = call(
        prepare_body,
        [((EXT, D), BF), ((PTS, EXT), F32)],
        (before, inputs, after, scale, rel),
        "VAVAA>AA",
        cost=(4e6, 1e6),
        limit=8,
    )
    (rest,) = call(
        rest_body,
        [((pn, zh_n - 1, packed, LANE), BF)],
        blocks,
        "V" * (zh_n - 1) + ">H",
        scratch=(pltpu.SemaphoreType.DMA((pn * (zh_n - 1),)),),
        cost=(1e6, 2e6),
        limit=4,
    )
    own1 = lax.all_to_all(rest, PLANE, 0, 0, tiled=True)
    other0 = lax.ppermute(own0, "core", swap)
    other1 = lax.ppermute(own1, "core", swap)
    wqkv, wout, whead, q, kv, probs, mixed, out, fore = call(
        functools.partial(forward_body, zh_n, rs, ro),
        [
            ((devices, rs, 3 * HD), BF),
            ((devices, ro, D), BF),
            ((devices, 2, rs // 2, NVAR), BF),
            ((PTS, HD), BF),
            ((EXT, D), BF),
            ((HEADS, PTS, EXT), BF),
            ((PTS, HD), BF),
            ((PTS, D), BF),
            ((members, PTS, NVAR), F32),
        ],
        (normed, inputs, count, own0, other0, own1, other1),
        "AAAVVVV>HHHHHHVVV",
        scratch=(
            pltpu.VMEM((devices, rs, 3 * HD), BF),
            pltpu.VMEM((devices, ro, D), BF),
            pltpu.VMEM((devices, 2, rs // 2, NVAR), BF),
            pltpu.VMEM((PTS, HD), BF),
            pltpu.VMEM((EXT, D), BF),
            pltpu.VMEM((HEADS, PTS, EXT), BF),
            pltpu.SemaphoreType.DMA((2, zh_n, 6)),
            pltpu.SemaphoreType.DMA((2, zh_n, 4)),
            pltpu.SemaphoreType.DMA((2, zh_n)),
            pltpu.SemaphoreType.DMA((6,)),
        ),
        cost=(2e9, 1e7),
        limit=24,
    )
    every = lax.all_to_all(fore, MEMBER, 0, 0, tiled=True)
    gf, wg = call(
        functools.partial(score_body, members, zh_n),
        [
            ((PTS, NVAR), BF),
            ((pn, zh_n, (D + HD) // devices, NVAR), BF),
        ],
        (every, fore, observed, mixed, out),
        "VVAVV>AA",
        cost=(1e8, 2e6),
        limit=8,
    )
    plane = lax.all_to_all(wg, PLANE, 0, 0, tiled=True)
    gq, mid, lower, upper = call(
        backward_body,
        [((PTS, HD), BF), ((PTS, D), F32), ((HALO, D), BF), ((HALO, D), BF)],
        (gf, whead, wout, q, kv, probs),
        "AHHHHH>AAAA",
        scratch=(
            pltpu.VMEM(whead.shape, BF),
            pltpu.VMEM(wout.shape, BF),
            pltpu.VMEM(q.shape, BF),
            pltpu.VMEM(kv.shape, BF),
            pltpu.VMEM(probs.shape, BF),
            pltpu.SemaphoreType.DMA((5,)),
        ),
        cost=(1e9, 4e6),
        limit=16,
    )
    last = lax.ppermute(lower, GRID, down)
    first = lax.ppermute(upper, GRID, up)
    (spread,) = call(
        spread_body,
        [((members, *wg.shape[1:]), BF)],
        (plane,),
        "V>A",
        cost=(1e6, 1e6),
        limit=4,
    )
    parts = lax.all_to_all(
        spread.reshape(members * zh_n, *wg.shape[2:]), COLUMN, 0, 0, tiled=True
    )
    total, grad_input = call(
        final_body,
        [((PTS, D), F32), ((PTS, D), BF)],
        (inputs, scale, gf, whead, wqkv, gq, mid, first, last),
        "AAAHHAAVV>AA",
        scratch=(
            pltpu.VMEM(whead.shape, BF),
            pltpu.VMEM(wqkv.shape, BF),
            pltpu.SemaphoreType.DMA((2,)),
        ),
        cost=(1e9, 4e6),
        limit=16,
    )
    scaling = 1.0 / math.sqrt(members * devices * PTS)
    mixing, head = call(
        functools.partial(weights_body, scaling),
        [((HD // devices, D), F32), ((D // devices, NVAR), F32)],
        (parts, whead),
        "VA>AA",
        cost=(1e8, 1e6),
        limit=8,
    )
    return grad_input[None], mixing, head, total[None]


def refined(mesh):
    members, devices = mesh.shape["member"], mesh.shape["grid"]
    cut = {64: (4, 4, 4), 4: (1, 2, 2), 8: (2, 2, 2)}[devices]
    return Mesh(
        mesh.devices.reshape(members // 2, 2, *cut), ("zl", "core", "zh", "y", "x")
    )


def solution(mesh):
    rows = P(GRID, None)

    return jax.shard_map(
        shards,
        mesh=refined(mesh),
        in_specs=(
            P(MEMBER, GRID, None),
            P(),
            rows,
            rows,
            rows,
            rows,
            rows,
            rows,
            rows,
        ),
        out_specs=(P(MEMBER, GRID, None), rows, rows, P(MEMBER, GRID, None)),
        check_vma=False,
    )
```

```python
import functools
import math

import jax
import jax.numpy as jnp
from jax import lax
from jax.experimental import pallas as pl
from jax.experimental.pallas import tpu as pltpu
from jax.sharding import Mesh, PartitionSpec as P


HEADS = 8
HDIM = 64
KNB = 8
HALO = 32
PTS = 128
EXT = PTS + 2 * HALO
D = 1024
HD = 512
NVAR = 128
LANE = 128

epsilon = 1e-05
smooth = 0.1

MEMBER = ("zl", "core")
GRID = ("zh", "y", "x")
PLANE = ("y", "x")

BF = jnp.bfloat16
F32 = jnp.float32


def nn(a, b):
    return lax.dot_general(a, b, (((1,), (0,)), ((), ())), preferred_element_type=F32)


def nt(a, b):
    return lax.dot_general(a, b, (((1,), (1,)), ((), ())), preferred_element_type=F32)


def tn(a, b):
    return lax.dot_general(a, b, (((0,), (0,)), ((), ())), preferred_element_type=F32)


SPECS = {
    "V": pl.BlockSpec(memory_space=pltpu.VMEM),
    "A": pl.BlockSpec(),
    "H": pl.BlockSpec(memory_space=pltpu.HBM),
}


def call(body, outs, args, places, scratch=(), cost=(1e9, 4e6), limit=16):
    taken, given = places.split(">")
    shapes = [
        jax.ShapeDtypeStruct(s, d) if at == "V" else pltpu.HBM(s, d)
        for (s, d), at in zip(outs, given, strict=True)
    ]
    args = [
        x if at == "V" else pltpu.with_memory_space_constraint(x, pltpu.HBM)
        for x, at in zip(args, taken, strict=True)
    ]
    return pl.pallas_call(
        body,
        out_shape=tuple(shapes),
        in_specs=[SPECS[at] for at in taken],
        out_specs=tuple(SPECS[at] for at in given),
        scratch_shapes=list(scratch),
        compiler_params=pltpu.CompilerParams(vmem_limit_bytes=limit << 20),
        cost_estimate=pl.CostEstimate(
            flops=int(cost[0]), bytes_accessed=int(cost[1]), transcendentals=0
        ),
    )(*args)


def normalised(rows):
    values = rows.astype(F32)
    center = values - jnp.mean(values, axis=-1, keepdims=True)
    inverse = lax.rsqrt(jnp.mean(center * center, axis=-1, keepdims=True) + epsilon)
    return center * inverse, inverse


def prepare_body(before, own, after, scale, rel, normed, count):
    for part, at in ((before, 0), (own, HALO), (after, HALO + PTS)):
        centred, _ = normalised(part[...])
        normed[at : at + part.shape[0], :] = (centred * scale[...]).astype(BF)
    place = lax.broadcasted_iota(jnp.int32, (PTS, EXT), 1)
    total = jnp.zeros((PTS, EXT), F32)
    for k in range(KNB):
        total = total + (place == rel[:, k : k + 1]).astype(F32)
    count[...] = total


def halves(tile_shape, head):
    lane = lax.broadcasted_iota(jnp.int32, tile_shape, 1)
    return (lane < HDIM) if head == 0 else (lane >= HDIM)


def fetched(pairs, sems):
    return [pltpu.make_async_copy(s, d, sems.at[i]) for i, (s, d) in enumerate(pairs)]


def send_out(pairs, sems):
    copies = fetched(pairs, sems)
    for copy in copies:
        copy.start()
    for copy in copies:
        copy.wait()


def pack_body(query, key, value, out, head, column, mine, sems):
    rs, ro = query.shape[0], out.shape[0]

    def put(row, tile):
        size = tile.shape[0]
        mine[row : row + size, :] = tile

    for c in range(2):

        @pl.when(lax.axis_index("core") == c)
        def _():
            for t in range(6):
                weight = (query, key, value)[(6 * c + t) // 4]
                lane = (6 * c + t) % 4 * LANE
                put(t * rs, weight[:, lane : lane + LANE])
            for t in range(4):
                lane = (4 * c + t) * LANE
                put(6 * rs + t * ro, out[:, lane : lane + LANE])
            put(6 * rs + 4 * ro, head[c * rs // 2 : (c + 1) * rs // 2, :])

    send_out([(mine, column.at[i]) for i in range(column.shape[0])], sems)


def forward_body(
    zh_n, rs, ro, normed, states, count, own, other,
    wqkv_out, wout_out, whead_out, q_out, kv_out, probs_out, mixed, out, fore, alone,
    wqkv, wout, whead, q, kv, probs, sq, so, sh, sems,
):
    core = lax.axis_index("core")

    def leaving(i):
        src, dst = (
            (wqkv, wqkv_out),
            (wout, wout_out),
            (whead, whead_out),
            (q, q_out),
            (kv, kv_out),
            (probs, probs_out),
        )[i]
        return pltpu.make_async_copy(src, dst, sems.at[i])

    pn = wqkv.shape[0] // zh_n
    qrows = 6 * rs
    orows = 4 * ro

    def inner(buf, c):
        for zh in range(zh_n):
            for t in range(6):
                yield (
                    buf.at[:, zh, pl.ds(t * rs, rs), :],
                    wqkv.at[pl.ds(zh * pn, pn), :, pl.ds((6 * c + t) * LANE, LANE)],
                    sq.at[c, zh, t],
                )

    def outer(buf, c):
        for zh in range(zh_n):
            at = pl.ds(zh * pn, pn)
            for t in range(4):
                yield (
                    buf.at[:, zh, pl.ds(qrows + t * ro, ro), :],
                    wout.at[at, :, pl.ds((4 * c + t) * LANE, LANE)],
                    so.at[c, zh, t],
                )
            yield (
                buf.at[:, zh, pl.ds(qrows + orows, rs // 2), :],
                whead.at[at, c],
                sh.at[c, zh],
            )

    def begin(*halves_of):
        for part in (inner, outer):
            for c in range(2):
                for src, dst, sem in part(halves_of[c], c):
                    pltpu.make_async_copy(src, dst, sem).start()

    def end(part):
        for c in range(2):
            for src, dst, sem in part(own, c):
                pltpu.make_async_copy(src, dst, sem).wait()

    @pl.when(core == 0)
    def _():
        begin(own, other)

    @pl.when(core != 0)
    def _():
        begin(other, own)

    end(inner)
    leaving(0).start()
    rows = normed[...]
    weights = wqkv[...].reshape(D, 3 * HD)
    q[...] = nn(rows[HALO : HALO + PTS], weights[:, :HD]).astype(BF)
    kv[...] = nn(rows, weights[:, HD:]).astype(BF)
    for i in range(3, 5):
        leaving(i).start()
    times = count[...]
    here = times > 0
    for pair in range(HEADS // 2):
        at = pl.ds(pair * LANE, LANE)
        q2, k2, v2 = q[:, at], kv[:, at], kv[:, pl.ds(HD + pair * LANE, LANE)]
        got = []
        for side in range(2):
            chosen = jnp.where(halves((PTS, LANE), side), q2, jnp.zeros_like(q2))
            score = nt(chosen, k2) * (1.0 / math.sqrt(HDIM))
            score = jnp.where(here, score, -1e30)
            highest = jnp.max(score, axis=-1, keepdims=True)
            power = jnp.exp(score - highest)
            prob = power / jnp.sum(times * power, axis=-1, keepdims=True)
            weight = (times * prob.astype(BF).astype(F32)).astype(BF)
            probs[2 * pair + side] = weight
            got.append(nn(weight, v2))
        mixed[:, at] = jnp.where(halves((PTS, LANE), 0), got[0], got[1]).astype(BF)
    leaving(5).start()
    end(outer)
    for i in range(1, 3):
        leaving(i).start()
    flat_out = wout[...].astype(F32).reshape(HD, D).astype(BF)
    flat_head = whead[...].astype(F32).reshape(D, NVAR).astype(BF)
    layer = (states[...].astype(F32) + nn(mixed[...], flat_out)).astype(BF)
    out[...] = layer
    mine = nn(layer, flat_head)
    alone[...] = mine
    for i in range(fore.shape[0]):
        fore[i] = mine.astype(BF)
    for i in range(6):
        leaving(i).wait()


def slope(z):
    return z * lax.rsqrt(z * z + smooth * smooth)


def score_body(members, zh_n, every, alone, observed, mixed, out, gf, wg):
    mine = alone[...]
    sent = mine.astype(BF).astype(F32)
    total = jnp.zeros_like(mine)
    for m in range(members):
        total = total + slope(sent - every[m].astype(F32))
    grad = (slope(mine - observed[...]) - total * (1.0 / (members - 1))).astype(BF)
    gf[...] = grad
    pn = wg.shape[0]
    heads = tn(out[...], grad)
    factor = tn(mixed[...], grad)
    rb, ra = D // (zh_n * pn), HD // (zh_n * pn)
    for zh in range(zh_n):
        wg[:, zh, 0:rb, :] = (
            heads[zh * pn * rb : (zh + 1) * pn * rb].reshape(pn, rb, NVAR).astype(BF)
        )
        wg[:, zh, rb : rb + ra, :] = (
            factor[zh * pn * ra : (zh + 1) * pn * ra].reshape(pn, ra, NVAR).astype(BF)
        )


def backward_body(
    gf, whead_in, wout_in, q_in, kv_in, probs_in, gq, mid, lower, upper,
    whead, wout, q, kv, probs, sems,
):
    copies = fetched(
        (
            (whead_in, whead),
            (wout_in, wout),
            (kv_in, kv),
            (probs_in, probs),
            (q_in, q),
        ),
        sems,
    )
    for copy in copies:
        copy.start()
    copies[0].wait()
    flat_head = whead[...].astype(F32).reshape(D, NVAR).astype(BF)
    go = nt(gf[...], flat_head).astype(BF)
    copies[1].wait()
    flat_out = wout[...].astype(F32).reshape(HD, D).astype(BF)
    gm = nt(go, flat_out).astype(BF)
    for copy in copies[2:]:
        copy.wait()
    for pair in range(HEADS // 2):
        at = pl.ds(pair * LANE, LANE)
        vat = pl.ds(HD + pair * LANE, LANE)
        q2, k2, v2 = q[:, at], kv[:, at], kv[:, vat]
        g2 = gm[:, pair * LANE : (pair + 1) * LANE]
        gqs, gks, gvs = [], [], []
        for side in range(2):
            chosen = jnp.where(halves((PTS, LANE), side), g2, jnp.zeros_like(g2))
            gp = nt(chosen, v2)
            held = probs[2 * pair + side]
            weight = held.astype(F32)
            centre = jnp.sum(weight * gp, axis=-1, keepdims=True)
            gs = (weight * (gp - centre) * (1.0 / math.sqrt(HDIM))).astype(BF)
            gqs.append(nn(gs, k2))
            gks.append(tn(gs, q2))
            gvs.append(tn(held, g2))
        gq[:, at] = jnp.where(halves((PTS, LANE), 0), gqs[0], gqs[1]).astype(BF)
        pick = halves((EXT, LANE), 0)
        for where_at, parts in ((at, gks), (vat, gvs)):
            total = jnp.where(pick, parts[0], parts[1])
            lower[:, where_at] = total[:HALO].astype(BF)
            mid[:, where_at] = total[HALO : HALO + PTS]
            upper[:, where_at] = total[HALO + PTS :].astype(BF)


def final_body(
    states, scale, gf, whead_in, wqkv_in, gq, mid, first, last, total, grad,
    whead, wqkv, sems,
):
    copies = fetched(((wqkv_in, wqkv), (whead_in, whead)), sems)
    for copy in copies:
        copy.start()
    centred, inverse = normalised(states[...])
    copies[1].wait()
    flat_head = whead[...].astype(F32).reshape(D, NVAR).astype(BF)
    total[...] = mid[...]
    total[:HALO, :] += first[...].astype(F32)
    total[PTS - HALO :, :] += last[...].astype(F32)
    kvs = total[...].astype(BF)
    copies[0].wait()
    weights = wqkv[...].reshape(D, 3 * HD)
    gn = nt(gq[...], weights[:, :HD]) + nt(kvs, weights[:, HD:])
    g = gn * scale[...]
    back = inverse * (
        g
        - jnp.mean(g, axis=-1, keepdims=True)
        - centred * jnp.mean(g * centred, axis=-1, keepdims=True)
    )
    grad[...] = (nt(gf[...], flat_head) + back).astype(BF)


def added(parts):
    total = parts[0].astype(F32)
    for i in range(1, parts.shape[0]):
        total = total + parts[i].astype(F32)
    return total


def sum_body(parts, total):
    total[...] = added(parts).astype(BF)


def spread_body(parts, spread):
    total = added(parts).astype(BF)
    for i in range(spread.shape[0]):
        spread[i] = total


def weights_body(scaling, parts, whead, mixing, head):
    flat_head = whead[...].astype(F32).reshape(D, NVAR).astype(BF)
    rb = head.shape[0]
    total = added(parts) * scaling
    head[...] = total[:rb]
    factor = total[rb:]
    high = factor.astype(BF)
    low = (factor - high.astype(F32)).astype(BF)
    mixing[...] = nt(high, flat_head) + nt(low, flat_head)


def shards(
    states, norm_scale, query, key, value, out_w, head_w, neighbours, observed
):
    members = lax.axis_size(MEMBER)
    devices = lax.axis_size(GRID)
    zh_n = lax.axis_size("zh")
    pn = lax.axis_size(PLANE)
    inputs = states[0]
    rs, ro = query.shape[0], out_w.shape[0]
    packed = 6 * rs + 4 * ro + rs // 2
    swap = [(0, 1), (1, 0)]
    up = [(i, i + 1) for i in range(devices - 1)]
    down = [(j, i) for i, j in up]

    column, _ = call(
        pack_body,
        [((zh_n, packed, LANE), BF), ((packed, LANE), BF)],
        (query, key, value, out_w, head_w),
        "AAAAA>HV",
        scratch=(pltpu.SemaphoreType.DMA((zh_n,)),),
        cost=(1e6, 1e6),
        limit=4,
    )
    column = lax.all_to_all(column, "zh", 0, 0, tiled=True)
    before = lax.ppermute(inputs[PTS - HALO :], GRID, up)
    after = lax.ppermute(inputs[:HALO], GRID, down)
    rel = neighbours - (lax.axis_index(GRID) * PTS - HALO)
    scale = norm_scale.reshape(1, D)
    normed, count = call(
        prepare_body,
        [((EXT, D), BF), ((PTS, EXT), F32)],
        (before, inputs, after, scale, rel),
        "VAVAA>AA",
        cost=(4e6, 1e6),
        limit=8,
    )
    spread = jnp.broadcast_to(column[None], (pn, *column.shape))
    own = lax.all_to_all(spread, PLANE, 0, 0, tiled=True)
    other = lax.ppermute(own, "core", swap)
    wqkv, wout, whead, q, kv, probs, mixed, out, fore, alone = call(
        functools.partial(forward_body, zh_n, rs, ro),
        [
            ((devices, rs, 3 * HD), BF),
            ((devices, ro, D), BF),
            ((devices, 2, rs // 2, NVAR), BF),
            ((PTS, HD), BF),
            ((EXT, D), BF),
            ((HEADS, PTS, EXT), BF),
            ((PTS, HD), BF),
            ((PTS, D), BF),
            ((members, PTS, NVAR), BF),
            ((PTS, NVAR), F32),
        ],
        (normed, inputs, count, own, other),
        "AAAVV>HHHHHHVVVV",
        scratch=(
            pltpu.VMEM((devices, rs, 3 * HD), BF),
            pltpu.VMEM((devices, ro, D), BF),
            pltpu.VMEM((devices, 2, rs // 2, NVAR), BF),
            pltpu.VMEM((PTS, HD), BF),
            pltpu.VMEM((EXT, D), BF),
            pltpu.VMEM((HEADS, PTS, EXT), BF),
            pltpu.SemaphoreType.DMA((2, zh_n, 6)),
            pltpu.SemaphoreType.DMA((2, zh_n, 4)),
            pltpu.SemaphoreType.DMA((2, zh_n)),
            pltpu.SemaphoreType.DMA((6,)),
        ),
        cost=(2e9, 1e7),
        limit=24,
    )
    every = lax.all_to_all(fore, MEMBER, 0, 0, tiled=True)
    gf, wg = call(
        functools.partial(score_body, members, zh_n),
        [
            ((PTS, NVAR), BF),
            ((pn, zh_n, (D + HD) // devices, NVAR), BF),
        ],
        (every, alone, observed, mixed, out),
        "VVVVV>AA",
        cost=(1e8, 2e6),
        limit=8,
    )
    plane = lax.all_to_all(wg, PLANE, 0, 0, tiled=True)
    gq, mid, lower, upper = call(
        backward_body,
        [((PTS, HD), BF), ((PTS, D), F32), ((HALO, D), BF), ((HALO, D), BF)],
        (gf, whead, wout, q, kv, probs),
        "AHHHHH>AAAA",
        scratch=(
            pltpu.VMEM(whead.shape, BF),
            pltpu.VMEM(wout.shape, BF),
            pltpu.VMEM(q.shape, BF),
            pltpu.VMEM(kv.shape, BF),
            pltpu.VMEM(probs.shape, BF),
            pltpu.SemaphoreType.DMA((5,)),
        ),
        cost=(1e9, 4e6),
        limit=16,
    )
    last = lax.ppermute(lower, GRID, down)
    first = lax.ppermute(upper, GRID, up)
    (partial,) = call(
        sum_body,
        [(wg.shape[1:], BF)],
        (plane,),
        "V>A",
        cost=(1e6, 1e6),
        limit=4,
    )
    column = lax.all_to_all(partial, "zh", 0, 0, tiled=True)
    (spread,) = call(
        spread_body,
        [((members, *wg.shape[2:]), BF)],
        (column,),
        "V>A",
        cost=(1e6, 1e6),
        limit=4,
    )
    parts = lax.all_to_all(spread, MEMBER, 0, 0, tiled=True)
    total, grad_input = call(
        final_body,
        [((PTS, D), F32), ((PTS, D), BF)],
        (inputs, scale, gf, whead, wqkv, gq, mid, first, last),
        "AAAHHAAVV>AA",
        scratch=(
            pltpu.VMEM(whead.shape, BF),
            pltpu.VMEM(wqkv.shape, BF),
            pltpu.SemaphoreType.DMA((2,)),
        ),
        cost=(1e9, 4e6),
        limit=16,
    )
    scaling = 1.0 / math.sqrt(members * devices * PTS)
    mixing, head = call(
        functools.partial(weights_body, scaling),
        [((HD // devices, D), F32), ((D // devices, NVAR), F32)],
        (parts, whead),
        "VA>AA",
        cost=(1e8, 1e6),
        limit=8,
    )
    return grad_input[None], mixing, head, total[None]


def refined(mesh):
    members, devices = mesh.shape["member"], mesh.shape["grid"]
    cut = {64: (4, 4, 4), 4: (1, 2, 2), 8: (2, 2, 2)}[devices]
    return Mesh(
        mesh.devices.reshape(members // 2, 2, *cut), ("zl", "core", "zh", "y", "x")
    )


def solution(mesh):
    rows = P(GRID, None)

    return jax.shard_map(
        shards,
        mesh=refined(mesh),
        in_specs=(
            P(MEMBER, GRID, None),
            P(),
            rows,
            rows,
            rows,
            rows,
            rows,
            rows,
            rows,
        ),
        out_specs=(P(MEMBER, GRID, None), rows, rows, P(MEMBER, GRID, None)),
        check_vma=False,
    )
```

```python
import functools
import math

import jax
import jax.numpy as jnp
from jax import lax
from jax.experimental import pallas as pl
from jax.experimental.pallas import tpu as pltpu
from jax.sharding import Mesh, PartitionSpec as P


HEADS = 8
HDIM = 64
KNB = 8
HALO = 32
PTS = 128
EXT = PTS + 2 * HALO
D = 1024
HD = 512
NVAR = 128
LANE = 128

epsilon = 1e-05
smooth = 0.1

MEMBER = ("zl", "core")
GRID = ("zh", "y", "x")
PLANE = ("y", "x")

BF = jnp.bfloat16
F32 = jnp.float32


def nn(a, b):
    return lax.dot_general(a, b, (((1,), (0,)), ((), ())), preferred_element_type=F32)


def nt(a, b):
    return lax.dot_general(a, b, (((1,), (1,)), ((), ())), preferred_element_type=F32)


def tn(a, b):
    return lax.dot_general(a, b, (((0,), (0,)), ((), ())), preferred_element_type=F32)


SPECS = {
    "V": pl.BlockSpec(memory_space=pltpu.VMEM),
    "A": pl.BlockSpec(),
    "H": pl.BlockSpec(memory_space=pltpu.HBM),
}


def call(body, outs, args, places, scratch=(), cost=(1e9, 4e6), limit=16):
    taken, given = places.split(">")
    shapes = [
        jax.ShapeDtypeStruct(s, d) if at == "V" else pltpu.HBM(s, d)
        for (s, d), at in zip(outs, given, strict=True)
    ]
    args = [
        x if at == "V" else pltpu.with_memory_space_constraint(x, pltpu.HBM)
        for x, at in zip(args, taken, strict=True)
    ]
    return pl.pallas_call(
        body,
        out_shape=tuple(shapes),
        in_specs=[SPECS[at] for at in taken],
        out_specs=tuple(SPECS[at] for at in given),
        scratch_shapes=list(scratch),
        compiler_params=pltpu.CompilerParams(vmem_limit_bytes=limit << 20),
        cost_estimate=pl.CostEstimate(
            flops=int(cost[0]), bytes_accessed=int(cost[1]), transcendentals=0
        ),
    )(*args)


def normalised(rows):
    values = rows.astype(F32)
    center = values - jnp.mean(values, axis=-1, keepdims=True)
    inverse = lax.rsqrt(jnp.mean(center * center, axis=-1, keepdims=True) + epsilon)
    return center * inverse, inverse


def taps_body(own, scale, rel, normed, count):
    centred, _ = normalised(own[...])
    normed[...] = (centred * scale[...]).astype(BF)
    place = lax.broadcasted_iota(jnp.int32, (PTS, EXT), 1)
    total = jnp.zeros((PTS, EXT), F32)
    for k in range(KNB):
        total = total + (place == rel[:, k : k + 1]).astype(F32)
    count[...] = total


def prepare_body(before, after, scale, first, last):
    for part, normed in ((before, first), (after, last)):
        centred, _ = normalised(part[...])
        normed[...] = (centred * scale[...]).astype(BF)


def halves(tile_shape, head):
    lane = lax.broadcasted_iota(jnp.int32, tile_shape, 1)
    return (lane < HDIM) if head == 0 else (lane >= HDIM)


def fetched(pairs, sems):
    return [pltpu.make_async_copy(s, d, sems.at[i]) for i, (s, d) in enumerate(pairs)]


def send_out(pairs, sems):
    copies = fetched(pairs, sems)
    for copy in copies:
        copy.start()
    for copy in copies:
        copy.wait()


def pack_body(query, key, value, out, head, column, mine, sems):
    rs, ro = query.shape[0], out.shape[0]

    def put(row, tile):
        size = tile.shape[0]
        mine[row : row + size, :] = tile

    for c in range(2):

        @pl.when(lax.axis_index("core") == c)
        def _():
            for t in range(6):
                weight = (query, key, value)[(6 * c + t) // 4]
                lane = (6 * c + t) % 4 * LANE
                put(t * rs, weight[:, lane : lane + LANE])
            for t in range(4):
                lane = (4 * c + t) * LANE
                put(6 * rs + t * ro, out[:, lane : lane + LANE])
            put(6 * rs + 4 * ro, head[c * rs // 2 : (c + 1) * rs // 2, :])

    send_out([(mine, column.at[i]) for i in range(column.shape[0])], sems)


def forward_body(
    zh_n, rs, ro, ahead, normed, behind, states, count, own, other,
    wqkv_out, wout_out, whead_out, q_out, kv_out, probs_out, mixed, out, fore, alone,
    qkv, probs, added_out, sq, so, sh, sems,
):
    core = lax.axis_index("core")
    pn = own.shape[0]
    qrows = 6 * rs
    orows = 4 * ro
    hr = rs // 2

    def pieces(buf, c):
        for zh in range(zh_n):
            at = pl.ds(zh * pn, pn)
            for t in range(6):
                yield (
                    buf.at[:, zh, pl.ds(t * rs, rs), :],
                    wqkv_out.at[at, :, pl.ds((6 * c + t) * LANE, LANE)],
                    sq.at[c, zh, t],
                )
            for t in range(4):
                yield (
                    buf.at[:, zh, pl.ds(qrows + t * ro, ro), :],
                    wout_out.at[at, :, pl.ds((4 * c + t) * LANE, LANE)],
                    so.at[c, zh, t],
                )
            yield (
                buf.at[:, zh, pl.ds(qrows + orows, hr), :],
                whead_out.at[at, c],
                sh.at[c, zh],
            )

    def begin(*halves_of):
        for c in range(2):
            for src, dst, sem in pieces(halves_of[c], c):
                pltpu.make_async_copy(src, dst, sem).start()

    @pl.when(core == 0)
    def _():
        begin(own, other)

    @pl.when(core != 0)
    def _():
        begin(other, own)

    rows = jnp.concatenate([ahead[...], normed[...], behind[...]], axis=0)
    width = 6 * LANE
    for buf, side in ((own, core), (other, 1 - core)):
        total = jnp.zeros((EXT, width), F32)
        for zh in range(zh_n):
            tiles = [
                buf[:, zh, t * rs : (t + 1) * rs, :].reshape(pn * rs, LANE)
                for t in range(6)
            ]
            depth = pn * rs
            total = total + nn(
                rows[:, zh * depth : (zh + 1) * depth], jnp.concatenate(tiles, axis=1)
            )
        qkv[:, pl.ds(pl.multiple_of(side * width, width), width)] = total.astype(BF)
    leaving = fetched(
        (
            (qkv.at[HALO : HALO + PTS, 0:HD], q_out),
            (qkv.at[:, HD : 3 * HD], kv_out),
            (probs, probs_out),
        ),
        sems,
    )
    leaving[0].start()
    leaving[1].start()
    times = count[...]
    here = times > 0
    for pair in range(HEADS // 2):
        at = pl.ds(pair * LANE, LANE)
        q2 = qkv[HALO : HALO + PTS, pair * LANE : (pair + 1) * LANE]
        k2 = qkv[:, HD + pair * LANE : HD + (pair + 1) * LANE]
        v2 = qkv[:, 2 * HD + pair * LANE : 2 * HD + (pair + 1) * LANE]
        got = []
        for side in range(2):
            chosen = jnp.where(halves((PTS, LANE), side), q2, jnp.zeros_like(q2))
            score = nt(chosen, k2) * (1.0 / math.sqrt(HDIM))
            score = jnp.where(here, score, -1e30)
            highest = jnp.max(score, axis=-1, keepdims=True)
            power = jnp.exp(score - highest)
            prob = power / jnp.sum(times * power, axis=-1, keepdims=True)
            weight = (times * prob.astype(BF).astype(F32)).astype(BF)
            probs[2 * pair + side] = weight
            got.append(nn(weight, v2))
        mixed[:, at] = jnp.where(halves((PTS, LANE), 0), got[0], got[1]).astype(BF)
    leaving[2].start()
    width = 4 * LANE
    attended = mixed[...]
    for buf, side in ((own, core), (other, 1 - core)):
        total = jnp.zeros((PTS, width), F32)
        depth = pn * ro
        for zh in range(zh_n):
            tiles = [
                buf[:, zh, qrows + t * ro : qrows + (t + 1) * ro, :]
                .astype(F32)
                .reshape(depth, LANE)
                .astype(BF)
                for t in range(4)
            ]
            total = total + nn(
                attended[:, zh * depth : (zh + 1) * depth],
                jnp.concatenate(tiles, axis=1),
            )
        added_out[:, pl.ds(pl.multiple_of(side * width, width), width)] = total
    layer = (states[...].astype(F32) + added_out[...]).astype(BF)
    out[...] = layer
    blocks = [
        [
            buf[:, zh, qrows + orows : qrows + orows + hr, :].astype(F32)
            for buf in (own, other)
        ]
        for zh in range(zh_n)
    ]
    mine_first = jnp.full((1, 1, 1), core, jnp.int32) == 0
    ordered = [
        jnp.stack([jnp.where(mine_first, a, b), jnp.where(mine_first, b, a)], axis=1)
        for a, b in blocks
    ]
    flat_head = jnp.concatenate(ordered, axis=0).reshape(D, NVAR).astype(BF)
    mine = nn(layer, flat_head)
    alone[...] = mine
    for i in range(fore.shape[0]):
        fore[i] = mine.astype(BF)
    for c in range(2):
        for src, dst, sem in pieces(own, c):
            pltpu.make_async_copy(src, dst, sem).wait()
    for copy in leaving:
        copy.wait()


def slope(z):
    return z * lax.rsqrt(z * z + smooth * smooth)


def score_body(members, zh_n, every, alone, observed, mixed, out, gf, held, wg):
    mine = alone[...]
    sent = mine.astype(BF).astype(F32)
    total = jnp.zeros_like(mine)
    for m in range(members):
        total = total + slope(sent - every[m].astype(F32))
    grad = (slope(mine - observed[...]) - total * (1.0 / (members - 1))).astype(BF)
    gf[...] = grad
    held[...] = grad
    pn = wg.shape[0]
    heads = tn(out[...], grad)
    factor = tn(mixed[...], grad)
    rb, ra = D // (zh_n * pn), HD // (zh_n * pn)
    for zh in range(zh_n):
        wg[:, zh, 0:rb, :] = (
            heads[zh * pn * rb : (zh + 1) * pn * rb].reshape(pn, rb, NVAR).astype(BF)
        )
        wg[:, zh, rb : rb + ra, :] = (
            factor[zh * pn * ra : (zh + 1) * pn * ra].reshape(pn, ra, NVAR).astype(BF)
        )


def backward_body(
    gf, whead_in, wout_in, q_in, kv_in, probs_in, gq, mid, lower, upper,
    whead, wout, q, kv, probs, sems,
):
    copies = fetched(
        (
            (whead_in, whead),
            (wout_in, wout),
            (kv_in, kv),
            (probs_in, probs),
            (q_in, q),
        ),
        sems,
    )
    for copy in copies:
        copy.start()
    copies[0].wait()
    flat_head = whead[...].astype(F32).reshape(D, NVAR).astype(BF)
    go = nt(gf[...], flat_head).astype(BF)
    copies[1].wait()
    flat_out = wout[...].astype(F32).reshape(HD, D).astype(BF)
    gm = nt(go, flat_out).astype(BF)
    for copy in copies[2:]:
        copy.wait()
    for pair in range(HEADS // 2):
        at = pl.ds(pair * LANE, LANE)
        vat = pl.ds(HD + pair * LANE, LANE)
        q2, k2, v2 = q[:, at], kv[:, at], kv[:, vat]
        g2 = gm[:, pair * LANE : (pair + 1) * LANE]
        gqs, gks, gvs = [], [], []
        for side in range(2):
            chosen = jnp.where(halves((PTS, LANE), side), g2, jnp.zeros_like(g2))
            gp = nt(chosen, v2)
            held = probs[2 * pair + side]
            weight = held.astype(F32)
            centre = jnp.sum(weight * gp, axis=-1, keepdims=True)
            gs = (weight * (gp - centre) * (1.0 / math.sqrt(HDIM))).astype(BF)
            gqs.append(nn(gs, k2))
            gks.append(tn(gs, q2))
            gvs.append(tn(held, g2))
        gq[:, at] = jnp.where(halves((PTS, LANE), 0), gqs[0], gqs[1]).astype(BF)
        pick = halves((EXT, LANE), 0)
        for where_at, parts in ((at, gks), (vat, gvs)):
            total = jnp.where(pick, parts[0], parts[1])
            lower[:, where_at] = total[:HALO].astype(BF)
            mid[:, where_at] = total[HALO : HALO + PTS]
            upper[:, where_at] = total[HALO + PTS :].astype(BF)


def final_body(states, scale, gf, whead, wqkv, gq, mid, first, last, total, grad):
    centred, inverse = normalised(states[...])
    flat_head = whead[...].astype(F32).reshape(D, NVAR).astype(BF)
    total[...] = mid[...]
    total[:HALO, :] += first[...].astype(F32)
    total[PTS - HALO :, :] += last[...].astype(F32)
    kvs = total[...].astype(BF)
    weights = wqkv[...].reshape(D, 3 * HD)
    gn = nt(gq[...], weights[:, :HD]) + nt(kvs, weights[:, HD:])
    g = gn * scale[...]
    back = inverse * (
        g
        - jnp.mean(g, axis=-1, keepdims=True)
        - centred * jnp.mean(g * centred, axis=-1, keepdims=True)
    )
    grad[...] = (nt(gf[...], flat_head) + back).astype(BF)


def added(parts):
    total = parts[0].astype(F32)
    for i in range(1, parts.shape[0]):
        total = total + parts[i].astype(F32)
    return total


def sum_body(parts, total):
    total[...] = added(parts).astype(BF)


def spread_body(parts, spread):
    total = added(parts).astype(BF)
    for i in range(spread.shape[0]):
        spread[i] = total


def weights_body(scaling, parts, whead, mixing, head):
    flat_head = whead[...].astype(F32).reshape(D, NVAR).astype(BF)
    rb = head.shape[0]
    total = added(parts) * scaling
    head[...] = total[:rb]
    factor = total[rb:]
    high = factor.astype(BF)
    low = (factor - high.astype(F32)).astype(BF)
    mixing[...] = nt(high, flat_head) + nt(low, flat_head)


def shards(
    states, norm_scale, query, key, value, out_w, head_w, neighbours, observed
):
    members = lax.axis_size(MEMBER)
    devices = lax.axis_size(GRID)
    zh_n = lax.axis_size("zh")
    pn = lax.axis_size(PLANE)
    inputs = states[0]
    rs, ro = query.shape[0], out_w.shape[0]
    packed = 6 * rs + 4 * ro + rs // 2
    swap = [(0, 1), (1, 0)]
    up = [(i, i + 1) for i in range(devices - 1)]
    down = [(j, i) for i, j in up]

    column, _ = call(
        pack_body,
        [((zh_n, packed, LANE), BF), ((packed, LANE), BF)],
        (query, key, value, out_w, head_w),
        "AAAAA>HV",
        scratch=(pltpu.SemaphoreType.DMA((zh_n,)),),
        cost=(1e6, 1e6),
        limit=4,
    )
    column = lax.all_to_all(column, "zh", 0, 0, tiled=True)
    before = lax.ppermute(inputs[PTS - HALO :], GRID, up)
    after = lax.ppermute(inputs[:HALO], GRID, down)
    rel = neighbours - (lax.axis_index(GRID) * PTS - HALO)
    scale = norm_scale.reshape(1, D)
    normed, count = call(
        taps_body,
        [((PTS, D), BF), ((PTS, EXT), F32)],
        (inputs, scale, rel),
        "AAA>AA",
        cost=(4e6, 1e6),
        limit=8,
    )
    ahead, behind = call(
        prepare_body,
        [((HALO, D), BF), ((HALO, D), BF)],
        (before, after, scale),
        "VVA>VV",
        cost=(4e6, 1e6),
        limit=8,
    )
    spread = jnp.broadcast_to(column[None], (pn, *column.shape))
    own = lax.all_to_all(spread, PLANE, 0, 0, tiled=True)
    other = lax.ppermute(own, "core", swap)
    wqkv, wout, whead, q, kv, probs, mixed, out, fore, alone = call(
        functools.partial(forward_body, zh_n, rs, ro),
        [
            ((devices, rs, 3 * HD), BF),
            ((devices, ro, D), BF),
            ((devices, 2, rs // 2, NVAR), BF),
            ((PTS, HD), BF),
            ((EXT, D), BF),
            ((HEADS, PTS, EXT), BF),
            ((PTS, HD), BF),
            ((PTS, D), BF),
            ((members, PTS, NVAR), BF),
            ((PTS, NVAR), F32),
        ],
        (ahead, normed, behind, inputs, count, own, other),
        "VAVAAVV>HHHHHHVVVV",
        scratch=(
            pltpu.VMEM((EXT, 3 * HD), BF),
            pltpu.VMEM((HEADS, PTS, EXT), BF),
            pltpu.VMEM((PTS, D), F32),
            pltpu.SemaphoreType.DMA((2, zh_n, 6)),
            pltpu.SemaphoreType.DMA((2, zh_n, 4)),
            pltpu.SemaphoreType.DMA((2, zh_n)),
            pltpu.SemaphoreType.DMA((3,)),
        ),
        cost=(2e9, 1e7),
        limit=24,
    )
    every = lax.all_to_all(fore, MEMBER, 0, 0, tiled=True)
    gf, held, wg = call(
        functools.partial(score_body, members, zh_n),
        [
            ((PTS, NVAR), BF),
            ((PTS, NVAR), BF),
            ((pn, zh_n, (D + HD) // devices, NVAR), BF),
        ],
        (every, alone, observed, mixed, out),
        "VVVVV>VAA",
        cost=(1e8, 2e6),
        limit=8,
    )
    plane = lax.all_to_all(wg, PLANE, 0, 0, tiled=True)
    gq, mid, lower, upper = call(
        backward_body,
        [((PTS, HD), BF), ((PTS, D), F32), ((HALO, D), BF), ((HALO, D), BF)],
        (gf, whead, wout, q, kv, probs),
        "VHHHHH>AAAA",
        scratch=(
            pltpu.VMEM(whead.shape, BF),
            pltpu.VMEM(wout.shape, BF),
            pltpu.VMEM(q.shape, BF),
            pltpu.VMEM(kv.shape, BF),
            pltpu.VMEM(probs.shape, BF),
            pltpu.SemaphoreType.DMA((5,)),
        ),
        cost=(1e9, 4e6),
        limit=16,
    )
    last = lax.ppermute(lower, GRID, down)
    first = lax.ppermute(upper, GRID, up)
    (partial,) = call(
        sum_body,
        [(wg.shape[1:], BF)],
        (plane,),
        "V>A",
        cost=(1e6, 1e6),
        limit=4,
    )
    column = lax.all_to_all(partial, "zh", 0, 0, tiled=True)
    (spread,) = call(
        spread_body,
        [((members, *wg.shape[2:]), BF)],
        (column,),
        "V>A",
        cost=(1e6, 1e6),
        limit=4,
    )
    parts = lax.all_to_all(spread, MEMBER, 0, 0, tiled=True)
    total, grad_input = call(
        final_body,
        [((PTS, D), F32), ((PTS, D), BF)],
        (inputs, scale, held, whead, wqkv, gq, mid, first, last),
        "AAAAVAAVV>AA",
        cost=(1e9, 4e6),
        limit=16,
    )
    scaling = 1.0 / math.sqrt(members * devices * PTS)
    mixing, head = call(
        functools.partial(weights_body, scaling),
        [((HD // devices, D), F32), ((D // devices, NVAR), F32)],
        (parts, whead),
        "VA>AA",
        cost=(1e8, 1e6),
        limit=8,
    )
    return grad_input[None], mixing, head, total[None]


def refined(mesh):
    members, devices = mesh.shape["member"], mesh.shape["grid"]
    cut = {64: (4, 4, 4), 4: (1, 2, 2), 8: (2, 2, 2)}[devices]
    return Mesh(
        mesh.devices.reshape(members // 2, 2, *cut), ("zl", "core", "zh", "y", "x")
    )


def solution(mesh):
    rows = P(GRID, None)

    return jax.shard_map(
        shards,
        mesh=refined(mesh),
        in_specs=(
            P(MEMBER, GRID, None),
            P(),
            rows,
            rows,
            rows,
            rows,
            rows,
            rows,
            rows,
        ),
        out_specs=(P(MEMBER, GRID, None), rows, rows, P(MEMBER, GRID, None)),
        check_vma=False,
    )
```

```python
import functools
import math

import jax
import jax.numpy as jnp
from jax import lax
from jax.experimental import pallas as pl
from jax.experimental.pallas import tpu as pltpu
from jax.sharding import Mesh, PartitionSpec as P


HEADS = 8
HDIM = 64
KNB = 8
HALO = 32
PTS = 128
EXT = PTS + 2 * HALO
D = 1024
HD = 512
NVAR = 128
LANE = 128

epsilon = 1e-05
smooth = 0.1

MEMBER = ("zl", "core")
GRID = ("zh", "y", "x")
PLANE = ("y", "x")

BF = jnp.bfloat16
F32 = jnp.float32


def nn(a, b):
    return lax.dot_general(a, b, (((1,), (0,)), ((), ())), preferred_element_type=F32)


def nt(a, b):
    return lax.dot_general(a, b, (((1,), (1,)), ((), ())), preferred_element_type=F32)


def tn(a, b):
    return lax.dot_general(a, b, (((0,), (0,)), ((), ())), preferred_element_type=F32)


SPECS = {
    "V": pl.BlockSpec(memory_space=pltpu.VMEM),
    "A": pl.BlockSpec(),
    "H": pl.BlockSpec(memory_space=pltpu.HBM),
}


def call(body, outs, args, places, scratch=(), cost=(1e9, 4e6), limit=16):
    taken, given = places.split(">")
    shapes = [
        jax.ShapeDtypeStruct(s, d) if at == "V" else pltpu.HBM(s, d)
        for (s, d), at in zip(outs, given, strict=True)
    ]
    args = [
        x if at == "V" else pltpu.with_memory_space_constraint(x, pltpu.HBM)
        for x, at in zip(args, taken, strict=True)
    ]
    return pl.pallas_call(
        body,
        out_shape=tuple(shapes),
        in_specs=[SPECS[at] for at in taken],
        out_specs=tuple(SPECS[at] for at in given),
        scratch_shapes=list(scratch),
        compiler_params=pltpu.CompilerParams(vmem_limit_bytes=limit << 20),
        cost_estimate=pl.CostEstimate(
            flops=int(cost[0]), bytes_accessed=int(cost[1]), transcendentals=0
        ),
    )(*args)


def normalised(rows):
    values = rows.astype(F32)
    center = values - jnp.mean(values, axis=-1, keepdims=True)
    inverse = lax.rsqrt(jnp.mean(center * center, axis=-1, keepdims=True) + epsilon)
    return center * inverse, inverse


def taps_body(own, scale, rel, normed, count):
    centred, _ = normalised(own[...])
    normed[...] = (centred * scale[...]).astype(BF)
    place = lax.broadcasted_iota(jnp.int32, (PTS, EXT), 1)
    total = jnp.zeros((PTS, EXT), F32)
    for k in range(KNB):
        total = total + (place == rel[:, k : k + 1]).astype(F32)
    count[...] = total


def prepare_body(before, after, scale, first, last):
    for part, normed in ((before, first), (after, last)):
        centred, _ = normalised(part[...])
        normed[...] = (centred * scale[...]).astype(BF)


def halves(tile_shape, head):
    lane = lax.broadcasted_iota(jnp.int32, tile_shape, 1)
    return (lane < HDIM) if head == 0 else (lane >= HDIM)


def fetched(pairs, sems):
    return [pltpu.make_async_copy(s, d, sems.at[i]) for i, (s, d) in enumerate(pairs)]


def send_out(pairs, sems):
    copies = fetched(pairs, sems)
    for copy in copies:
        copy.start()
    for copy in copies:
        copy.wait()


def pack_body(query, key, value, out, head, column, mine, sems):
    rs, ro = query.shape[0], out.shape[0]

    def put(row, tile):
        size = tile.shape[0]
        mine[row : row + size, :] = tile

    for c in range(2):

        @pl.when(lax.axis_index("core") == c)
        def _():
            for t in range(6):
                weight = (query, key, value)[(6 * c + t) // 4]
                lane = (6 * c + t) % 4 * LANE
                put(t * rs, weight[:, lane : lane + LANE])
            for t in range(4):
                lane = (4 * c + t) * LANE
                put(6 * rs + t * ro, out[:, lane : lane + LANE])
            put(6 * rs + 4 * ro, head[c * rs // 2 : (c + 1) * rs // 2, :])

    send_out([(mine, column.at[i]) for i in range(column.shape[0])], sems)


def places(side, ny, nx):
    return [
        jnp.where(side == 0, y * nx + x, x * ny + y)
        for y in range(ny)
        for x in range(nx)
    ]


def tile_at(buf, order, zh, start, size):
    return jnp.concatenate([buf[i, zh, start : start + size, :] for i in order], axis=0)


def narrow_tile(buf, order, zh, start, size):
    parts = [buf[i, zh, start : start + size, :].astype(F32) for i in order]
    return jnp.concatenate(parts, axis=0).astype(BF)


def lanes(side, width):
    return pl.ds(pl.multiple_of(side * width, width), width)


def forward_body(
    ny, nx, rs, ro, ahead, normed, behind, states, count, own, other,
    own_out, other_out, q_out, kv_out, probs_out, whead, mixed, out, fore, alone,
    qkv, probs, added_out, sems,
):
    core = lax.axis_index("core")
    pn, zh_n = own.shape[:2]
    qrows = 6 * rs
    orows = 4 * ro
    hr = rs // 2
    raw = [
        pltpu.make_async_copy(own, own_out, sems.at[3]),
        pltpu.make_async_copy(other, other_out, sems.at[4]),
    ]
    for copy in raw:
        copy.start()
    sides = [
        (own, core, places(core, ny, nx)),
        (other, 1 - core, places(1 - core, ny, nx)),
    ]

    rows = jnp.concatenate([ahead[...], normed[...], behind[...]], axis=0)
    width = 6 * LANE
    for buf, side, order in sides:
        total = jnp.zeros((EXT, width), F32)
        for zh in range(zh_n):
            tiles = [tile_at(buf, order, zh, t * rs, rs) for t in range(6)]
            depth = pn * rs
            total = total + nn(
                rows[:, zh * depth : (zh + 1) * depth], jnp.concatenate(tiles, axis=1)
            )
        qkv[:, lanes(side, width)] = total.astype(BF)
    leaving = fetched(
        (
            (qkv.at[HALO : HALO + PTS, 0:HD], q_out),
            (qkv.at[:, HD : 3 * HD], kv_out),
            (probs, probs_out),
        ),
        sems,
    )
    leaving[0].start()
    leaving[1].start()
    times = count[...]
    here = times > 0
    for pair in range(HEADS // 2):
        at = pl.ds(pair * LANE, LANE)
        q2 = qkv[HALO : HALO + PTS, pair * LANE : (pair + 1) * LANE]
        k2 = qkv[:, HD + pair * LANE : HD + (pair + 1) * LANE]
        v2 = qkv[:, 2 * HD + pair * LANE : 2 * HD + (pair + 1) * LANE]
        got = []
        for side in range(2):
            chosen = jnp.where(halves((PTS, LANE), side), q2, jnp.zeros_like(q2))
            score = nt(chosen, k2) * (1.0 / math.sqrt(HDIM))
            score = jnp.where(here, score, -1e30)
            highest = jnp.max(score, axis=-1, keepdims=True)
            power = jnp.exp(score - highest)
            prob = power / jnp.sum(times * power, axis=-1, keepdims=True)
            weight = (times * prob.astype(BF).astype(F32)).astype(BF)
            probs[2 * pair + side] = weight
            got.append(nn(weight, v2))
        mixed[:, at] = jnp.where(halves((PTS, LANE), 0), got[0], got[1]).astype(BF)
    leaving[2].start()
    width = 4 * LANE
    attended = mixed[...]
    for buf, side, order in sides:
        total = jnp.zeros((PTS, width), F32)
        depth = pn * ro
        for zh in range(zh_n):
            tiles = [narrow_tile(buf, order, zh, qrows + t * ro, ro) for t in range(4)]
            total = total + nn(
                attended[:, zh * depth : (zh + 1) * depth],
                jnp.concatenate(tiles, axis=1),
            )
        added_out[:, lanes(side, width)] = total
    layer = (states[...].astype(F32) + added_out[...]).astype(BF)
    out[...] = layer
    at_head = qrows + orows
    first_is_own = jnp.full((hr, NVAR), core, jnp.int32) == 0
    pieces = []
    for zh in range(zh_n):
        for i, j in zip(sides[0][2], sides[1][2]):
            a = own[i, zh, at_head : at_head + hr, :].astype(F32)
            b = other[j, zh, at_head : at_head + hr, :].astype(F32)
            pieces += [jnp.where(first_is_own, a, b), jnp.where(first_is_own, b, a)]
    flat_head = jnp.concatenate(pieces, axis=0).astype(BF)
    whead[...] = flat_head
    mine = nn(layer, flat_head)
    alone[...] = mine
    for i in range(fore.shape[0]):
        fore[i] = mine.astype(BF)
    for copy in raw + leaving:
        copy.wait()


def slope(z):
    return z * lax.rsqrt(z * z + smooth * smooth)


def score_body(members, zh_n, every, alone, observed, mixed, out, gf, wg):
    mine = alone[...]
    sent = mine.astype(BF).astype(F32)
    total = jnp.zeros_like(mine)
    for m in range(members):
        total = total + slope(sent - every[m].astype(F32))
    grad = (slope(mine - observed[...]) - total * (1.0 / (members - 1))).astype(BF)
    gf[...] = grad
    pn = wg.shape[0]
    heads = tn(out[...], grad)
    factor = tn(mixed[...], grad)
    rb, ra = D // (zh_n * pn), HD // (zh_n * pn)
    for zh in range(zh_n):
        wg[:, zh, 0:rb, :] = (
            heads[zh * pn * rb : (zh + 1) * pn * rb].reshape(pn, rb, NVAR).astype(BF)
        )
        wg[:, zh, rb : rb + ra, :] = (
            factor[zh * pn * ra : (zh + 1) * pn * ra].reshape(pn, ra, NVAR).astype(BF)
        )


def backward_body(
    ny, nx, at_out, ro, gf_in, whead_in, own_in, other_in, q_in, kv_in, probs_in,
    gq, mid, lower, upper,
    gf, whead, own, other, q, kv, probs, go, sems,
):
    zh_n = own.shape[1]
    core = lax.axis_index("core")
    size = own.shape[2]
    copies = fetched(
        (
            (gf_in, gf),
            (whead_in, whead),
            (own_in.at[:, :, pl.ds(at_out, size), :], own),
            (other_in.at[:, :, pl.ds(at_out, size), :], other),
            (kv_in, kv),
            (probs_in, probs),
            (q_in, q),
        ),
        sems,
    )
    for copy in copies:
        copy.start()
    copies[0].wait()
    copies[1].wait()
    go[...] = nt(gf[...], whead[...]).astype(BF)
    copies[2].wait()
    copies[3].wait()
    columns = [0.0] * zh_n
    for buf, side in ((own, core), (other, 1 - core)):
        order = places(side, ny, nx)
        given = go[:, lanes(side, 4 * LANE)]
        for zh in range(zh_n):
            tiles = [narrow_tile(buf, order, zh, t * ro, ro) for t in range(4)]
            columns[zh] = columns[zh] + nt(given, jnp.concatenate(tiles, axis=1))
    gm = jnp.concatenate(columns, axis=1).astype(BF)
    for copy in copies[4:]:
        copy.wait()
    for pair in range(HEADS // 2):
        at = pl.ds(pair * LANE, LANE)
        vat = pl.ds(HD + pair * LANE, LANE)
        q2, k2, v2 = q[:, at], kv[:, at], kv[:, vat]
        g2 = gm[:, pair * LANE : (pair + 1) * LANE]
        gqs, gks, gvs = [], [], []
        for side in range(2):
            chosen = jnp.where(halves((PTS, LANE), side), g2, jnp.zeros_like(g2))
            gp = nt(chosen, v2)
            held = probs[2 * pair + side]
            weight = held.astype(F32)
            centre = jnp.sum(weight * gp, axis=-1, keepdims=True)
            gs = (weight * (gp - centre) * (1.0 / math.sqrt(HDIM))).astype(BF)
            gqs.append(nn(gs, k2))
            gks.append(tn(gs, q2))
            gvs.append(tn(held, g2))
        gq[:, at] = jnp.where(halves((PTS, LANE), 0), gqs[0], gqs[1]).astype(BF)
        pick = halves((EXT, LANE), 0)
        for where_at, parts in ((at, gks), (vat, gvs)):
            total = jnp.where(pick, parts[0], parts[1])
            lower[:, where_at] = total[:HALO].astype(BF)
            mid[:, where_at] = total[HALO : HALO + PTS]
            upper[:, where_at] = total[HALO + PTS :].astype(BF)


def final_body(
    ny, nx, rs, states, scale, gf, whead, own, other_in, gq, mid, first, last,
    total, grad, given, other, sems,
):
    (arriving,) = fetched(
        ((other_in.at[:, :, pl.ds(0, other.shape[2]), :], other),), sems
    )
    arriving.start()
    zh_n = own.shape[1]
    core = lax.axis_index("core")
    centred, inverse = normalised(states[...])
    total[...] = mid[...]
    total[:HALO, :] += first[...].astype(F32)
    total[PTS - HALO :, :] += last[...].astype(F32)
    given[:, :HD] = gq[...]
    given[:, HD:] = total[...].astype(BF)
    columns = [0.0] * zh_n
    for buf, side in ((own, core), (other, 1 - core)):
        if buf is other:
            arriving.wait()
        order = places(side, ny, nx)
        part = given[:, lanes(side, 6 * LANE)]
        for zh in range(zh_n):
            tiles = [tile_at(buf, order, zh, t * rs, rs) for t in range(6)]
            columns[zh] = columns[zh] + nt(part, jnp.concatenate(tiles, axis=1))
    gn = jnp.concatenate(columns, axis=1)
    g = gn * scale[...]
    back = inverse * (
        g
        - jnp.mean(g, axis=-1, keepdims=True)
        - centred * jnp.mean(g * centred, axis=-1, keepdims=True)
    )
    grad[...] = (nt(gf[...], whead[...]) + back).astype(BF)


def added(parts):
    total = parts[0].astype(F32)
    for i in range(1, parts.shape[0]):
        total = total + parts[i].astype(F32)
    return total


def sum_body(parts, total):
    total[...] = added(parts).astype(BF)


def spread_body(parts, spread):
    total = added(parts).astype(BF)
    for i in range(spread.shape[0]):
        spread[i] = total


def weights_body(scaling, parts, whead, mixing, head):
    flat_head = whead[...]
    rb = head.shape[0]
    total = added(parts) * scaling
    head[...] = total[:rb]
    factor = total[rb:]
    high = factor.astype(BF)
    low = (factor - high.astype(F32)).astype(BF)
    mixing[...] = nt(high, flat_head) + nt(low, flat_head)


def shards(
    states, norm_scale, query, key, value, out_w, head_w, neighbours, observed
):
    members = lax.axis_size(MEMBER)
    devices = lax.axis_size(GRID)
    zh_n = lax.axis_size("zh")
    pn = lax.axis_size(PLANE)
    inputs = states[0]
    rs, ro = query.shape[0], out_w.shape[0]
    packed = 6 * rs + 4 * ro + rs // 2
    swap = [(0, 1), (1, 0)]
    up = [(i, i + 1) for i in range(devices - 1)]
    down = [(j, i) for i, j in up]

    column, _ = call(
        pack_body,
        [((zh_n, packed, LANE), BF), ((packed, LANE), BF)],
        (query, key, value, out_w, head_w),
        "AAAAA>HV",
        scratch=(pltpu.SemaphoreType.DMA((zh_n,)),),
        cost=(1e6, 1e6),
        limit=4,
    )
    column = lax.all_to_all(column, "zh", 0, 0, tiled=True)
    before = lax.ppermute(inputs[PTS - HALO :], GRID, up)
    after = lax.ppermute(inputs[:HALO], GRID, down)
    rel = neighbours - (lax.axis_index(GRID) * PTS - HALO)
    scale = norm_scale.reshape(1, D)
    normed, count = call(
        taps_body,
        [((PTS, D), BF), ((PTS, EXT), F32)],
        (inputs, scale, rel),
        "AAA>AA",
        cost=(4e6, 1e6),
        limit=8,
    )
    ahead, behind = call(
        prepare_body,
        [((HALO, D), BF), ((HALO, D), BF)],
        (before, after, scale),
        "VVA>VV",
        cost=(4e6, 1e6),
        limit=8,
    )
    ny, nx = lax.axis_size("y"), lax.axis_size("x")
    along_x = [[y * nx + x for x in range(nx)] for y in range(ny)]
    along_y = [[y * nx + x for y in range(ny)] for x in range(nx)]

    def widened(block, first, second):
        groups = first + [[pn + i for i in group] for group in second]
        n = len(first[0])
        return lax.all_to_all(
            jnp.broadcast_to(block[None], (n, *block.shape)),
            ("core", "y", "x"),
            0,
            0,
            axis_index_groups=groups,
            tiled=True,
        )

    line = widened(column, along_x, along_y)
    own = widened(line, along_y, along_x).reshape(pn, *column.shape)
    other = lax.ppermute(own, "core", swap)
    own_hbm, other_hbm, q, kv, probs, whead, mixed, out, fore, alone = call(
        functools.partial(forward_body, ny, nx, rs, ro),
        [
            (own.shape, BF),
            (own.shape, BF),
            ((PTS, HD), BF),
            ((EXT, D), BF),
            ((HEADS, PTS, EXT), BF),
            ((D, NVAR), BF),
            ((PTS, HD), BF),
            ((PTS, D), BF),
            ((members, PTS, NVAR), BF),
            ((PTS, NVAR), F32),
        ],
        (ahead, normed, behind, inputs, count, own, other),
        "VAVAAVV>HHHHHAVVVV",
        scratch=(
            pltpu.VMEM((EXT, 3 * HD), BF),
            pltpu.VMEM((HEADS, PTS, EXT), BF),
            pltpu.VMEM((PTS, D), F32),
            pltpu.SemaphoreType.DMA((5,)),
        ),
        cost=(2e9, 1e7),
        limit=24,
    )
    every = lax.all_to_all(fore, MEMBER, 0, 0, tiled=True)
    gf, wg = call(
        functools.partial(score_body, members, zh_n),
        [
            ((PTS, NVAR), BF),
            ((pn, zh_n, (D + HD) // devices, NVAR), BF),
        ],
        (every, alone, observed, mixed, out),
        "VVVVV>AA",
        cost=(1e8, 2e6),
        limit=8,
    )
    plane = lax.all_to_all(wg, PLANE, 0, 0, tiled=True)
    gq, mid, lower, upper = call(
        functools.partial(backward_body, ny, nx, 6 * rs, ro),
        [((PTS, HD), BF), ((PTS, D), F32), ((HALO, D), BF), ((HALO, D), BF)],
        (gf, whead, own_hbm, other_hbm, q, kv, probs),
        "HHHHHHH>AAAA",
        scratch=(
            pltpu.VMEM(gf.shape, BF),
            pltpu.VMEM(whead.shape, BF),
            pltpu.VMEM((pn, zh_n, 4 * ro, LANE), BF),
            pltpu.VMEM((pn, zh_n, 4 * ro, LANE), BF),
            pltpu.VMEM(q.shape, BF),
            pltpu.VMEM(kv.shape, BF),
            pltpu.VMEM(probs.shape, BF),
            pltpu.VMEM((PTS, D), BF),
            pltpu.SemaphoreType.DMA((7,)),
        ),
        cost=(1e9, 4e6),
        limit=16,
    )
    last = lax.ppermute(lower, GRID, down)
    first = lax.ppermute(upper, GRID, up)
    (partial,) = call(
        sum_body,
        [(wg.shape[1:], BF)],
        (plane,),
        "V>A",
        cost=(1e6, 1e6),
        limit=4,
    )
    column = lax.all_to_all(partial, "zh", 0, 0, tiled=True)
    (spread,) = call(
        spread_body,
        [((members, *wg.shape[2:]), BF)],
        (column,),
        "V>A",
        cost=(1e6, 1e6),
        limit=4,
    )
    parts = lax.all_to_all(spread, MEMBER, 0, 0, tiled=True)
    total, grad_input = call(
        functools.partial(final_body, ny, nx, rs),
        [((PTS, D), F32), ((PTS, D), BF)],
        (inputs, scale, gf, whead, own_hbm, other_hbm, gq, mid, first, last),
        "AAAAVHAAVV>AA",
        scratch=(
            pltpu.VMEM((PTS, 3 * HD), BF),
            pltpu.VMEM((pn, zh_n, 6 * rs, LANE), BF),
            pltpu.SemaphoreType.DMA((1,)),
        ),
        cost=(1e9, 4e6),
        limit=16,
    )
    scaling = 1.0 / math.sqrt(members * devices * PTS)
    mixing, head = call(
        functools.partial(weights_body, scaling),
        [((HD // devices, D), F32), ((D // devices, NVAR), F32)],
        (parts, whead),
        "VA>AA",
        cost=(1e8, 1e6),
        limit=8,
    )
    return grad_input[None], mixing, head, total[None]


def refined(mesh):
    members, devices = mesh.shape["member"], mesh.shape["grid"]
    cut = {64: (4, 4, 4), 4: (1, 2, 2), 8: (2, 2, 2)}[devices]
    return Mesh(
        mesh.devices.reshape(members // 2, 2, *cut), ("zl", "core", "zh", "y", "x")
    )


def solution(mesh):
    rows = P(GRID, None)

    return jax.shard_map(
        shards,
        mesh=refined(mesh),
        in_specs=(
            P(MEMBER, GRID, None),
            P(),
            rows,
            rows,
            rows,
            rows,
            rows,
            rows,
            rows,
        ),
        out_specs=(P(MEMBER, GRID, None), rows, rows, P(MEMBER, GRID, None)),
        check_vma=False,
    )
```

```python
import functools
import math

import jax
import jax.numpy as jnp
from jax import lax
from jax.experimental import pallas as pl
from jax.experimental.pallas import tpu as pltpu
from jax.sharding import Mesh, PartitionSpec as P


HEADS = 8
HDIM = 64
KNB = 8
HALO = 32
PTS = 128
EXT = PTS + 2 * HALO
D = 1024
HD = 512
NVAR = 128
LANE = 128

epsilon = 1e-05
smooth = 0.1

MEMBER = ("zl", "core")
GRID = ("zh", "y", "x")
PLANE = ("y", "x")

BF = jnp.bfloat16
F32 = jnp.float32


def nn(a, b):
    return lax.dot_general(a, b, (((1,), (0,)), ((), ())), preferred_element_type=F32)


def nt(a, b):
    return lax.dot_general(a, b, (((1,), (1,)), ((), ())), preferred_element_type=F32)


def tn(a, b):
    return lax.dot_general(a, b, (((0,), (0,)), ((), ())), preferred_element_type=F32)


SPECS = {
    "V": pl.BlockSpec(memory_space=pltpu.VMEM),
    "A": pl.BlockSpec(),
    "H": pl.BlockSpec(memory_space=pltpu.HBM),
}


def call(body, outs, args, places, scratch=(), cost=(1e9, 4e6), limit=16):
    taken, given = places.split(">")
    shapes = [
        jax.ShapeDtypeStruct(s, d) if at == "V" else pltpu.HBM(s, d)
        for (s, d), at in zip(outs, given, strict=True)
    ]
    args = [
        x if at == "V" else pltpu.with_memory_space_constraint(x, pltpu.HBM)
        for x, at in zip(args, taken, strict=True)
    ]
    return pl.pallas_call(
        body,
        out_shape=tuple(shapes),
        in_specs=[SPECS[at] for at in taken],
        out_specs=tuple(SPECS[at] for at in given),
        scratch_shapes=list(scratch),
        compiler_params=pltpu.CompilerParams(vmem_limit_bytes=limit << 20),
        cost_estimate=pl.CostEstimate(
            flops=int(cost[0]), bytes_accessed=int(cost[1]), transcendentals=0
        ),
    )(*args)


def normalised(rows):
    values = rows.astype(F32)
    center = values - jnp.mean(values, axis=-1, keepdims=True)
    inverse = lax.rsqrt(jnp.mean(center * center, axis=-1, keepdims=True) + epsilon)
    return center * inverse, inverse


def taps_body(own, scale, rel, normed, count):
    centred, _ = normalised(own[...])
    normed[...] = (centred * scale[...]).astype(BF)
    place = lax.broadcasted_iota(jnp.int32, (PTS, EXT), 1)
    total = jnp.zeros((PTS, EXT), F32)
    for k in range(KNB):
        total = total + (place == rel[:, k : k + 1]).astype(F32)
    count[...] = total


def halves(tile_shape, head):
    lane = lax.broadcasted_iota(jnp.int32, tile_shape, 1)
    return (lane < HDIM) if head == 0 else (lane >= HDIM)


def fetched(pairs, sems):
    return [pltpu.make_async_copy(s, d, sems.at[i]) for i, (s, d) in enumerate(pairs)]


def pack_body(query, key, value, out, head, column):
    rs, ro = query.shape[0], out.shape[0]

    def put(row, tile):
        size = tile.shape[0]
        for i in range(column.shape[0]):
            column[i, row : row + size, :] = tile

    for c in range(2):

        @pl.when(lax.axis_index("core") == c)
        def _():
            for t in range(6):
                weight = (query, key, value)[(6 * c + t) // 4]
                lane = (6 * c + t) % 4 * LANE
                put(t * rs, weight[:, lane : lane + LANE])
            for t in range(4):
                lane = (4 * c + t) * LANE
                put(6 * rs + t * ro, out[:, lane : lane + LANE])
            put(6 * rs + 4 * ro, head[c * rs // 2 : (c + 1) * rs // 2, :])


def places(side, ny, nx):
    return [
        y * nx + x if side == 0 else x * ny + y for y in range(ny) for x in range(nx)
    ]


def on_each_core(body):
    for c in range(2):
        pl.when(lax.axis_index("core") == c)(functools.partial(body, c))


def tile_at(buf, order, zh, start, size):
    return jnp.concatenate([buf[i, zh, start : start + size, :] for i in order], axis=0)


def narrow_tile(buf, order, zh, start, size):
    parts = [buf[i, zh, start : start + size, :].astype(F32) for i in order]
    return jnp.concatenate(parts, axis=0).astype(BF)


def projected(rows, buf, order, rs):
    total = 0.0
    depth = buf.shape[0] * rs
    for zh in range(buf.shape[1]):
        tiles = [tile_at(buf, order, zh, t * rs, rs) for t in range(6)]
        total = total + nn(
            rows[:, zh * depth : (zh + 1) * depth], jnp.concatenate(tiles, axis=1)
        )
    return total.astype(BF)


def early_body(
    ny, nx, rs, before, after, scale, normed, own, ahead, behind, part
):
    for block, to in ((before, ahead), (after, behind)):
        centred, _ = normalised(block[...])
        to[...] = (centred * scale[...]).astype(BF)
    rows = jnp.concatenate([ahead[...], normed[...], behind[...]], axis=0)

    def project(c):
        part[...] = projected(rows, own, places(c, ny, nx), rs)

    on_each_core(project)


def forward_body(
    ny, nx, rs, ro, ahead, normed, behind, part, states, count, own, other,
    raw, q_out, kv_out, probs_out, whead, mixed, out, fore, alone,
    qkv, probs, added_out, sems,
):
    pn, zh_n = own.shape[:2]
    qrows = 6 * rs
    orows = 4 * ro
    hr = rs // 2
    raws = fetched(((own, raw.at[0]), (other, raw.at[1])), sems.at[pl.ds(3, 2)])
    for copy in raws:
        copy.start()
    rows = jnp.concatenate([ahead[...], normed[...], behind[...]], axis=0)
    width = 6 * LANE

    def project(c):
        there = projected(rows, other, places(1 - c, ny, nx), rs)
        qkv[:, c * width : (c + 1) * width] = part[...]
        qkv[:, (1 - c) * width : (2 - c) * width] = there

    on_each_core(project)
    leaving = fetched(
        (
            (qkv.at[HALO : HALO + PTS, 0:HD], q_out),
            (qkv.at[:, HD : 3 * HD], kv_out),
            (probs, probs_out),
        ),
        sems,
    )
    leaving[0].start()
    leaving[1].start()
    times = count[...]
    here = times > 0
    for pair in range(HEADS // 2):
        at = pl.ds(pair * LANE, LANE)
        q2 = qkv[HALO : HALO + PTS, pair * LANE : (pair + 1) * LANE]
        k2 = qkv[:, HD + pair * LANE : HD + (pair + 1) * LANE]
        v2 = qkv[:, 2 * HD + pair * LANE : 2 * HD + (pair + 1) * LANE]
        got = []
        for side in range(2):
            chosen = jnp.where(halves((PTS, LANE), side), q2, jnp.zeros_like(q2))
            score = nt(chosen, k2) * (1.0 / math.sqrt(HDIM))
            score = jnp.where(here, score, -1e30)
            highest = jnp.max(score, axis=-1, keepdims=True)
            power = jnp.exp(score - highest)
            prob = power / jnp.sum(times * power, axis=-1, keepdims=True)
            weight = (times * prob.astype(BF).astype(F32)).astype(BF)
            probs[2 * pair + side] = weight
            got.append(nn(weight, v2))
        mixed[:, at] = jnp.where(halves((PTS, LANE), 0), got[0], got[1]).astype(BF)
    leaving[2].start()
    attended = mixed[...]
    at_head = qrows + orows

    def finish(c):
        wide = 4 * LANE
        depth = pn * ro
        orders = [places(0, ny, nx), places(1, ny, nx)]
        bufs = (own, other) if c == 0 else (other, own)
        for side in range(2):
            total = 0.0
            for zh in range(zh_n):
                tiles = [
                    narrow_tile(bufs[side], orders[side], zh, qrows + t * ro, ro)
                    for t in range(4)
                ]
                total = total + nn(
                    attended[:, zh * depth : (zh + 1) * depth],
                    jnp.concatenate(tiles, axis=1),
                )
            added_out[:, side * wide : (side + 1) * wide] = total
        pieces = []
        for zh in range(zh_n):
            for ij in zip(*orders):
                for side in range(2):
                    block = bufs[side][ij[side], zh, at_head : at_head + hr, :]
                    pieces.append(block.astype(F32))
        whead[...] = jnp.concatenate(pieces, axis=0).astype(BF)

    on_each_core(finish)
    layer = (states[...].astype(F32) + added_out[...]).astype(BF)
    out[...] = layer
    mine = nn(layer, whead[...])
    alone[...] = mine
    for i in range(fore.shape[0]):
        fore[i] = mine.astype(BF)
    for copy in raws + leaving:
        copy.wait()


def slope(z):
    return z * lax.rsqrt(z * z + smooth * smooth)


def score_body(members, zh_n, every, alone, observed, mixed, out, gf, wg):
    mine = alone[...]
    sent = mine.astype(BF).astype(F32)
    total = jnp.zeros_like(mine)
    for m in range(members):
        total = total + slope(sent - every[m].astype(F32))
    grad = (slope(mine - observed[...]) - total * (1.0 / (members - 1))).astype(BF)
    gf[...] = grad
    pn = wg.shape[0]
    heads = tn(out[...], grad)
    factor = tn(mixed[...], grad)
    rb, ra = D // (zh_n * pn), HD // (zh_n * pn)
    for zh in range(zh_n):
        wg[:, zh, 0:rb, :] = (
            heads[zh * pn * rb : (zh + 1) * pn * rb].reshape(pn, rb, NVAR).astype(BF)
        )
        wg[:, zh, rb : rb + ra, :] = (
            factor[zh * pn * ra : (zh + 1) * pn * ra].reshape(pn, ra, NVAR).astype(BF)
        )


def backward_body(
    ny, nx, at_out, ro, gf_in, whead_in, raw_in, q_in, kv_in, probs_in,
    gq, mid, lower, upper,
    gf, whead, raw, q, kv, probs, gm_held, sems,
):
    zh_n = raw.shape[2]
    size = raw.shape[3]
    copies = fetched(
        (
            (gf_in, gf),
            (whead_in, whead),
            (raw_in.at[:, :, :, pl.ds(at_out, size), :], raw),
            (kv_in, kv),
            (probs_in, probs),
            (q_in, q),
        ),
        sems,
    )
    for copy in copies:
        copy.start()
    copies[0].wait()
    copies[1].wait()
    go = nt(gf[...], whead[...]).astype(BF)
    copies[2].wait()

    def widen(c):
        columns = [0.0] * zh_n
        for side in range(2):
            order = places(side, ny, nx)
            given = go[:, side * 4 * LANE : (side + 1) * 4 * LANE]
            for zh in range(zh_n):
                tiles = [
                    narrow_tile(raw.at[side ^ c], order, zh, t * ro, ro)
                    for t in range(4)
                ]
                columns[zh] = columns[zh] + nt(given, jnp.concatenate(tiles, axis=1))
        gm_held[...] = jnp.concatenate(columns, axis=1).astype(BF)

    on_each_core(widen)
    gm = gm_held[...]
    for copy in copies[3:]:
        copy.wait()
    for pair in range(HEADS // 2):
        at = pl.ds(pair * LANE, LANE)
        vat = pl.ds(HD + pair * LANE, LANE)
        q2, k2, v2 = q[:, at], kv[:, at], kv[:, vat]
        g2 = gm[:, pair * LANE : (pair + 1) * LANE]
        gqs, gks, gvs = [], [], []
        for side in range(2):
            chosen = jnp.where(halves((PTS, LANE), side), g2, jnp.zeros_like(g2))
            gp = nt(chosen, v2)
            held = probs[2 * pair + side]
            weight = held.astype(F32)
            centre = jnp.sum(weight * gp, axis=-1, keepdims=True)
            gs = (weight * (gp - centre) * (1.0 / math.sqrt(HDIM))).astype(BF)
            gqs.append(nn(gs, k2))
            gks.append(tn(gs, q2))
            gvs.append(tn(held, g2))
        gq[:, at] = jnp.where(halves((PTS, LANE), 0), gqs[0], gqs[1]).astype(BF)
        pick = halves((EXT, LANE), 0)
        for where_at, parts in ((at, gks), (vat, gvs)):
            total = jnp.where(pick, parts[0], parts[1])
            lower[:, where_at] = total[:HALO].astype(BF)
            mid[:, where_at] = total[HALO : HALO + PTS]
            upper[:, where_at] = total[HALO + PTS :].astype(BF)


def final_body(
    ny, nx, rs, states, scale, gf, whead, raw_in, gq, mid, first, last,
    total, grad, given, held, raw, sems,
):
    zh_n = raw.shape[2]
    copies = fetched(
        [
            (raw_in.at[:, :, zh, pl.ds(0, raw.shape[3]), :], raw.at[:, :, zh])
            for zh in range(zh_n)
        ],
        sems,
    )
    for copy in copies:
        copy.start()
    centred, inverse = normalised(states[...])
    total[...] = mid[...]
    total[:HALO, :] += first[...].astype(F32)
    total[PTS - HALO :, :] += last[...].astype(F32)
    given[:, :HD] = gq[...]
    given[:, HD:] = total[...].astype(BF)

    def widen(c):
        depth = raw.shape[1] * rs
        for zh in range(zh_n):
            copies[zh].wait()
            column = 0.0
            for side in range(2):
                order = places(side, ny, nx)
                part = given[:, side * 6 * LANE : (side + 1) * 6 * LANE]
                tiles = [
                    tile_at(raw.at[side ^ c], order, zh, t * rs, rs) for t in range(6)
                ]
                column = column + nt(part, jnp.concatenate(tiles, axis=1))
            held[:, zh * depth : (zh + 1) * depth] = column

    on_each_core(widen)
    gn = held[...]
    g = gn * scale[...]
    back = inverse * (
        g
        - jnp.mean(g, axis=-1, keepdims=True)
        - centred * jnp.mean(g * centred, axis=-1, keepdims=True)
    )
    grad[...] = (nt(gf[...], whead[...]) + back).astype(BF)


def added(parts):
    total = parts[0].astype(F32)
    for i in range(1, parts.shape[0]):
        total = total + parts[i].astype(F32)
    return total


def sum_body(parts, total):
    total[...] = added(parts).astype(BF)


def spread_body(parts, spread):
    total = added(parts).astype(BF)
    for i in range(spread.shape[0]):
        spread[i] = total


def weights_body(scaling, parts, whead, mixing, head):
    flat_head = whead[...]
    rb = head.shape[0]
    total = added(parts) * scaling
    head[...] = total[:rb]
    factor = total[rb:]
    high = factor.astype(BF)
    low = (factor - high.astype(F32)).astype(BF)
    mixing[...] = nt(high, flat_head) + nt(low, flat_head)


def shards(
    states, norm_scale, query, key, value, out_w, head_w, neighbours, observed
):
    members = lax.axis_size(MEMBER)
    devices = lax.axis_size(GRID)
    zh_n = lax.axis_size("zh")
    pn = lax.axis_size(PLANE)
    inputs = states[0]
    rs, ro = query.shape[0], out_w.shape[0]
    packed = 6 * rs + 4 * ro + rs // 2
    swap = [(0, 1), (1, 0)]
    up = [(i, i + 1) for i in range(devices - 1)]
    down = [(j, i) for i, j in up]

    (column,) = call(
        pack_body,
        [((zh_n, packed, LANE), BF)],
        (query, key, value, out_w, head_w),
        "AAAAA>V",
        cost=(1e6, 1e6),
        limit=4,
    )
    column = lax.all_to_all(column, "zh", 0, 0, tiled=True)
    before = lax.ppermute(inputs[PTS - HALO :], GRID, up)
    after = lax.ppermute(inputs[:HALO], GRID, down)
    rel = neighbours - (lax.axis_index(GRID) * PTS - HALO)
    scale = norm_scale.reshape(1, D)
    normed, count = call(
        taps_body,
        [((PTS, D), BF), ((PTS, EXT), F32)],
        (inputs, scale, rel),
        "AAA>AA",
        cost=(4e6, 1e6),
        limit=8,
    )
    ny, nx = lax.axis_size("y"), lax.axis_size("x")
    along_x = [[y * nx + x for x in range(nx)] for y in range(ny)]
    along_y = [[y * nx + x for y in range(ny)] for x in range(nx)]

    def widened(block, first, second):
        groups = first + [[pn + i for i in group] for group in second]
        n = len(first[0])
        return lax.all_to_all(
            jnp.broadcast_to(block[None], (n, *block.shape)),
            ("core", "y", "x"),
            0,
            0,
            axis_index_groups=groups,
            tiled=True,
        )

    line = widened(column, along_x, along_y)
    own = widened(line, along_y, along_x).reshape(pn, *column.shape)
    other = lax.ppermute(own, "core", swap)
    ahead, behind, part = call(
        functools.partial(early_body, ny, nx, rs),
        [((HALO, D), BF), ((HALO, D), BF), ((EXT, 6 * LANE), BF)],
        (before, after, scale, normed, own),
        "VVAAV>VVV",
        cost=(3e8, 4e6),
        limit=8,
    )
    raw, q, kv, probs, whead, mixed, out, fore, alone = call(
        functools.partial(forward_body, ny, nx, rs, ro),
        [
            ((2, *own.shape), BF),
            ((PTS, HD), BF),
            ((EXT, D), BF),
            ((HEADS, PTS, EXT), BF),
            ((D, NVAR), BF),
            ((PTS, HD), BF),
            ((PTS, D), BF),
            ((members, PTS, NVAR), BF),
            ((PTS, NVAR), F32),
        ],
        (ahead, normed, behind, part, inputs, count, own, other),
        "VAVVAAVV>HHHHAVVVV",
        scratch=(
            pltpu.VMEM((EXT, 3 * HD), BF),
            pltpu.VMEM((HEADS, PTS, EXT), BF),
            pltpu.VMEM((PTS, D), F32),
            pltpu.SemaphoreType.DMA((5,)),
        ),
        cost=(2e9, 1e7),
        limit=24,
    )
    every = lax.all_to_all(fore, MEMBER, 0, 0, tiled=True)
    gf, wg = call(
        functools.partial(score_body, members, zh_n),
        [
            ((PTS, NVAR), BF),
            ((pn, zh_n, (D + HD) // devices, NVAR), BF),
        ],
        (every, alone, observed, mixed, out),
        "VVVVV>AA",
        cost=(1e8, 2e6),
        limit=8,
    )
    plane = lax.all_to_all(wg, PLANE, 0, 0, tiled=True)
    gq, mid, lower, upper = call(
        functools.partial(backward_body, ny, nx, 6 * rs, ro),
        [((PTS, HD), BF), ((PTS, D), F32), ((HALO, D), BF), ((HALO, D), BF)],
        (gf, whead, raw, q, kv, probs),
        "HHHHHH>AAAA",
        scratch=(
            pltpu.VMEM(gf.shape, BF),
            pltpu.VMEM(whead.shape, BF),
            pltpu.VMEM((2, pn, zh_n, 4 * ro, LANE), BF),
            pltpu.VMEM(q.shape, BF),
            pltpu.VMEM(kv.shape, BF),
            pltpu.VMEM(probs.shape, BF),
            pltpu.VMEM((PTS, HD), BF),
            pltpu.SemaphoreType.DMA((6,)),
        ),
        cost=(1e9, 4e6),
        limit=16,
    )
    last = lax.ppermute(lower, GRID, down)
    first = lax.ppermute(upper, GRID, up)
    (partial,) = call(
        sum_body,
        [(wg.shape[1:], BF)],
        (plane,),
        "V>A",
        cost=(1e6, 1e6),
        limit=4,
    )
    column = lax.all_to_all(partial, "zh", 0, 0, tiled=True)
    (spread,) = call(
        spread_body,
        [((members, *wg.shape[2:]), BF)],
        (column,),
        "V>A",
        cost=(1e6, 1e6),
        limit=4,
    )
    parts = lax.all_to_all(spread, MEMBER, 0, 0, tiled=True)
    total, grad_input = call(
        functools.partial(final_body, ny, nx, rs),
        [((PTS, D), F32), ((PTS, D), BF)],
        (inputs, scale, gf, whead, raw, gq, mid, first, last),
        "AAAAHAAVV>AA",
        scratch=(
            pltpu.VMEM((PTS, 3 * HD), BF),
            pltpu.VMEM((PTS, D), F32),
            pltpu.VMEM((2, pn, zh_n, 6 * rs, LANE), BF),
            pltpu.SemaphoreType.DMA((zh_n,)),
        ),
        cost=(1e9, 4e6),
        limit=16,
    )
    scaling = 1.0 / math.sqrt(members * devices * PTS)
    mixing, head = call(
        functools.partial(weights_body, scaling),
        [((HD // devices, D), F32), ((D // devices, NVAR), F32)],
        (parts, whead),
        "VA>AA",
        cost=(1e8, 1e6),
        limit=8,
    )
    return grad_input[None], mixing, head, total[None]


def refined(mesh):
    members, devices = mesh.shape["member"], mesh.shape["grid"]
    cut = {64: (4, 4, 4), 4: (1, 2, 2), 8: (2, 2, 2)}[devices]
    return Mesh(
        mesh.devices.reshape(members // 2, 2, *cut), ("zl", "core", "zh", "y", "x")
    )


def solution(mesh):
    rows = P(GRID, None)

    return jax.shard_map(
        shards,
        mesh=refined(mesh),
        in_specs=(
            P(MEMBER, GRID, None),
            P(),
            rows,
            rows,
            rows,
            rows,
            rows,
            rows,
            rows,
        ),
        out_specs=(P(MEMBER, GRID, None), rows, rows, P(MEMBER, GRID, None)),
        check_vma=False,
    )
```

```python
import functools
import math

import jax
import jax.numpy as jnp
from jax import lax
from jax.experimental import pallas as pl
from jax.experimental.pallas import tpu as pltpu
from jax.sharding import Mesh, PartitionSpec as P


HEADS = 8
HDIM = 64
KNB = 8
HALO = 32
PTS = 128
EXT = PTS + 2 * HALO
D = 1024
HD = 512
NVAR = 128
LANE = 128

epsilon = 1e-05
smooth = 0.1

MEMBER = ("zl", "core")
GRID = ("zh", "y", "x")
PLANE = ("y", "x")

BF = jnp.bfloat16
F32 = jnp.float32


def nn(a, b):
    return lax.dot_general(a, b, (((1,), (0,)), ((), ())), preferred_element_type=F32)


def nt(a, b):
    return lax.dot_general(a, b, (((1,), (1,)), ((), ())), preferred_element_type=F32)


def tn(a, b):
    return lax.dot_general(a, b, (((0,), (0,)), ((), ())), preferred_element_type=F32)


SPECS = {
    "V": pl.BlockSpec(memory_space=pltpu.VMEM),
    "A": pl.BlockSpec(),
    "H": pl.BlockSpec(memory_space=pltpu.HBM),
}


def call(body, outs, args, places, scratch=(), cost=(1e9, 4e6), limit=16):
    taken, given = places.split(">")
    shapes = [
        jax.ShapeDtypeStruct(s, d) if at == "V" else pltpu.HBM(s, d)
        for (s, d), at in zip(outs, given, strict=True)
    ]
    args = [
        x if at == "V" else pltpu.with_memory_space_constraint(x, pltpu.HBM)
        for x, at in zip(args, taken, strict=True)
    ]
    return pl.pallas_call(
        body,
        out_shape=tuple(shapes),
        in_specs=[SPECS[at] for at in taken],
        out_specs=tuple(SPECS[at] for at in given),
        scratch_shapes=list(scratch),
        compiler_params=pltpu.CompilerParams(vmem_limit_bytes=limit << 20),
        cost_estimate=pl.CostEstimate(
            flops=int(cost[0]), bytes_accessed=int(cost[1]), transcendentals=0
        ),
    )(*args)


def normalised(rows):
    values = rows.astype(F32)
    center = values - jnp.mean(values, axis=-1, keepdims=True)
    inverse = lax.rsqrt(jnp.mean(center * center, axis=-1, keepdims=True) + epsilon)
    return center * inverse, inverse


def taps_body(own, scale, rel, normed, count):
    centred, _ = normalised(own[...])
    normed[...] = (centred * scale[...]).astype(BF)
    place = lax.broadcasted_iota(jnp.int32, (PTS, EXT), 1)
    total = jnp.zeros((PTS, EXT), F32)
    for k in range(KNB):
        total = total + (place == rel[:, k : k + 1]).astype(F32)
    count[...] = total


def halves(tile_shape, head):
    lane = lax.broadcasted_iota(jnp.int32, tile_shape, 1)
    return (lane < HDIM) if head == 0 else (lane >= HDIM)


def fetched(pairs, sems):
    return [pltpu.make_async_copy(s, d, sems.at[i]) for i, (s, d) in enumerate(pairs)]


def pack_body(query, key, value, out, head, column):
    rs, ro = query.shape[0], out.shape[0]

    def put(row, tile):
        size = tile.shape[0]
        for i in range(column.shape[0]):
            column[i, row : row + size, :] = tile

    for c in range(2):

        @pl.when(lax.axis_index("core") == c)
        def _():
            for t in range(6):
                weight = (query, key, value)[(6 * c + t) // 4]
                lane = (6 * c + t) % 4 * LANE
                put(t * rs, weight[:, lane : lane + LANE])
            for t in range(4):
                lane = (4 * c + t) * LANE
                put(6 * rs + t * ro, out[:, lane : lane + LANE])
            put(6 * rs + 4 * ro, head[c * rs // 2 : (c + 1) * rs // 2, :])


def places(side, ny, nx):
    return [
        y * nx + x if side == 0 else x * ny + y for y in range(ny) for x in range(nx)
    ]


def on_each_core(body):
    for c in range(2):
        pl.when(lax.axis_index("core") == c)(functools.partial(body, c))


def tile_at(buf, order, zh, start, size):
    return jnp.concatenate([buf[i, zh, start : start + size, :] for i in order], axis=0)


def narrow_tile(buf, order, zh, start, size):
    parts = [buf[i, zh, start : start + size, :].astype(F32) for i in order]
    return jnp.concatenate(parts, axis=0).astype(BF)


def projected(rows, buf, order, rs):
    total = 0.0
    depth = buf.shape[0] * rs
    for zh in range(buf.shape[1]):
        tiles = [tile_at(buf, order, zh, t * rs, rs) for t in range(6)]
        total = total + nn(
            rows[:, zh * depth : (zh + 1) * depth], jnp.concatenate(tiles, axis=1)
        )
    return total.astype(BF)


def is_even(shape):
    return jnp.full(shape, lax.rem(lax.axis_index("x"), 2), jnp.int32) == 0


def early_body(
    ny, nx, rs, inside, across, scale, normed, own, ahead, behind, part
):
    even = is_even((HALO, D))
    a, b = inside[...].astype(F32), across[...].astype(F32)
    for block, to in ((jnp.where(even, b, a), ahead), (jnp.where(even, a, b), behind)):
        centred, _ = normalised(block)
        to[...] = (centred * scale[...]).astype(BF)
    rows = jnp.concatenate([ahead[...], normed[...], behind[...]], axis=0)

    def project(c):
        part[...] = projected(rows, own, places(c, ny, nx), rs)

    on_each_core(project)


def forward_body(
    ny, nx, rs, ro, ahead, normed, behind, part, states, count, own, other,
    raw_in, raw_out, q_out, kv_out, probs_out, whead, mixed, out, fore, alone,
    qkv, probs, added_out, sems,
):
    pn, zh_n = own.shape[:2]
    qrows = 6 * rs
    orows = 4 * ro
    hr = rs // 2
    raws = fetched(
        [
            (buf.at[:, :, pl.ds(start, to.shape[3]), :], to.at[i])
            for i, buf in enumerate((own, other))
            for start, to in ((qrows, raw_out), (0, raw_in))
        ],
        sems.at[pl.ds(3, 4)],
    )
    for copy in raws:
        copy.start()
    rows = jnp.concatenate([ahead[...], normed[...], behind[...]], axis=0)
    width = 6 * LANE

    def project(c):
        there = projected(rows, other, places(1 - c, ny, nx), rs)
        qkv[:, c * width : (c + 1) * width] = part[...]
        qkv[:, (1 - c) * width : (2 - c) * width] = there

    on_each_core(project)
    leaving = fetched(
        (
            (qkv.at[HALO : HALO + PTS, 0:HD], q_out),
            (qkv.at[:, HD : 3 * HD], kv_out),
            (probs, probs_out),
        ),
        sems,
    )
    leaving[0].start()
    leaving[1].start()
    times = count[...]
    here = times > 0
    for pair in range(HEADS // 2):
        at = pl.ds(pair * LANE, LANE)
        q2 = qkv[HALO : HALO + PTS, pair * LANE : (pair + 1) * LANE]
        k2 = qkv[:, HD + pair * LANE : HD + (pair + 1) * LANE]
        v2 = qkv[:, 2 * HD + pair * LANE : 2 * HD + (pair + 1) * LANE]
        got = []
        for side in range(2):
            chosen = jnp.where(halves((PTS, LANE), side), q2, jnp.zeros_like(q2))
            score = nt(chosen, k2) * (1.0 / math.sqrt(HDIM))
            score = jnp.where(here, score, -1e30)
            highest = jnp.max(score, axis=-1, keepdims=True)
            power = jnp.exp(score - highest)
            prob = power / jnp.sum(times * power, axis=-1, keepdims=True)
            weight = (times * prob.astype(BF).astype(F32)).astype(BF)
            probs[2 * pair + side] = weight
            got.append(nn(weight, v2))
        mixed[:, at] = jnp.where(halves((PTS, LANE), 0), got[0], got[1]).astype(BF)
    leaving[2].start()
    attended = mixed[...]
    at_head = qrows + orows

    def finish(c):
        wide = 4 * LANE
        depth = pn * ro
        orders = [places(0, ny, nx), places(1, ny, nx)]
        bufs = (own, other) if c == 0 else (other, own)
        for side in range(2):
            total = 0.0
            for zh in range(zh_n):
                tiles = [
                    narrow_tile(bufs[side], orders[side], zh, qrows + t * ro, ro)
                    for t in range(4)
                ]
                total = total + nn(
                    attended[:, zh * depth : (zh + 1) * depth],
                    jnp.concatenate(tiles, axis=1),
                )
            added_out[:, side * wide : (side + 1) * wide] = total
        pieces = []
        for zh in range(zh_n):
            for ij in zip(*orders):
                for side in range(2):
                    block = bufs[side][ij[side], zh, at_head : at_head + hr, :]
                    pieces.append(block.astype(F32))
        whead[...] = jnp.concatenate(pieces, axis=0).astype(BF)

    on_each_core(finish)
    layer = (states[...].astype(F32) + added_out[...]).astype(BF)
    out[...] = layer
    mine = nn(layer, whead[...])
    alone[...] = mine
    for i in range(fore.shape[0]):
        fore[i] = mine.astype(BF)
    for copy in raws + leaving:
        copy.wait()


def slope(z):
    return z * lax.rsqrt(z * z + smooth * smooth)


def score_body(members, zh_n, every, alone, observed, mixed, out, gf, wg):
    mine = alone[...]
    sent = mine.astype(BF).astype(F32)
    total = jnp.zeros_like(mine)
    for m in range(members):
        total = total + slope(sent - every[m].astype(F32))
    grad = (slope(mine - observed[...]) - total * (1.0 / (members - 1))).astype(BF)
    gf[...] = grad
    pn = wg.shape[0]
    heads = tn(out[...], grad)
    factor = tn(mixed[...], grad)
    rb, ra = D // (zh_n * pn), HD // (zh_n * pn)
    for zh in range(zh_n):
        wg[:, zh, 0:rb, :] = (
            heads[zh * pn * rb : (zh + 1) * pn * rb].reshape(pn, rb, NVAR).astype(BF)
        )
        wg[:, zh, rb : rb + ra, :] = (
            factor[zh * pn * ra : (zh + 1) * pn * ra].reshape(pn, ra, NVAR).astype(BF)
        )


def backward_body(
    ny, nx, ro, gf_in, whead_in, raw_in, q_in, kv_in, probs_in,
    gq, mid, inside, across,
    gf, whead, raw, q, kv, probs, gm_held, sems,
):
    zh_n = raw.shape[2]
    copies = fetched(
        (
            (gf_in, gf),
            (whead_in, whead),
            (raw_in, raw),
            (kv_in, kv),
            (probs_in, probs),
            (q_in, q),
        ),
        sems,
    )
    for copy in copies:
        copy.start()
    copies[0].wait()
    copies[1].wait()
    go = nt(gf[...], whead[...]).astype(BF)
    copies[2].wait()

    def widen(c):
        columns = [0.0] * zh_n
        for side in range(2):
            order = places(side, ny, nx)
            given = go[:, side * 4 * LANE : (side + 1) * 4 * LANE]
            for zh in range(zh_n):
                tiles = [
                    narrow_tile(raw.at[side ^ c], order, zh, t * ro, ro)
                    for t in range(4)
                ]
                columns[zh] = columns[zh] + nt(given, jnp.concatenate(tiles, axis=1))
        gm_held[...] = jnp.concatenate(columns, axis=1).astype(BF)

    on_each_core(widen)
    gm = gm_held[...]
    for copy in copies[3:]:
        copy.wait()
    for pair in range(HEADS // 2):
        at = pl.ds(pair * LANE, LANE)
        vat = pl.ds(HD + pair * LANE, LANE)
        q2, k2, v2 = q[:, at], kv[:, at], kv[:, vat]
        g2 = gm[:, pair * LANE : (pair + 1) * LANE]
        gqs, gks, gvs = [], [], []
        for side in range(2):
            chosen = jnp.where(halves((PTS, LANE), side), g2, jnp.zeros_like(g2))
            gp = nt(chosen, v2)
            held = probs[2 * pair + side]
            weight = held.astype(F32)
            centre = jnp.sum(weight * gp, axis=-1, keepdims=True)
            gs = (weight * (gp - centre) * (1.0 / math.sqrt(HDIM))).astype(BF)
            gqs.append(nn(gs, k2))
            gks.append(tn(gs, q2))
            gvs.append(tn(held, g2))
        gq[:, at] = jnp.where(halves((PTS, LANE), 0), gqs[0], gqs[1]).astype(BF)
        pick = halves((EXT, LANE), 0)
        even = is_even((HALO, LANE))
        for where_at, parts in ((at, gks), (vat, gvs)):
            total = jnp.where(pick, parts[0], parts[1])
            lower, upper = total[:HALO], total[HALO + PTS :]
            inside[:, where_at] = jnp.where(even, upper, lower).astype(BF)
            across[:, where_at] = jnp.where(even, lower, upper).astype(BF)
            mid[:, where_at] = total[HALO : HALO + PTS]


def final_body(
    ny, nx, rs, states, scale, gf, whead, raw, gq, mid, inside, across,
    total, grad, given, held,
):
    zh_n = raw.shape[2]
    centred, inverse = normalised(states[...])
    total[...] = mid[...]
    even = is_even((HALO, D))
    a, b = inside[...].astype(F32), across[...].astype(F32)
    total[:HALO, :] += jnp.where(even, b, a)
    total[PTS - HALO :, :] += jnp.where(even, a, b)
    given[:, :HD] = gq[...]
    given[:, HD:] = total[...].astype(BF)

    def widen(c):
        depth = raw.shape[1] * rs
        for zh in range(zh_n):
            column = 0.0
            for side in range(2):
                order = places(side, ny, nx)
                part = given[:, side * 6 * LANE : (side + 1) * 6 * LANE]
                tiles = [
                    tile_at(raw.at[side ^ c], order, zh, t * rs, rs) for t in range(6)
                ]
                column = column + nt(part, jnp.concatenate(tiles, axis=1))
            held[:, zh * depth : (zh + 1) * depth] = column

    on_each_core(widen)
    gn = held[...]
    g = gn * scale[...]
    back = inverse * (
        g
        - jnp.mean(g, axis=-1, keepdims=True)
        - centred * jnp.mean(g * centred, axis=-1, keepdims=True)
    )
    grad[...] = (nt(gf[...], whead[...]) + back).astype(BF)


def added(parts):
    total = parts[0].astype(F32)
    for i in range(1, parts.shape[0]):
        total = total + parts[i].astype(F32)
    return total


def sum_body(parts, total):
    total[...] = added(parts).astype(BF)


def spread_body(parts, spread):
    total = added(parts).astype(BF)
    for i in range(spread.shape[0]):
        spread[i] = total


def weights_body(scaling, parts, whead, mixing, head):
    flat_head = whead[...]
    rb = head.shape[0]
    total = added(parts) * scaling
    head[...] = total[:rb]
    factor = total[rb:]
    high = factor.astype(BF)
    low = (factor - high.astype(F32)).astype(BF)
    mixing[...] = nt(high, flat_head) + nt(low, flat_head)


def shards(
    states, norm_scale, query, key, value, out_w, head_w, neighbours, observed
):
    members = lax.axis_size(MEMBER)
    devices = lax.axis_size(GRID)
    zh_n = lax.axis_size("zh")
    pn = lax.axis_size(PLANE)
    inputs = states[0]
    rs, ro = query.shape[0], out_w.shape[0]
    packed = 6 * rs + 4 * ro + rs // 2
    swap = [(0, 1), (1, 0)]
    inner = [(i, i ^ 1) for i in range(devices)]
    outer = [(i, i + 1 if i % 2 else i - 1) for i in range(1, devices - 1)]

    (column,) = call(
        pack_body,
        [((zh_n, packed, LANE), BF)],
        (query, key, value, out_w, head_w),
        "AAAAA>V",
        cost=(1e6, 1e6),
        limit=4,
    )
    column = lax.all_to_all(column, "zh", 0, 0, tiled=True)
    even = lax.rem(lax.axis_index("x"), 2) == 0
    inside = lax.ppermute(
        jnp.where(even, inputs[PTS - HALO :], inputs[:HALO]), GRID, inner
    )
    across = lax.ppermute(
        jnp.where(even, inputs[:HALO], inputs[PTS - HALO :]), GRID, outer
    )
    rel = neighbours - (lax.axis_index(GRID) * PTS - HALO)
    scale = norm_scale.reshape(1, D)
    normed, count = call(
        taps_body,
        [((PTS, D), BF), ((PTS, EXT), F32)],
        (inputs, scale, rel),
        "AAA>AA",
        cost=(4e6, 1e6),
        limit=8,
    )
    ny, nx = lax.axis_size("y"), lax.axis_size("x")
    along_x = [[y * nx + x for x in range(nx)] for y in range(ny)]
    along_y = [[y * nx + x for y in range(ny)] for x in range(nx)]

    def widened(block, first, second):
        groups = first + [[pn + i for i in group] for group in second]
        n = len(first[0])
        return lax.all_to_all(
            jnp.broadcast_to(block[None], (n, *block.shape)),
            ("core", "y", "x"),
            0,
            0,
            axis_index_groups=groups,
            tiled=True,
        )

    line = widened(column, along_x, along_y)
    own = widened(line, along_y, along_x).reshape(pn, *column.shape)
    other = lax.ppermute(own, "core", swap)
    ahead, behind, part = call(
        functools.partial(early_body, ny, nx, rs),
        [((HALO, D), BF), ((HALO, D), BF), ((EXT, 6 * LANE), BF)],
        (inside, across, scale, normed, own),
        "VVAAV>VVV",
        cost=(3e8, 4e6),
        limit=8,
    )
    raw_in, raw_out, q, kv, probs, whead, mixed, out, fore, alone = call(
        functools.partial(forward_body, ny, nx, rs, ro),
        [
            ((2, pn, zh_n, 6 * rs, LANE), BF),
            ((2, pn, zh_n, 4 * ro, LANE), BF),
            ((PTS, HD), BF),
            ((EXT, D), BF),
            ((HEADS, PTS, EXT), BF),
            ((D, NVAR), BF),
            ((PTS, HD), BF),
            ((PTS, D), BF),
            ((members, PTS, NVAR), BF),
            ((PTS, NVAR), F32),
        ],
        (ahead, normed, behind, part, inputs, count, own, other),
        "VAVVAAVV>HHHHHAVVVV",
        scratch=(
            pltpu.VMEM((EXT, 3 * HD), BF),
            pltpu.VMEM((HEADS, PTS, EXT), BF),
            pltpu.VMEM((PTS, D), F32),
            pltpu.SemaphoreType.DMA((7,)),
        ),
        cost=(2e9, 1e7),
        limit=24,
    )
    every = lax.all_to_all(fore, MEMBER, 0, 0, tiled=True)
    gf, wg = call(
        functools.partial(score_body, members, zh_n),
        [
            ((PTS, NVAR), BF),
            ((pn, zh_n, (D + HD) // devices, NVAR), BF),
        ],
        (every, alone, observed, mixed, out),
        "VVVVV>AA",
        cost=(1e8, 2e6),
        limit=8,
    )
    plane = lax.all_to_all(wg, PLANE, 0, 0, tiled=True)
    gq, mid, inside, across = call(
        functools.partial(backward_body, ny, nx, ro),
        [((PTS, HD), BF), ((PTS, D), F32), ((HALO, D), BF), ((HALO, D), BF)],
        (gf, whead, raw_out, q, kv, probs),
        "HHHHHH>AAAA",
        scratch=(
            pltpu.VMEM(gf.shape, BF),
            pltpu.VMEM(whead.shape, BF),
            pltpu.VMEM((2, pn, zh_n, 4 * ro, LANE), BF),
            pltpu.VMEM(q.shape, BF),
            pltpu.VMEM(kv.shape, BF),
            pltpu.VMEM(probs.shape, BF),
            pltpu.VMEM((PTS, HD), BF),
            pltpu.SemaphoreType.DMA((6,)),
        ),
        cost=(1e9, 4e6),
        limit=16,
    )
    inside = lax.ppermute(inside, GRID, inner)
    across = lax.ppermute(across, GRID, outer)
    (partial,) = call(
        sum_body,
        [(wg.shape[1:], BF)],
        (plane,),
        "V>A",
        cost=(1e6, 1e6),
        limit=4,
    )
    column = lax.all_to_all(partial, "zh", 0, 0, tiled=True)
    (spread,) = call(
        spread_body,
        [((members, *wg.shape[2:]), BF)],
        (column,),
        "V>A",
        cost=(1e6, 1e6),
        limit=4,
    )
    parts = lax.all_to_all(spread, MEMBER, 0, 0, tiled=True)
    total, grad_input = call(
        functools.partial(final_body, ny, nx, rs),
        [((PTS, D), F32), ((PTS, D), BF)],
        (inputs, scale, gf, whead, raw_in, gq, mid, inside, across),
        "AAAAVAAVV>AA",
        scratch=(
            pltpu.VMEM((PTS, 3 * HD), BF),
            pltpu.VMEM((PTS, D), F32),
        ),
        cost=(1e9, 4e6),
        limit=16,
    )
    scaling = 1.0 / math.sqrt(members * devices * PTS)
    mixing, head = call(
        functools.partial(weights_body, scaling),
        [((HD // devices, D), F32), ((D // devices, NVAR), F32)],
        (parts, whead),
        "VA>AA",
        cost=(1e8, 1e6),
        limit=8,
    )
    return grad_input[None], mixing, head, total[None]


def refined(mesh):
    members, devices = mesh.shape["member"], mesh.shape["grid"]
    cut = {64: (4, 4, 4), 4: (1, 2, 2), 8: (2, 2, 2)}[devices]
    return Mesh(
        mesh.devices.reshape(members // 2, 2, *cut), ("zl", "core", "zh", "y", "x")
    )


def solution(mesh):
    rows = P(GRID, None)

    return jax.shard_map(
        shards,
        mesh=refined(mesh),
        in_specs=(
            P(MEMBER, GRID, None),
            P(),
            rows,
            rows,
            rows,
            rows,
            rows,
            rows,
            rows,
        ),
        out_specs=(P(MEMBER, GRID, None), rows, rows, P(MEMBER, GRID, None)),
        check_vma=False,
    )
```

```python
import functools
import math

import jax
import jax.numpy as jnp
from jax import lax
from jax.experimental import pallas as pl
from jax.experimental.pallas import tpu as pltpu
from jax.sharding import Mesh, PartitionSpec as P


HEADS = 8
HDIM = 64
KNB = 8
HALO = 32
PTS = 128
EXT = PTS + 2 * HALO
D = 1024
HD = 512
NVAR = 128
LANE = 128

epsilon = 1e-05
smooth = 0.1

MEMBER = ("zl", "core")
GRID = ("zh", "y", "x")
PLANE = ("y", "x")
COLUMN = ("zl", "core", "zh")

BF = jnp.bfloat16
F32 = jnp.float32


def nn(a, b):
    return lax.dot_general(a, b, (((1,), (0,)), ((), ())), preferred_element_type=F32)


def nt(a, b):
    return lax.dot_general(a, b, (((1,), (1,)), ((), ())), preferred_element_type=F32)


def tn(a, b):
    return lax.dot_general(a, b, (((0,), (0,)), ((), ())), preferred_element_type=F32)


SPECS = {
    "V": pl.BlockSpec(memory_space=pltpu.VMEM),
    "A": pl.BlockSpec(),
    "H": pl.BlockSpec(memory_space=pltpu.HBM),
}


def call(body, outs, args, places, scratch=(), cost=(1e9, 4e6), limit=16):
    taken, given = places.split(">")
    shapes = [
        jax.ShapeDtypeStruct(s, d) if at == "V" else pltpu.HBM(s, d)
        for (s, d), at in zip(outs, given, strict=True)
    ]
    args = [
        x if at == "V" else pltpu.with_memory_space_constraint(x, pltpu.HBM)
        for x, at in zip(args, taken, strict=True)
    ]
    return pl.pallas_call(
        body,
        out_shape=tuple(shapes),
        in_specs=[SPECS[at] for at in taken],
        out_specs=tuple(SPECS[at] for at in given),
        scratch_shapes=list(scratch),
        compiler_params=pltpu.CompilerParams(vmem_limit_bytes=limit << 20),
        cost_estimate=pl.CostEstimate(
            flops=int(cost[0]), bytes_accessed=int(cost[1]), transcendentals=0
        ),
    )(*args)


def normalised(rows):
    values = rows.astype(F32)
    center = values - jnp.mean(values, axis=-1, keepdims=True)
    inverse = lax.rsqrt(jnp.mean(center * center, axis=-1, keepdims=True) + epsilon)
    return center * inverse, inverse


def taps_body(own, scale, rel, normed, count):
    centred, _ = normalised(own[...])
    normed[...] = (centred * scale[...]).astype(BF)
    place = lax.broadcasted_iota(jnp.int32, (PTS, EXT), 1)
    total = jnp.zeros((PTS, EXT), F32)
    for k in range(KNB):
        total = total + (place == rel[:, k : k + 1]).astype(F32)
    count[...] = total


def halves(tile_shape, head):
    lane = lax.broadcasted_iota(jnp.int32, tile_shape, 1)
    return (lane < HDIM) if head == 0 else (lane >= HDIM)


def fetched(pairs, sems):
    return [pltpu.make_async_copy(s, d, sems.at[i]) for i, (s, d) in enumerate(pairs)]


def pack_body(query, key, value, out, head, column):
    rs, ro = query.shape[0], out.shape[0]

    def put(row, tile):
        size = tile.shape[0]
        for i in range(column.shape[0]):
            column[i, row : row + size, :] = tile

    for c in range(2):

        @pl.when(lax.axis_index("core") == c)
        def _():
            for t in range(6):
                weight = (query, key, value)[(6 * c + t) // 4]
                lane = (6 * c + t) % 4 * LANE
                put(t * rs, weight[:, lane : lane + LANE])
            for t in range(4):
                lane = (4 * c + t) * LANE
                put(6 * rs + t * ro, out[:, lane : lane + LANE])
            put(6 * rs + 4 * ro, head[c * rs // 2 : (c + 1) * rs // 2, :])


def places(side, ny, nx):
    return [
        y * nx + x if side == 0 else x * ny + y for y in range(ny) for x in range(nx)
    ]


def on_each_core(body):
    for c in range(2):
        pl.when(lax.axis_index("core") == c)(functools.partial(body, c))


def tile_at(buf, order, zh, start, size):
    return jnp.concatenate([buf[i, zh, start : start + size, :] for i in order], axis=0)


def narrow_tile(buf, order, zh, start, size):
    parts = [buf[i, zh, start : start + size, :].astype(F32) for i in order]
    return jnp.concatenate(parts, axis=0).astype(BF)


def projected(rows, buf, order, rs):
    total = 0.0
    depth = buf.shape[0] * rs
    for zh in range(buf.shape[1]):
        tiles = [tile_at(buf, order, zh, t * rs, rs) for t in range(6)]
        total = total + nn(
            rows[:, zh * depth : (zh + 1) * depth], jnp.concatenate(tiles, axis=1)
        )
    return total.astype(BF)


def is_even(shape):
    return jnp.full(shape, lax.rem(lax.axis_index("x"), 2), jnp.int32) == 0


def early_body(
    ny, nx, rs, inside, across, scale, normed, own, ahead, behind, part
):
    even = is_even((HALO, D))
    a, b = inside[...].astype(F32), across[...].astype(F32)
    for block, to in ((jnp.where(even, b, a), ahead), (jnp.where(even, a, b), behind)):
        centred, _ = normalised(block)
        to[...] = (centred * scale[...]).astype(BF)
    rows = jnp.concatenate([ahead[...], normed[...], behind[...]], axis=0)

    def project(c):
        part[...] = projected(rows, own, places(c, ny, nx), rs)

    on_each_core(project)


def forward_body(
    ny, nx, rs, ro, ahead, normed, behind, part, states, count, own, other,
    raw_in, raw_out, q_out, kv_out, probs_out, whead, mixed, out, fore, alone,
    qkv, probs, added_out, sems,
):
    pn, zh_n = own.shape[:2]
    qrows = 6 * rs
    orows = 4 * ro
    hr = rs // 2
    raws = fetched(
        [
            (buf.at[:, :, pl.ds(start, to.shape[3]), :], to.at[i])
            for i, buf in enumerate((own, other))
            for start, to in ((qrows, raw_out), (0, raw_in))
        ],
        sems.at[pl.ds(3, 4)],
    )
    for copy in raws:
        copy.start()
    rows = jnp.concatenate([ahead[...], normed[...], behind[...]], axis=0)
    width = 6 * LANE

    def project(c):
        there = projected(rows, other, places(1 - c, ny, nx), rs)
        qkv[:, c * width : (c + 1) * width] = part[...]
        qkv[:, (1 - c) * width : (2 - c) * width] = there

    on_each_core(project)
    leaving = fetched(
        (
            (qkv.at[HALO : HALO + PTS, 0:HD], q_out),
            (qkv.at[:, HD : 3 * HD], kv_out),
            (probs, probs_out),
        ),
        sems,
    )
    leaving[0].start()
    leaving[1].start()
    times = count[...]
    here = times > 0
    for pair in range(HEADS // 2):
        at = pl.ds(pair * LANE, LANE)
        q2 = qkv[HALO : HALO + PTS, pair * LANE : (pair + 1) * LANE]
        k2 = qkv[:, HD + pair * LANE : HD + (pair + 1) * LANE]
        v2 = qkv[:, 2 * HD + pair * LANE : 2 * HD + (pair + 1) * LANE]
        got = []
        for side in range(2):
            chosen = jnp.where(halves((PTS, LANE), side), q2, jnp.zeros_like(q2))
            score = nt(chosen, k2) * (1.0 / math.sqrt(HDIM))
            score = jnp.where(here, score, -1e30)
            highest = jnp.max(score, axis=-1, keepdims=True)
            power = jnp.exp(score - highest)
            prob = power / jnp.sum(times * power, axis=-1, keepdims=True)
            weight = (times * prob.astype(BF).astype(F32)).astype(BF)
            probs[2 * pair + side] = weight
            got.append(nn(weight, v2))
        mixed[:, at] = jnp.where(halves((PTS, LANE), 0), got[0], got[1]).astype(BF)
    leaving[2].start()
    attended = mixed[...]
    at_head = qrows + orows

    def finish(c):
        wide = 4 * LANE
        depth = pn * ro
        orders = [places(0, ny, nx), places(1, ny, nx)]
        bufs = (own, other) if c == 0 else (other, own)
        for side in range(2):
            total = 0.0
            for zh in range(zh_n):
                tiles = [
                    narrow_tile(bufs[side], orders[side], zh, qrows + t * ro, ro)
                    for t in range(4)
                ]
                total = total + nn(
                    attended[:, zh * depth : (zh + 1) * depth],
                    jnp.concatenate(tiles, axis=1),
                )
            added_out[:, side * wide : (side + 1) * wide] = total
        pieces = []
        for zh in range(zh_n):
            for ij in zip(*orders):
                for side in range(2):
                    block = bufs[side][ij[side], zh, at_head : at_head + hr, :]
                    pieces.append(block.astype(F32))
        whead[...] = jnp.concatenate(pieces, axis=0).astype(BF)

    on_each_core(finish)
    layer = (states[...].astype(F32) + added_out[...]).astype(BF)
    out[...] = layer
    mine = nn(layer, whead[...])
    alone[...] = mine
    for i in range(fore.shape[0]):
        fore[i] = mine.astype(BF)
    for copy in raws + leaving:
        copy.wait()


def slope(z):
    return z * lax.rsqrt(z * z + smooth * smooth)


def score_body(members, zh_n, every, alone, observed, mixed, out, gf, wg):
    mine = alone[...]
    sent = mine.astype(BF).astype(F32)
    total = jnp.zeros_like(mine)
    for m in range(members):
        total = total + slope(sent - every[m].astype(F32))
    grad = (slope(mine - observed[...]) - total * (1.0 / (members - 1))).astype(BF)
    gf[...] = grad
    pn = wg.shape[0]
    heads = tn(out[...], grad)
    factor = tn(mixed[...], grad)
    rb, ra = D // (zh_n * pn), HD // (zh_n * pn)
    for zh in range(zh_n):
        wg[:, zh, 0:rb, :] = (
            heads[zh * pn * rb : (zh + 1) * pn * rb].reshape(pn, rb, NVAR).astype(BF)
        )
        wg[:, zh, rb : rb + ra, :] = (
            factor[zh * pn * ra : (zh + 1) * pn * ra].reshape(pn, ra, NVAR).astype(BF)
        )


def backward_body(
    ny, nx, ro, gf_in, whead_in, raw_in, q_in, kv_in, probs_in,
    gq, mid, inside, across,
    gf, whead, raw, q, kv, probs, gm_held, sems,
):
    zh_n = raw.shape[2]
    copies = fetched(
        (
            (gf_in, gf),
            (whead_in, whead),
            (raw_in, raw),
            (kv_in, kv),
            (probs_in, probs),
            (q_in, q),
        ),
        sems,
    )
    for copy in copies:
        copy.start()
    copies[0].wait()
    copies[1].wait()
    go = nt(gf[...], whead[...]).astype(BF)
    copies[2].wait()

    def widen(c):
        columns = [0.0] * zh_n
        for side in range(2):
            order = places(side, ny, nx)
            given = go[:, side * 4 * LANE : (side + 1) * 4 * LANE]
            for zh in range(zh_n):
                tiles = [
                    narrow_tile(raw.at[side ^ c], order, zh, t * ro, ro)
                    for t in range(4)
                ]
                columns[zh] = columns[zh] + nt(given, jnp.concatenate(tiles, axis=1))
        gm_held[...] = jnp.concatenate(columns, axis=1).astype(BF)

    on_each_core(widen)
    gm = gm_held[...]
    for copy in copies[3:]:
        copy.wait()
    for pair in range(HEADS // 2):
        at = pl.ds(pair * LANE, LANE)
        vat = pl.ds(HD + pair * LANE, LANE)
        q2, k2, v2 = q[:, at], kv[:, at], kv[:, vat]
        g2 = gm[:, pair * LANE : (pair + 1) * LANE]
        gqs, gks, gvs = [], [], []
        for side in range(2):
            chosen = jnp.where(halves((PTS, LANE), side), g2, jnp.zeros_like(g2))
            gp = nt(chosen, v2)
            held = probs[2 * pair + side]
            weight = held.astype(F32)
            centre = jnp.sum(weight * gp, axis=-1, keepdims=True)
            gs = (weight * (gp - centre) * (1.0 / math.sqrt(HDIM))).astype(BF)
            gqs.append(nn(gs, k2))
            gks.append(tn(gs, q2))
            gvs.append(tn(held, g2))
        gq[:, at] = jnp.where(halves((PTS, LANE), 0), gqs[0], gqs[1]).astype(BF)
        pick = halves((EXT, LANE), 0)
        even = is_even((HALO, LANE))
        for where_at, parts in ((at, gks), (vat, gvs)):
            total = jnp.where(pick, parts[0], parts[1])
            lower, upper = total[:HALO], total[HALO + PTS :]
            inside[:, where_at] = jnp.where(even, upper, lower).astype(BF)
            across[:, where_at] = jnp.where(even, lower, upper).astype(BF)
            mid[:, where_at] = total[HALO : HALO + PTS]


def final_body(
    ny, nx, rs, states, scale, gf, whead, raw, gq, mid, inside, across,
    total, grad, head_again, given, held,
):
    zh_n = raw.shape[2]
    head_again[...] = whead[...]
    centred, inverse = normalised(states[...])
    total[...] = mid[...]
    even = is_even((HALO, D))
    a, b = inside[...].astype(F32), across[...].astype(F32)
    total[:HALO, :] += jnp.where(even, b, a)
    total[PTS - HALO :, :] += jnp.where(even, a, b)
    given[:, :HD] = gq[...]
    given[:, HD:] = total[...].astype(BF)

    def widen(c):
        depth = raw.shape[1] * rs
        for zh in range(zh_n):
            column = 0.0
            for side in range(2):
                order = places(side, ny, nx)
                part = given[:, side * 6 * LANE : (side + 1) * 6 * LANE]
                tiles = [
                    tile_at(raw.at[side ^ c], order, zh, t * rs, rs) for t in range(6)
                ]
                column = column + nt(part, jnp.concatenate(tiles, axis=1))
            held[:, zh * depth : (zh + 1) * depth] = column

    on_each_core(widen)
    gn = held[...]
    g = gn * scale[...]
    back = inverse * (
        g
        - jnp.mean(g, axis=-1, keepdims=True)
        - centred * jnp.mean(g * centred, axis=-1, keepdims=True)
    )
    grad[...] = (nt(gf[...], whead[...]) + back).astype(BF)


def added(parts):
    total = parts[0].astype(F32)
    for i in range(1, parts.shape[0]):
        total = total + parts[i].astype(F32)
    return total


def spread_body(parts, spread):
    total = added(parts).astype(BF)
    for i in range(spread.shape[0]):
        spread[i] = total


def weights_body(scaling, parts, whead, mixing, head):
    flat_head = whead[...]
    rb = head.shape[0]
    total = added(parts) * scaling
    head[...] = total[:rb]
    factor = total[rb:]
    high = factor.astype(BF)
    low = (factor - high.astype(F32)).astype(BF)
    mixing[...] = nt(high, flat_head) + nt(low, flat_head)


def shards(
    states, norm_scale, query, key, value, out_w, head_w, neighbours, observed
):
    members = lax.axis_size(MEMBER)
    devices = lax.axis_size(GRID)
    zh_n = lax.axis_size("zh")
    pn = lax.axis_size(PLANE)
    inputs = states[0]
    rs, ro = query.shape[0], out_w.shape[0]
    packed = 6 * rs + 4 * ro + rs // 2
    swap = [(0, 1), (1, 0)]
    inner = [(i, i ^ 1) for i in range(devices)]
    outer = [(i, i + 1 if i % 2 else i - 1) for i in range(1, devices - 1)]

    (column,) = call(
        pack_body,
        [((zh_n, packed, LANE), BF)],
        (query, key, value, out_w, head_w),
        "AAAAA>V",
        cost=(1e6, 1e6),
        limit=4,
    )
    column = lax.all_to_all(column, "zh", 0, 0, tiled=True)
    even = lax.rem(lax.axis_index("x"), 2) == 0
    inside = lax.ppermute(
        jnp.where(even, inputs[PTS - HALO :], inputs[:HALO]), GRID, inner
    )
    across = lax.ppermute(
        jnp.where(even, inputs[:HALO], inputs[PTS - HALO :]), GRID, outer
    )
    rel = neighbours - (lax.axis_index(GRID) * PTS - HALO)
    scale = norm_scale.reshape(1, D)
    normed, count = call(
        taps_body,
        [((PTS, D), BF), ((PTS, EXT), F32)],
        (inputs, scale, rel),
        "AAA>AA",
        cost=(4e6, 1e6),
        limit=8,
    )
    ny, nx = lax.axis_size("y"), lax.axis_size("x")
    along_x = [[y * nx + x for x in range(nx)] for y in range(ny)]
    along_y = [[y * nx + x for y in range(ny)] for x in range(nx)]

    def widened(block, first, second):
        groups = first + [[pn + i for i in group] for group in second]
        n = len(first[0])
        return lax.all_to_all(
            jnp.broadcast_to(block[None], (n, *block.shape)),
            ("core", "y", "x"),
            0,
            0,
            axis_index_groups=groups,
            tiled=True,
        )

    line = widened(column, along_x, along_y)
    own = widened(line, along_y, along_x).reshape(pn, *column.shape)
    other = lax.ppermute(own, "core", swap)
    ahead, behind, part = call(
        functools.partial(early_body, ny, nx, rs),
        [((HALO, D), BF), ((HALO, D), BF), ((EXT, 6 * LANE), BF)],
        (inside, across, scale, normed, own),
        "VVAAV>VVV",
        cost=(3e8, 4e6),
        limit=8,
    )
    raw_in, raw_out, q, kv, probs, whead, mixed, out, fore, alone = call(
        functools.partial(forward_body, ny, nx, rs, ro),
        [
            ((2, pn, zh_n, 6 * rs, LANE), BF),
            ((2, pn, zh_n, 4 * ro, LANE), BF),
            ((PTS, HD), BF),
            ((EXT, D), BF),
            ((HEADS, PTS, EXT), BF),
            ((D, NVAR), BF),
            ((PTS, HD), BF),
            ((PTS, D), BF),
            ((members, PTS, NVAR), BF),
            ((PTS, NVAR), F32),
        ],
        (ahead, normed, behind, part, inputs, count, own, other),
        "VAVVAAVV>HHHHHAVVVV",
        scratch=(
            pltpu.VMEM((EXT, 3 * HD), BF),
            pltpu.VMEM((HEADS, PTS, EXT), BF),
            pltpu.VMEM((PTS, D), F32),
            pltpu.SemaphoreType.DMA((7,)),
        ),
        cost=(2e9, 1e7),
        limit=24,
    )
    every = lax.all_to_all(fore, MEMBER, 0, 0, tiled=True)
    gf, wg = call(
        functools.partial(score_body, members, zh_n),
        [
            ((PTS, NVAR), BF),
            ((pn, zh_n, (D + HD) // devices, NVAR), BF),
        ],
        (every, alone, observed, mixed, out),
        "VVVVV>AA",
        cost=(1e8, 2e6),
        limit=8,
    )
    plane = lax.all_to_all(wg, PLANE, 0, 0, tiled=True)
    gq, mid, inside, across = call(
        functools.partial(backward_body, ny, nx, ro),
        [((PTS, HD), BF), ((PTS, D), F32), ((HALO, D), BF), ((HALO, D), BF)],
        (gf, whead, raw_out, q, kv, probs),
        "HHHHHH>AAAA",
        scratch=(
            pltpu.VMEM(gf.shape, BF),
            pltpu.VMEM(whead.shape, BF),
            pltpu.VMEM((2, pn, zh_n, 4 * ro, LANE), BF),
            pltpu.VMEM(q.shape, BF),
            pltpu.VMEM(kv.shape, BF),
            pltpu.VMEM(probs.shape, BF),
            pltpu.VMEM((PTS, HD), BF),
            pltpu.SemaphoreType.DMA((6,)),
        ),
        cost=(1e9, 4e6),
        limit=16,
    )
    inside = lax.ppermute(inside, GRID, inner)
    across = lax.ppermute(across, GRID, outer)
    (spread,) = call(
        spread_body,
        [((members, *wg.shape[1:]), BF)],
        (plane,),
        "V>A",
        cost=(1e6, 1e6),
        limit=4,
    )
    parts = lax.all_to_all(
        spread.reshape(members * zh_n, *wg.shape[2:]), COLUMN, 0, 0, tiled=True
    )
    total, grad_input, head_again = call(
        functools.partial(final_body, ny, nx, rs),
        [((PTS, D), F32), ((PTS, D), BF), ((D, NVAR), BF)],
        (inputs, scale, gf, whead, raw_in, gq, mid, inside, across),
        "AAAAVAAVV>AAV",
        scratch=(
            pltpu.VMEM((PTS, 3 * HD), BF),
            pltpu.VMEM((PTS, D), F32),
        ),
        cost=(1e9, 4e6),
        limit=16,
    )
    scaling = 1.0 / math.sqrt(members * devices * PTS)
    mixing, head = call(
        functools.partial(weights_body, scaling),
        [((HD // devices, D), F32), ((D // devices, NVAR), F32)],
        (parts, head_again),
        "VV>AA",
        cost=(1e8, 1e6),
        limit=8,
    )
    return grad_input[None], mixing, head, total[None]


def refined(mesh):
    members, devices = mesh.shape["member"], mesh.shape["grid"]
    cut = {64: (4, 4, 4), 4: (1, 2, 2), 8: (2, 2, 2)}[devices]
    return Mesh(
        mesh.devices.reshape(members // 2, 2, *cut), ("zl", "core", "zh", "y", "x")
    )


def solution(mesh):
    rows = P(GRID, None)

    return jax.shard_map(
        shards,
        mesh=refined(mesh),
        in_specs=(
            P(MEMBER, GRID, None),
            P(),
            rows,
            rows,
            rows,
            rows,
            rows,
            rows,
            rows,
        ),
        out_specs=(P(MEMBER, GRID, None), rows, rows, P(MEMBER, GRID, None)),
        check_vma=False,
    )
```

```python
import functools
import math

import jax
import jax.numpy as jnp
from jax import lax
from jax.experimental import pallas as pl
from jax.experimental.pallas import tpu as pltpu
from jax.sharding import Mesh, PartitionSpec as P


HEADS = 8
HDIM = 64
KNB = 8
HALO = 32
PTS = 128
EXT = PTS + 2 * HALO
D = 1024
HD = 512
NVAR = 128
LANE = 128

epsilon = 1e-05
smooth = 0.1

MEMBER = ("zl", "core")
GRID = ("zh", "y", "x")
PLANE = ("y", "x")

BF = jnp.bfloat16
F32 = jnp.float32


def nn(a, b):
    return lax.dot_general(a, b, (((1,), (0,)), ((), ())), preferred_element_type=F32)


def nt(a, b):
    return lax.dot_general(a, b, (((1,), (1,)), ((), ())), preferred_element_type=F32)


def tn(a, b):
    return lax.dot_general(a, b, (((0,), (0,)), ((), ())), preferred_element_type=F32)


SPECS = {
    "V": pl.BlockSpec(memory_space=pltpu.VMEM),
    "A": pl.BlockSpec(),
    "H": pl.BlockSpec(memory_space=pltpu.HBM),
}


def call(body, outs, args, places, scratch=(), cost=(1e9, 4e6), limit=16):
    taken, given = places.split(">")
    shapes = [
        jax.ShapeDtypeStruct(s, d) if at == "V" else pltpu.HBM(s, d)
        for (s, d), at in zip(outs, given, strict=True)
    ]
    args = [
        x if at == "V" else pltpu.with_memory_space_constraint(x, pltpu.HBM)
        for x, at in zip(args, taken, strict=True)
    ]
    return pl.pallas_call(
        body,
        out_shape=tuple(shapes),
        in_specs=[SPECS[at] for at in taken],
        out_specs=tuple(SPECS[at] for at in given),
        scratch_shapes=list(scratch),
        compiler_params=pltpu.CompilerParams(vmem_limit_bytes=limit << 20),
        cost_estimate=pl.CostEstimate(
            flops=int(cost[0]), bytes_accessed=int(cost[1]), transcendentals=0
        ),
    )(*args)


def normalised(rows):
    values = rows.astype(F32)
    center = values - jnp.mean(values, axis=-1, keepdims=True)
    inverse = lax.rsqrt(jnp.mean(center * center, axis=-1, keepdims=True) + epsilon)
    return center * inverse, inverse


def taps_body(own, scale, rel, normed, count):
    centred, _ = normalised(own[...])
    normed[...] = (centred * scale[...]).astype(BF)
    place = lax.broadcasted_iota(jnp.int32, (PTS, EXT), 1)
    total = jnp.zeros((PTS, EXT), F32)
    for k in range(KNB):
        total = total + (place == rel[:, k : k + 1]).astype(F32)
    count[...] = total


def halves(tile_shape, head):
    lane = lax.broadcasted_iota(jnp.int32, tile_shape, 1)
    return (lane < HDIM) if head == 0 else (lane >= HDIM)


def fetched(pairs, sems):
    return [pltpu.make_async_copy(s, d, sems.at[i]) for i, (s, d) in enumerate(pairs)]


def pack_body(query, key, value, out, head, column):
    rs, ro = query.shape[0], out.shape[0]

    def put(row, tile):
        size = tile.shape[0]
        for i in range(column.shape[0]):
            column[i, row : row + size, :] = tile

    for c in range(2):

        @pl.when(lax.axis_index("core") == c)
        def _():
            for t in range(6):
                weight = (query, key, value)[(6 * c + t) // 4]
                lane = (6 * c + t) % 4 * LANE
                put(t * rs, weight[:, lane : lane + LANE])
            for t in range(4):
                lane = (4 * c + t) * LANE
                put(6 * rs + t * ro, out[:, lane : lane + LANE])
            put(6 * rs + 4 * ro, head[c * rs // 2 : (c + 1) * rs // 2, :])


def places(side, ny, nx):
    return [
        y * nx + x if side == 0 else x * ny + y for y in range(ny) for x in range(nx)
    ]


def on_each_core(body):
    for c in range(2):
        pl.when(lax.axis_index("core") == c)(functools.partial(body, c))


def tile_at(buf, order, zh, start, size):
    return jnp.concatenate([buf[i, zh, start : start + size, :] for i in order], axis=0)


def narrow_tile(buf, order, zh, start, size):
    parts = [buf[i, zh, start : start + size, :].astype(F32) for i in order]
    return jnp.concatenate(parts, axis=0).astype(BF)


def projected(rows, buf, order, rs):
    total = 0.0
    depth = buf.shape[0] * rs
    for zh in range(buf.shape[1]):
        tiles = [tile_at(buf, order, zh, t * rs, rs) for t in range(6)]
        total = total + nn(
            rows[:, zh * depth : (zh + 1) * depth], jnp.concatenate(tiles, axis=1)
        )
    return total.astype(BF)


def is_even(shape):
    return jnp.full(shape, lax.rem(lax.axis_index("x"), 2), jnp.int32) == 0


def early_body(
    ny, nx, rs, inside, across, scale, normed, own, ahead, behind, part
):
    even = is_even((HALO, D))
    a, b = inside[...].astype(F32), across[...].astype(F32)
    for block, to in ((jnp.where(even, b, a), ahead), (jnp.where(even, a, b), behind)):
        centred, _ = normalised(block)
        to[...] = (centred * scale[...]).astype(BF)
    rows = jnp.concatenate([ahead[...], normed[...], behind[...]], axis=0)

    def project(c):
        part[...] = projected(rows, own, places(c, ny, nx), rs)

    on_each_core(project)


def forward_body(
    ny, nx, rs, ro, ahead, normed, behind, part, states, count, own, other,
    raw_in, raw_out, q_out, kv_out, probs_out, whead, mixed, out, fore, alone,
    qkv, probs, added_out, sems,
):
    pn, zh_n = own.shape[:2]
    qrows = 6 * rs
    orows = 4 * ro
    hr = rs // 2
    raws = fetched(
        [
            (buf.at[:, :, pl.ds(start, to.shape[3]), :], to.at[i])
            for i, buf in enumerate((own, other))
            for start, to in ((qrows, raw_out), (0, raw_in))
        ],
        sems.at[pl.ds(3, 4)],
    )
    for copy in raws:
        copy.start()
    rows = jnp.concatenate([ahead[...], normed[...], behind[...]], axis=0)
    width = 6 * LANE

    def project(c):
        there = projected(rows, other, places(1 - c, ny, nx), rs)
        qkv[:, c * width : (c + 1) * width] = part[...]
        qkv[:, (1 - c) * width : (2 - c) * width] = there

    on_each_core(project)
    leaving = fetched(
        (
            (qkv.at[HALO : HALO + PTS, 0:HD], q_out),
            (qkv.at[:, HD : 3 * HD], kv_out),
            (probs, probs_out),
        ),
        sems,
    )
    leaving[0].start()
    leaving[1].start()
    times = count[...]
    here = times > 0
    for pair in range(HEADS // 2):
        at = pl.ds(pair * LANE, LANE)
        q2 = qkv[HALO : HALO + PTS, pair * LANE : (pair + 1) * LANE]
        k2 = qkv[:, HD + pair * LANE : HD + (pair + 1) * LANE]
        v2 = qkv[:, 2 * HD + pair * LANE : 2 * HD + (pair + 1) * LANE]
        got = []
        for side in range(2):
            chosen = jnp.where(halves((PTS, LANE), side), q2, jnp.zeros_like(q2))
            score = nt(chosen, k2) * (1.0 / math.sqrt(HDIM))
            score = jnp.where(here, score, -1e30)
            highest = jnp.max(score, axis=-1, keepdims=True)
            power = jnp.exp(score - highest)
            prob = power / jnp.sum(times * power, axis=-1, keepdims=True)
            weight = (times * prob.astype(BF).astype(F32)).astype(BF)
            probs[2 * pair + side] = weight
            got.append(nn(weight, v2))
        mixed[:, at] = jnp.where(halves((PTS, LANE), 0), got[0], got[1]).astype(BF)
    leaving[2].start()
    attended = mixed[...]
    at_head = qrows + orows

    def finish(c):
        wide = 4 * LANE
        depth = pn * ro
        orders = [places(0, ny, nx), places(1, ny, nx)]
        bufs = (own, other) if c == 0 else (other, own)
        for side in range(2):
            total = 0.0
            for zh in range(zh_n):
                tiles = [
                    narrow_tile(bufs[side], orders[side], zh, qrows + t * ro, ro)
                    for t in range(4)
                ]
                total = total + nn(
                    attended[:, zh * depth : (zh + 1) * depth],
                    jnp.concatenate(tiles, axis=1),
                )
            added_out[:, side * wide : (side + 1) * wide] = total
        pieces = []
        for zh in range(zh_n):
            for ij in zip(*orders):
                for side in range(2):
                    block = bufs[side][ij[side], zh, at_head : at_head + hr, :]
                    pieces.append(block.astype(F32))
        whead[...] = jnp.concatenate(pieces, axis=0).astype(BF)

    on_each_core(finish)
    layer = (states[...].astype(F32) + added_out[...]).astype(BF)
    out[...] = layer
    mine = nn(layer, whead[...])
    alone[...] = mine
    for i in range(fore.shape[0]):
        fore[i] = mine.astype(BF)
    for copy in raws + leaving:
        copy.wait()


def slope(z):
    return z * lax.rsqrt(z * z + smooth * smooth)


def score_body(members, zh_n, every, alone, observed, mixed, out, gf, wg):
    mine = alone[...]
    sent = mine.astype(BF).astype(F32)
    total = jnp.zeros_like(mine)
    for m in range(members):
        total = total + slope(sent - every[m].astype(F32))
    grad = (slope(mine - observed[...]) - total * (1.0 / (members - 1))).astype(BF)
    gf[...] = grad
    pn = wg.shape[0]
    heads = tn(out[...], grad)
    factor = tn(mixed[...], grad)
    rb, ra = D // (zh_n * pn), HD // (zh_n * pn)
    for zh in range(zh_n):
        wg[:, zh, 0:rb, :] = (
            heads[zh * pn * rb : (zh + 1) * pn * rb].reshape(pn, rb, NVAR).astype(BF)
        )
        wg[:, zh, rb : rb + ra, :] = (
            factor[zh * pn * ra : (zh + 1) * pn * ra].reshape(pn, ra, NVAR).astype(BF)
        )


def backward_body(
    ny, nx, ro, gf_in, whead_in, raw_in, q_in, kv_in, probs_in,
    gq, mid, inside, across,
    gf, whead, raw, q, kv, probs, gm_held, sems,
):
    zh_n = raw.shape[2]
    copies = fetched(
        (
            (gf_in, gf),
            (whead_in, whead),
            (raw_in, raw),
            (kv_in, kv),
            (probs_in, probs),
            (q_in, q),
        ),
        sems,
    )
    for copy in copies:
        copy.start()
    copies[0].wait()
    copies[1].wait()
    go = nt(gf[...], whead[...]).astype(BF)
    copies[2].wait()

    def widen(c):
        columns = [0.0] * zh_n
        for side in range(2):
            order = places(side, ny, nx)
            given = go[:, side * 4 * LANE : (side + 1) * 4 * LANE]
            for zh in range(zh_n):
                tiles = [
                    narrow_tile(raw.at[side ^ c], order, zh, t * ro, ro)
                    for t in range(4)
                ]
                columns[zh] = columns[zh] + nt(given, jnp.concatenate(tiles, axis=1))
        gm_held[...] = jnp.concatenate(columns, axis=1).astype(BF)

    on_each_core(widen)
    gm = gm_held[...]
    for copy in copies[3:]:
        copy.wait()
    for pair in range(HEADS // 2):
        at = pl.ds(pair * LANE, LANE)
        vat = pl.ds(HD + pair * LANE, LANE)
        q2, k2, v2 = q[:, at], kv[:, at], kv[:, vat]
        g2 = gm[:, pair * LANE : (pair + 1) * LANE]
        gqs, gks, gvs = [], [], []
        for side in range(2):
            chosen = jnp.where(halves((PTS, LANE), side), g2, jnp.zeros_like(g2))
            gp = nt(chosen, v2)
            held = probs[2 * pair + side]
            weight = held.astype(F32)
            centre = jnp.sum(weight * gp, axis=-1, keepdims=True)
            gs = (weight * (gp - centre) * (1.0 / math.sqrt(HDIM))).astype(BF)
            gqs.append(nn(gs, k2))
            gks.append(tn(gs, q2))
            gvs.append(tn(held, g2))
        gq[:, at] = jnp.where(halves((PTS, LANE), 0), gqs[0], gqs[1]).astype(BF)
        pick = halves((EXT, LANE), 0)
        even = is_even((HALO, LANE))
        for where_at, parts in ((at, gks), (vat, gvs)):
            total = jnp.where(pick, parts[0], parts[1])
            lower, upper = total[:HALO], total[HALO + PTS :]
            inside[:, where_at] = jnp.where(even, upper, lower).astype(BF)
            across[:, where_at] = jnp.where(even, lower, upper).astype(BF)
            mid[:, where_at] = total[HALO : HALO + PTS]


def final_body(
    ny, nx, rs, states, scale, gf, whead, raw, gq, mid, inside, across,
    total, grad, given, held,
):
    zh_n = raw.shape[2]
    centred, inverse = normalised(states[...])
    total[...] = mid[...]
    even = is_even((HALO, D))
    a, b = inside[...].astype(F32), across[...].astype(F32)
    total[:HALO, :] += jnp.where(even, b, a)
    total[PTS - HALO :, :] += jnp.where(even, a, b)
    given[:, :HD] = gq[...]
    given[:, HD:] = total[...].astype(BF)

    def widen(c):
        depth = raw.shape[1] * rs
        for zh in range(zh_n):
            column = 0.0
            for side in range(2):
                order = places(side, ny, nx)
                part = given[:, side * 6 * LANE : (side + 1) * 6 * LANE]
                tiles = [
                    tile_at(raw.at[side ^ c], order, zh, t * rs, rs) for t in range(6)
                ]
                column = column + nt(part, jnp.concatenate(tiles, axis=1))
            held[:, zh * depth : (zh + 1) * depth] = column

    on_each_core(widen)
    gn = held[...]
    g = gn * scale[...]
    back = inverse * (
        g
        - jnp.mean(g, axis=-1, keepdims=True)
        - centred * jnp.mean(g * centred, axis=-1, keepdims=True)
    )
    grad[...] = (nt(gf[...], whead[...]) + back).astype(BF)


def added(parts):
    total = parts[0].astype(F32)
    for i in range(1, parts.shape[0]):
        total = total + parts[i].astype(F32)
    return total


def sum_body(parts, total):
    total[...] = added(parts).astype(BF)


def spread_body(parts, spread):
    total = added(parts).astype(BF)
    for i in range(spread.shape[0]):
        spread[i] = total


def weights_body(scaling, parts, whead_in, mixing, head, whead, sems):
    (arriving,) = fetched(((whead_in, whead),), sems)
    arriving.start()
    rb = head.shape[0]
    total = added(parts) * scaling
    head[...] = total[:rb]
    factor = total[rb:]
    high = factor.astype(BF)
    low = (factor - high.astype(F32)).astype(BF)
    arriving.wait()
    flat_head = whead[...]
    mixing[...] = nt(high, flat_head) + nt(low, flat_head)


def shards(
    states, norm_scale, query, key, value, out_w, head_w, neighbours, observed
):
    members = lax.axis_size(MEMBER)
    devices = lax.axis_size(GRID)
    zh_n = lax.axis_size("zh")
    pn = lax.axis_size(PLANE)
    inputs = states[0]
    rs, ro = query.shape[0], out_w.shape[0]
    packed = 6 * rs + 4 * ro + rs // 2
    swap = [(0, 1), (1, 0)]
    inner = [(i, i ^ 1) for i in range(devices)]
    outer = [(i, i + 1 if i % 2 else i - 1) for i in range(1, devices - 1)]

    (column,) = call(
        pack_body,
        [((zh_n, packed, LANE), BF)],
        (query, key, value, out_w, head_w),
        "AAAAA>V",
        cost=(1e6, 1e6),
        limit=4,
    )
    column = lax.all_to_all(column, "zh", 0, 0, tiled=True)
    even = lax.rem(lax.axis_index("x"), 2) == 0
    inside = lax.ppermute(
        jnp.where(even, inputs[PTS - HALO :], inputs[:HALO]), GRID, inner
    )
    across = lax.ppermute(
        jnp.where(even, inputs[:HALO], inputs[PTS - HALO :]), GRID, outer
    )
    rel = neighbours - (lax.axis_index(GRID) * PTS - HALO)
    scale = norm_scale.reshape(1, D)
    normed, count = call(
        taps_body,
        [((PTS, D), BF), ((PTS, EXT), F32)],
        (inputs, scale, rel),
        "AAA>AA",
        cost=(4e6, 1e6),
        limit=8,
    )
    ny, nx = lax.axis_size("y"), lax.axis_size("x")
    along_x = [[y * nx + x for x in range(nx)] for y in range(ny)]
    along_y = [[y * nx + x for y in range(ny)] for x in range(nx)]

    def widened(block, first, second):
        groups = first + [[pn + i for i in group] for group in second]
        n = len(first[0])
        return lax.all_to_all(
            jnp.broadcast_to(block[None], (n, *block.shape)),
            ("core", "y", "x"),
            0,
            0,
            axis_index_groups=groups,
            tiled=True,
        )

    line = widened(column, along_x, along_y)
    own = widened(line, along_y, along_x).reshape(pn, *column.shape)
    other = lax.ppermute(own, "core", swap)
    ahead, behind, part = call(
        functools.partial(early_body, ny, nx, rs),
        [((HALO, D), BF), ((HALO, D), BF), ((EXT, 6 * LANE), BF)],
        (inside, across, scale, normed, own),
        "VVAAV>VVV",
        cost=(3e8, 4e6),
        limit=8,
    )
    raw_in, raw_out, q, kv, probs, whead, mixed, out, fore, alone = call(
        functools.partial(forward_body, ny, nx, rs, ro),
        [
            ((2, pn, zh_n, 6 * rs, LANE), BF),
            ((2, pn, zh_n, 4 * ro, LANE), BF),
            ((PTS, HD), BF),
            ((EXT, D), BF),
            ((HEADS, PTS, EXT), BF),
            ((D, NVAR), BF),
            ((PTS, HD), BF),
            ((PTS, D), BF),
            ((members, PTS, NVAR), BF),
            ((PTS, NVAR), F32),
        ],
        (ahead, normed, behind, part, inputs, count, own, other),
        "VAVVAAVV>HHHHHAVVVV",
        scratch=(
            pltpu.VMEM((EXT, 3 * HD), BF),
            pltpu.VMEM((HEADS, PTS, EXT), BF),
            pltpu.VMEM((PTS, D), F32),
            pltpu.SemaphoreType.DMA((7,)),
        ),
        cost=(2e9, 1e7),
        limit=24,
    )
    every = lax.all_to_all(fore, MEMBER, 0, 0, tiled=True)
    gf, wg = call(
        functools.partial(score_body, members, zh_n),
        [
            ((PTS, NVAR), BF),
            ((pn, zh_n, (D + HD) // devices, NVAR), BF),
        ],
        (every, alone, observed, mixed, out),
        "VVVVV>AA",
        cost=(1e8, 2e6),
        limit=8,
    )
    plane = lax.all_to_all(wg, PLANE, 0, 0, tiled=True)
    gq, mid, inside, across = call(
        functools.partial(backward_body, ny, nx, ro),
        [((PTS, HD), BF), ((PTS, D), F32), ((HALO, D), BF), ((HALO, D), BF)],
        (gf, whead, raw_out, q, kv, probs),
        "HHHHHH>AAAA",
        scratch=(
            pltpu.VMEM(gf.shape, BF),
            pltpu.VMEM(whead.shape, BF),
            pltpu.VMEM((2, pn, zh_n, 4 * ro, LANE), BF),
            pltpu.VMEM(q.shape, BF),
            pltpu.VMEM(kv.shape, BF),
            pltpu.VMEM(probs.shape, BF),
            pltpu.VMEM((PTS, HD), BF),
            pltpu.SemaphoreType.DMA((6,)),
        ),
        cost=(1e9, 4e6),
        limit=16,
    )
    inside = lax.ppermute(inside, GRID, inner)
    across = lax.ppermute(across, GRID, outer)
    (partial,) = call(
        sum_body,
        [(wg.shape[1:], BF)],
        (plane,),
        "V>A",
        cost=(1e6, 1e6),
        limit=4,
    )
    column = lax.all_to_all(partial, "zh", 0, 0, tiled=True)
    (spread,) = call(
        spread_body,
        [((members, *wg.shape[2:]), BF)],
        (column,),
        "V>A",
        cost=(1e6, 1e6),
        limit=4,
    )
    parts = lax.all_to_all(spread, MEMBER, 0, 0, tiled=True)
    total, grad_input = call(
        functools.partial(final_body, ny, nx, rs),
        [((PTS, D), F32), ((PTS, D), BF)],
        (inputs, scale, gf, whead, raw_in, gq, mid, inside, across),
        "AAAAVAAVV>AA",
        scratch=(
            pltpu.VMEM((PTS, 3 * HD), BF),
            pltpu.VMEM((PTS, D), F32),
        ),
        cost=(1e9, 4e6),
        limit=16,
    )
    scaling = 1.0 / math.sqrt(members * devices * PTS)
    mixing, head = call(
        functools.partial(weights_body, scaling),
        [((HD // devices, D), F32), ((D // devices, NVAR), F32)],
        (parts, whead),
        "VH>AA",
        scratch=(pltpu.VMEM((D, NVAR), BF), pltpu.SemaphoreType.DMA((1,))),
        cost=(1e8, 1e6),
        limit=8,
    )
    return grad_input[None], mixing, head, total[None]


def refined(mesh):
    members, devices = mesh.shape["member"], mesh.shape["grid"]
    cut = {64: (4, 4, 4), 4: (1, 2, 2), 8: (2, 2, 2)}[devices]
    return Mesh(
        mesh.devices.reshape(members // 2, 2, *cut), ("zl", "core", "zh", "y", "x")
    )


def solution(mesh):
    rows = P(GRID, None)

    return jax.shard_map(
        shards,
        mesh=refined(mesh),
        in_specs=(
            P(MEMBER, GRID, None),
            P(),
            rows,
            rows,
            rows,
            rows,
            rows,
            rows,
            rows,
        ),
        out_specs=(P(MEMBER, GRID, None), rows, rows, P(MEMBER, GRID, None)),
        check_vma=False,
    )
```

```python
import functools
import math

import jax
import jax.numpy as jnp
from jax import lax
from jax.experimental import pallas as pl
from jax.experimental.pallas import tpu as pltpu
from jax.sharding import Mesh, PartitionSpec as P


HEADS = 8
HDIM = 64
KNB = 8
HALO = 32
PTS = 128
EXT = PTS + 2 * HALO
D = 1024
HD = 512
NVAR = 128
LANE = 128

epsilon = 1e-05
smooth = 0.1

MEMBER = ("zl", "core")
GRID = ("zh", "y", "x")
PLANE = ("y", "x")

BF = jnp.bfloat16
F32 = jnp.float32


def nn(a, b):
    return lax.dot_general(a, b, (((1,), (0,)), ((), ())), preferred_element_type=F32)


def nt(a, b):
    return lax.dot_general(a, b, (((1,), (1,)), ((), ())), preferred_element_type=F32)


def tn(a, b):
    return lax.dot_general(a, b, (((0,), (0,)), ((), ())), preferred_element_type=F32)


SPECS = {
    "V": pl.BlockSpec(memory_space=pltpu.VMEM),
    "A": pl.BlockSpec(),
    "H": pl.BlockSpec(memory_space=pltpu.HBM),
}


def call(body, outs, args, places, scratch=(), cost=(1e9, 4e6), limit=16):
    taken, given = places.split(">")
    shapes = [
        jax.ShapeDtypeStruct(s, d) if at == "V" else pltpu.HBM(s, d)
        for (s, d), at in zip(outs, given, strict=True)
    ]
    args = [
        x if at == "V" else pltpu.with_memory_space_constraint(x, pltpu.HBM)
        for x, at in zip(args, taken, strict=True)
    ]
    return pl.pallas_call(
        body,
        out_shape=tuple(shapes),
        in_specs=[SPECS[at] for at in taken],
        out_specs=tuple(SPECS[at] for at in given),
        scratch_shapes=list(scratch),
        compiler_params=pltpu.CompilerParams(vmem_limit_bytes=limit << 20),
        cost_estimate=pl.CostEstimate(
            flops=int(cost[0]), bytes_accessed=int(cost[1]), transcendentals=0
        ),
    )(*args)


def normalised(rows):
    values = rows.astype(F32)
    center = values - jnp.mean(values, axis=-1, keepdims=True)
    inverse = lax.rsqrt(jnp.mean(center * center, axis=-1, keepdims=True) + epsilon)
    return center * inverse, inverse


def taps_body(own, scale, rel, normed, count):
    centred, _ = normalised(own[...])
    normed[...] = (centred * scale[...]).astype(BF)
    place = lax.broadcasted_iota(jnp.int32, (PTS, EXT), 1)
    total = jnp.zeros((PTS, EXT), F32)
    for k in range(KNB):
        total = total + (place == rel[:, k : k + 1]).astype(F32)
    count[...] = total


def halves(tile_shape, head):
    lane = lax.broadcasted_iota(jnp.int32, tile_shape, 1)
    return (lane < HDIM) if head == 0 else (lane >= HDIM)


def fetched(pairs, sems):
    return [pltpu.make_async_copy(s, d, sems.at[i]) for i, (s, d) in enumerate(pairs)]


def pack_body(query, key, value, out, head, column):
    rs, ro = query.shape[0], out.shape[0]

    def put(row, tile):
        size = tile.shape[0]
        for i in range(column.shape[0]):
            column[i, row : row + size, :] = tile

    for c in range(2):

        @pl.when(lax.axis_index("core") == c)
        def _():
            for t in range(6):
                weight = (query, key, value)[(6 * c + t) // 4]
                lane = (6 * c + t) % 4 * LANE
                put(t * rs, weight[:, lane : lane + LANE])
            for t in range(4):
                lane = (4 * c + t) * LANE
                put(6 * rs + t * ro, out[:, lane : lane + LANE])
            put(6 * rs + 4 * ro, head[c * rs // 2 : (c + 1) * rs // 2, :])


def places(side, ny, nx):
    return [
        y * nx + x if side == 0 else x * ny + y for y in range(ny) for x in range(nx)
    ]


def on_each_core(body):
    for c in range(2):
        pl.when(lax.axis_index("core") == c)(functools.partial(body, c))


def tile_at(buf, order, zh, start, size):
    return jnp.concatenate([buf[i, zh, start : start + size, :] for i in order], axis=0)


def narrow_tile(buf, order, zh, start, size):
    parts = [buf[i, zh, start : start + size, :].astype(F32) for i in order]
    return jnp.concatenate(parts, axis=0).astype(BF)


def projected(rows, buf, order, rs):
    total = 0.0
    depth = buf.shape[0] * rs
    for zh in range(buf.shape[1]):
        tiles = [tile_at(buf, order, zh, t * rs, rs) for t in range(6)]
        total = total + nn(
            rows[:, zh * depth : (zh + 1) * depth], jnp.concatenate(tiles, axis=1)
        )
    return total.astype(BF)


def is_even(shape):
    return jnp.full(shape, lax.rem(lax.axis_index("x"), 2), jnp.int32) == 0


def early_body(
    ny, nx, rs, inside, across, scale, normed, own, ahead, behind, part
):
    even = is_even((HALO, D))
    a, b = inside[...].astype(F32), across[...].astype(F32)
    for block, to in ((jnp.where(even, b, a), ahead), (jnp.where(even, a, b), behind)):
        centred, _ = normalised(block)
        to[...] = (centred * scale[...]).astype(BF)
    rows = jnp.concatenate([ahead[...], normed[...], behind[...]], axis=0)

    def project(c):
        part[...] = projected(rows, own, places(c, ny, nx), rs)

    on_each_core(project)


def forward_body(
    ny, nx, rs, ro, ahead, normed, behind, part, states, count, own, other,
    raw_in, raw_out, q_out, kv_out, probs_out, whead, mixed, out, fore, alone,
    qkv, probs, added_out, sems,
):
    pn, zh_n = own.shape[:2]
    qrows = 6 * rs
    orows = 4 * ro
    hr = rs // 2
    raws = fetched(
        [
            (buf.at[:, :, pl.ds(start, to.shape[3]), :], to.at[i])
            for i, buf in enumerate((own, other))
            for start, to in ((qrows, raw_out), (0, raw_in))
        ],
        sems.at[pl.ds(3, 4)],
    )
    for copy in raws:
        copy.start()
    rows = jnp.concatenate([ahead[...], normed[...], behind[...]], axis=0)
    width = 6 * LANE

    def project(c):
        there = projected(rows, other, places(1 - c, ny, nx), rs)
        qkv[:, c * width : (c + 1) * width] = part[...]
        qkv[:, (1 - c) * width : (2 - c) * width] = there

    on_each_core(project)
    leaving = fetched(
        (
            (qkv.at[HALO : HALO + PTS, 0:HD], q_out),
            (qkv.at[:, HD : 3 * HD], kv_out),
            (probs, probs_out),
        ),
        sems,
    )
    leaving[0].start()
    leaving[1].start()
    times = count[...]
    here = times > 0
    for pair in range(HEADS // 2):
        at = pl.ds(pair * LANE, LANE)
        q2 = qkv[HALO : HALO + PTS, pair * LANE : (pair + 1) * LANE]
        k2 = qkv[:, HD + pair * LANE : HD + (pair + 1) * LANE]
        v2 = qkv[:, 2 * HD + pair * LANE : 2 * HD + (pair + 1) * LANE]
        got = []
        for side in range(2):
            chosen = jnp.where(halves((PTS, LANE), side), q2, jnp.zeros_like(q2))
            score = nt(chosen, k2) * (1.0 / math.sqrt(HDIM))
            score = jnp.where(here, score, -1e30)
            highest = jnp.max(score, axis=-1, keepdims=True)
            power = jnp.exp(score - highest)
            prob = power / jnp.sum(times * power, axis=-1, keepdims=True)
            weight = (times * prob.astype(BF).astype(F32)).astype(BF)
            probs[2 * pair + side] = weight
            got.append(nn(weight, v2))
        mixed[:, at] = jnp.where(halves((PTS, LANE), 0), got[0], got[1]).astype(BF)
    leaving[2].start()
    attended = mixed[...]
    at_head = qrows + orows

    def finish(c):
        wide = 4 * LANE
        depth = pn * ro
        orders = [places(0, ny, nx), places(1, ny, nx)]
        bufs = (own, other) if c == 0 else (other, own)
        for side in range(2):
            total = 0.0
            for zh in range(zh_n):
                tiles = [
                    narrow_tile(bufs[side], orders[side], zh, qrows + t * ro, ro)
                    for t in range(4)
                ]
                total = total + nn(
                    attended[:, zh * depth : (zh + 1) * depth],
                    jnp.concatenate(tiles, axis=1),
                )
            added_out[:, side * wide : (side + 1) * wide] = total
        pieces = []
        for zh in range(zh_n):
            for ij in zip(*orders):
                for side in range(2):
                    block = bufs[side][ij[side], zh, at_head : at_head + hr, :]
                    pieces.append(block.astype(F32))
        whead[...] = jnp.concatenate(pieces, axis=0).astype(BF)

    on_each_core(finish)
    layer = (states[...].astype(F32) + added_out[...]).astype(BF)
    out[...] = layer
    mine = nn(layer, whead[...])
    alone[...] = mine
    for i in range(fore.shape[0]):
        fore[i] = mine.astype(BF)
    for copy in raws + leaving:
        copy.wait()


def slope(z):
    return z * lax.rsqrt(z * z + smooth * smooth)


def score_body(members, zh_n, every, alone, observed, mixed, out, gf, wg):
    mine = alone[...]
    sent = mine.astype(BF).astype(F32)
    total = jnp.zeros_like(mine)
    for m in range(members):
        total = total + slope(sent - every[m].astype(F32))
    grad = (slope(mine - observed[...]) - total * (1.0 / (members - 1))).astype(BF)
    gf[...] = grad
    pn = wg.shape[0]
    heads = tn(out[...], grad)
    factor = tn(mixed[...], grad)
    rb, ra = D // (zh_n * pn), HD // (zh_n * pn)
    for zh in range(zh_n):
        wg[:, zh, 0:rb, :] = (
            heads[zh * pn * rb : (zh + 1) * pn * rb].reshape(pn, rb, NVAR).astype(BF)
        )
        wg[:, zh, rb : rb + ra, :] = (
            factor[zh * pn * ra : (zh + 1) * pn * ra].reshape(pn, ra, NVAR).astype(BF)
        )


def backward_body(
    ny, nx, ro, gf_in, whead_in, raw_in, q_in, kv_in, probs_in,
    gq, mid, inside, across,
    gf, whead, raw, q, kv, probs, gm_held, sems,
):
    zh_n = raw.shape[2]
    copies = fetched(
        (
            (gf_in, gf),
            (whead_in, whead),
            (raw_in, raw),
            (kv_in, kv),
            (probs_in, probs),
            (q_in, q),
        ),
        sems,
    )
    for copy in copies:
        copy.start()
    copies[0].wait()
    copies[1].wait()
    go = nt(gf[...], whead[...]).astype(BF)
    copies[2].wait()

    def widen(c):
        columns = [0.0] * zh_n
        for side in range(2):
            order = places(side, ny, nx)
            given = go[:, side * 4 * LANE : (side + 1) * 4 * LANE]
            for zh in range(zh_n):
                tiles = [
                    narrow_tile(raw.at[side ^ c], order, zh, t * ro, ro)
                    for t in range(4)
                ]
                columns[zh] = columns[zh] + nt(given, jnp.concatenate(tiles, axis=1))
        gm_held[...] = jnp.concatenate(columns, axis=1).astype(BF)

    on_each_core(widen)
    gm = gm_held[...]
    for copy in copies[3:]:
        copy.wait()
    for pair in range(HEADS // 2):
        at = pl.ds(pair * LANE, LANE)
        vat = pl.ds(HD + pair * LANE, LANE)
        q2, k2, v2 = q[:, at], kv[:, at], kv[:, vat]
        g2 = gm[:, pair * LANE : (pair + 1) * LANE]
        gqs, gks, gvs = [], [], []
        for side in range(2):
            chosen = jnp.where(halves((PTS, LANE), side), g2, jnp.zeros_like(g2))
            gp = nt(chosen, v2)
            held = probs[2 * pair + side]
            weight = held.astype(F32)
            centre = jnp.sum(weight * gp, axis=-1, keepdims=True)
            gs = (weight * (gp - centre) * (1.0 / math.sqrt(HDIM))).astype(BF)
            gqs.append(nn(gs, k2))
            gks.append(tn(gs, q2))
            gvs.append(tn(held, g2))
        gq[:, at] = jnp.where(halves((PTS, LANE), 0), gqs[0], gqs[1]).astype(BF)
        pick = halves((EXT, LANE), 0)
        even = is_even((HALO, LANE))
        for where_at, parts in ((at, gks), (vat, gvs)):
            total = jnp.where(pick, parts[0], parts[1])
            lower, upper = total[:HALO], total[HALO + PTS :]
            inside[:, where_at] = jnp.where(even, upper, lower).astype(BF)
            across[:, where_at] = jnp.where(even, lower, upper).astype(BF)
            mid[:, where_at] = total[HALO : HALO + PTS]


def final_body(
    ny, nx, rs, states, scale, gf, whead, raw, gq, mid, inside, across,
    total, grad, given, held,
):
    zh_n = raw.shape[2]
    centred, inverse = normalised(states[...])
    total[...] = mid[...]
    even = is_even((HALO, D))
    a, b = inside[...].astype(F32), across[...].astype(F32)
    total[:HALO, :] += jnp.where(even, b, a)
    total[PTS - HALO :, :] += jnp.where(even, a, b)
    given[:, :HD] = gq[...]
    given[:, HD:] = total[...].astype(BF)

    def widen(c):
        depth = raw.shape[1] * rs
        for zh in range(zh_n):
            column = 0.0
            for side in range(2):
                order = places(side, ny, nx)
                part = given[:, side * 6 * LANE : (side + 1) * 6 * LANE]
                tiles = [
                    tile_at(raw.at[side ^ c], order, zh, t * rs, rs) for t in range(6)
                ]
                column = column + nt(part, jnp.concatenate(tiles, axis=1))
            held[:, zh * depth : (zh + 1) * depth] = column

    on_each_core(widen)
    gn = held[...]
    g = gn * scale[...]
    back = inverse * (
        g
        - jnp.mean(g, axis=-1, keepdims=True)
        - centred * jnp.mean(g * centred, axis=-1, keepdims=True)
    )
    grad[...] = (nt(gf[...], whead[...]) + back).astype(BF)


def added(parts):
    total = parts[0].astype(F32)
    for i in range(1, parts.shape[0]):
        total = total + parts[i].astype(F32)
    return total


def sum_body(parts, total):
    total[...] = added(parts).astype(BF)


def spread_body(parts, spread):
    total = added(parts).astype(BF)
    for i in range(spread.shape[0]):
        spread[i] = total


def weights_body(scaling, parts, whead_in, mixing, head, whead, sems):
    (arriving,) = fetched(((whead_in, whead),), sems)
    arriving.start()
    rb = head.shape[0]
    total = added(parts) * scaling
    head[...] = total[:rb]
    factor = total[rb:]
    high = factor.astype(BF)
    low = (factor - high.astype(F32)).astype(BF)
    arriving.wait()
    flat_head = whead[...]
    mixing[...] = nt(high, flat_head) + nt(low, flat_head)


def shards(
    states, norm_scale, query, key, value, out_w, head_w, neighbours, observed
):
    members = lax.axis_size(MEMBER)
    devices = lax.axis_size(GRID)
    zh_n = lax.axis_size("zh")
    pn = lax.axis_size(PLANE)
    inputs = states[0]
    rs, ro = query.shape[0], out_w.shape[0]
    packed = 6 * rs + 4 * ro + rs // 2
    swap = [(0, 1), (1, 0)]
    inner = [(i, i ^ 1) for i in range(devices)]
    outer = [(i, i + 1 if i % 2 else i - 1) for i in range(1, devices - 1)]

    (column,) = call(
        pack_body,
        [((zh_n, packed, LANE), BF)],
        (query, key, value, out_w, head_w),
        "AAAAA>V",
        cost=(1e6, 1e6),
        limit=4,
    )
    column = lax.all_to_all(column, "zh", 0, 0, tiled=True)
    even = lax.rem(lax.axis_index("x"), 2) == 0
    inside = lax.ppermute(
        jnp.where(even, inputs[PTS - HALO :], inputs[:HALO]), GRID, inner
    )
    across = lax.ppermute(
        jnp.where(even, inputs[:HALO], inputs[PTS - HALO :]), GRID, outer
    )
    rel = neighbours - (lax.axis_index(GRID) * PTS - HALO)
    scale = norm_scale.reshape(1, D)
    normed, count = call(
        taps_body,
        [((PTS, D), BF), ((PTS, EXT), F32)],
        (inputs, scale, rel),
        "VAA>VV",
        cost=(4e6, 1e6),
        limit=8,
    )
    ny, nx = lax.axis_size("y"), lax.axis_size("x")
    along_x = [[y * nx + x for x in range(nx)] for y in range(ny)]
    along_y = [[y * nx + x for y in range(ny)] for x in range(nx)]

    def widened(block, first, second):
        groups = first + [[pn + i for i in group] for group in second]
        n = len(first[0])
        return lax.all_to_all(
            jnp.broadcast_to(block[None], (n, *block.shape)),
            ("core", "y", "x"),
            0,
            0,
            axis_index_groups=groups,
            tiled=True,
        )

    line = widened(column, along_x, along_y)
    own = widened(line, along_y, along_x).reshape(pn, *column.shape)
    other = lax.ppermute(own, "core", swap)
    ahead, behind, part = call(
        functools.partial(early_body, ny, nx, rs),
        [((HALO, D), BF), ((HALO, D), BF), ((EXT, 6 * LANE), BF)],
        (inside, across, scale, normed, own),
        "VVAVV>VVV",
        cost=(3e8, 4e6),
        limit=8,
    )
    raw_in, raw_out, q, kv, probs, whead, mixed, out, fore, alone = call(
        functools.partial(forward_body, ny, nx, rs, ro),
        [
            ((2, pn, zh_n, 6 * rs, LANE), BF),
            ((2, pn, zh_n, 4 * ro, LANE), BF),
            ((PTS, HD), BF),
            ((EXT, D), BF),
            ((HEADS, PTS, EXT), BF),
            ((D, NVAR), BF),
            ((PTS, HD), BF),
            ((PTS, D), BF),
            ((members, PTS, NVAR), BF),
            ((PTS, NVAR), F32),
        ],
        (ahead, normed, behind, part, inputs, count, own, other),
        "VVVVVVVV>HHHHHAVVVV",
        scratch=(
            pltpu.VMEM((EXT, 3 * HD), BF),
            pltpu.VMEM((HEADS, PTS, EXT), BF),
            pltpu.VMEM((PTS, D), F32),
            pltpu.SemaphoreType.DMA((7,)),
        ),
        cost=(2e9, 1e7),
        limit=24,
    )
    every = lax.all_to_all(fore, MEMBER, 0, 0, tiled=True)
    gf, wg = call(
        functools.partial(score_body, members, zh_n),
        [
            ((PTS, NVAR), BF),
            ((pn, zh_n, (D + HD) // devices, NVAR), BF),
        ],
        (every, alone, observed, mixed, out),
        "VVVVV>AA",
        cost=(1e8, 2e6),
        limit=8,
    )
    plane = lax.all_to_all(wg, PLANE, 0, 0, tiled=True)
    gq, mid, inside, across = call(
        functools.partial(backward_body, ny, nx, ro),
        [((PTS, HD), BF), ((PTS, D), F32), ((HALO, D), BF), ((HALO, D), BF)],
        (gf, whead, raw_out, q, kv, probs),
        "HHHHHH>AAAA",
        scratch=(
            pltpu.VMEM(gf.shape, BF),
            pltpu.VMEM(whead.shape, BF),
            pltpu.VMEM((2, pn, zh_n, 4 * ro, LANE), BF),
            pltpu.VMEM(q.shape, BF),
            pltpu.VMEM(kv.shape, BF),
            pltpu.VMEM(probs.shape, BF),
            pltpu.VMEM((PTS, HD), BF),
            pltpu.SemaphoreType.DMA((6,)),
        ),
        cost=(1e9, 4e6),
        limit=16,
    )
    inside = lax.ppermute(inside, GRID, inner)
    across = lax.ppermute(across, GRID, outer)
    (partial,) = call(
        sum_body,
        [(wg.shape[1:], BF)],
        (plane,),
        "V>A",
        cost=(1e6, 1e6),
        limit=4,
    )
    column = lax.all_to_all(partial, "zh", 0, 0, tiled=True)
    (spread,) = call(
        spread_body,
        [((members, *wg.shape[2:]), BF)],
        (column,),
        "V>A",
        cost=(1e6, 1e6),
        limit=4,
    )
    parts = lax.all_to_all(spread, MEMBER, 0, 0, tiled=True)
    total, grad_input = call(
        functools.partial(final_body, ny, nx, rs),
        [((PTS, D), F32), ((PTS, D), BF)],
        (inputs, scale, gf, whead, raw_in, gq, mid, inside, across),
        "AAAAVAAVV>AA",
        scratch=(
            pltpu.VMEM((PTS, 3 * HD), BF),
            pltpu.VMEM((PTS, D), F32),
        ),
        cost=(1e9, 4e6),
        limit=16,
    )
    scaling = 1.0 / math.sqrt(members * devices * PTS)
    mixing, head = call(
        functools.partial(weights_body, scaling),
        [((HD // devices, D), F32), ((D // devices, NVAR), F32)],
        (parts, whead),
        "VH>AA",
        scratch=(pltpu.VMEM((D, NVAR), BF), pltpu.SemaphoreType.DMA((1,))),
        cost=(1e8, 1e6),
        limit=8,
    )
    return grad_input[None], mixing, head, total[None]


def refined(mesh):
    members, devices = mesh.shape["member"], mesh.shape["grid"]
    cut = {64: (4, 4, 4), 4: (1, 2, 2), 8: (2, 2, 2)}[devices]
    return Mesh(
        mesh.devices.reshape(members // 2, 2, *cut), ("zl", "core", "zh", "y", "x")
    )


def solution(mesh):
    rows = P(GRID, None)

    return jax.shard_map(
        shards,
        mesh=refined(mesh),
        in_specs=(
            P(MEMBER, GRID, None),
            P(),
            rows,
            rows,
            rows,
            rows,
            rows,
            rows,
            rows,
        ),
        out_specs=(P(MEMBER, GRID, None), rows, rows, P(MEMBER, GRID, None)),
        check_vma=False,
    )
```
